32 devices in a mesh: ctx: 8 (over z, core), fsdp: 4 (over y, x).
Axes of the slice: x: 2, y: 2, z: 4, core: 2. Of those that a mesh axis runs over, the one named last changes fastest.
Arguments:
- tokens: bfloat16 [4, 2048, 2048], P('fsdp', 'ctx'), may hold values from -6 to 6
- seq_ids: int32 [4, 2048], P('fsdp', 'ctx'), may hold values from 0 to 1, as said below
- positions: int32 [4, 2048], P('fsdp', 'ctx'), may hold values from 0 to 1791, as said below
- block_ids: int32 [4, 2048], P('fsdp', 'ctx'), may hold values from 0 to 6, as said below
- gain_attn: float32 [2048], P(('ctx', 'fsdp')), may hold values from 0.5 to 1.5
- w_query: float32 [2048, 2048], P(('ctx', 'fsdp')), may hold values from -0.4375 to 0.4375
- key_weight_matrix: float32 [2048, 512], P(('ctx', 'fsdp')), may hold values from -0.4375 to 0.4375
- value_weight_matrix: float32 [2048, 512], P(('ctx', 'fsdp')), may hold values from -0.125 to 0.125
- w_out: float32 [2048, 2048], P(('ctx', 'fsdp')), may hold values from -4 to 4
- gain_mlp: float32 [2048], P(('ctx', 'fsdp')), may hold values from 0.5 to 1.5
- w_gate: float32 [2048, 8192], P(('ctx', 'fsdp')), may hold values from -0.125 to 0.125
- w_up: float32 [2048, 8192], P(('ctx', 'fsdp')), may hold values from -0.125 to 0.125
- w_down: float32 [2048, 8192], P(('ctx', 'fsdp')), may hold values from -0.625 to 0.625
- out_grad: bfloat16 [4, 2048, 2048], P('fsdp', 'ctx'), may hold values from -6 to 6
Outputs:
- layer_out: bfloat16 [4, 2048, 2048], P('fsdp', 'ctx')
- input_grad: float32 [4, 2048, 2048], P('fsdp', 'ctx')
- grad_gain_attn: float32 [2048], P(('ctx', 'fsdp'))
- grad_query: float32 [2048, 2048], P(('ctx', 'fsdp'))
- grad_key: float32 [2048, 512], P(('ctx', 'fsdp'))
- grad_value: float32 [2048, 512], P(('ctx', 'fsdp'))
- grad_out: float32 [2048, 2048], P(('ctx', 'fsdp'))
- grad_gain_mlp: float32 [2048], P(('ctx', 'fsdp'))
- grad_gate: float32 [2048, 8192], P(('ctx', 'fsdp'))
- grad_up: float32 [2048, 8192], P(('ctx', 'fsdp'))
- grad_down: float32 [2048, 8192], P(('ctx', 'fsdp'))
The draws below stay inside these ranges and needn't reach their ends.
Inputs may be any that keep to these rules, and one draw needn't show every extreme that they name: `seq_ids`: each row of 2048 tokens holds two sequences, ids 0 then 1, each of 256 tokens or more. `positions`: A token's place within its sequence, counted from 0. `block_ids`: the token's position divided by 256, rounded down.
All inputs are finite; a program needn't handle non-finite values.
Results may differ from the reference program's by a relative error of at most 0.025.
Values may be sent and summed in bfloat16 or wider, within the bound.
A program may use at most 1.125 GiB of HBM per device.

```python
import math
import jax
import jax.numpy as jnp
from jax import lax

MODEL_WIDTH = 2048
QUERY_HEADS = 32
KEY_VALUE_HEADS = 8
HEAD_SIZE = 64
FF = 8192
BLOCK = 256
SEQ_TOK = 2048
GROUPS = 4


def split_tokens(key):
    low_end = SEQ_TOK // 8
    cuts = jax.random.randint(jax.random.fold_in(key, 11), (GROUPS, 1), low_end, SEQ_TOK - low_end + 1)
    first_row = jnp.arange(GROUPS, dtype=jnp.int32)[:, None] == 0
    cuts = jnp.where(first_row, low_end, cuts).astype(jnp.int32)
    places = jnp.arange(SEQ_TOK, dtype=jnp.int32)[None, :]
    second = (places >= cuts).astype(jnp.int32)
    within = places - second * cuts
    return (second, within)


def draw_seq_ids(key, part):
    return split_tokens(key)[0]


def draw_positions(key, part):
    return split_tokens(key)[1]


def draw_block_ids(key, part):
    return split_tokens(key)[1] // BLOCK


def steps_of(rng, extent, cuts, low, top_value):
    level = 1.0
    for axis_at, parts in cuts:
        draws = jax.random.uniform(jax.random.fold_in(jax.random.fold_in(rng, 6), axis_at), (parts,), jnp.float32, low / len(cuts), top_value / len(cuts))
        level = level * jnp.repeat(jnp.exp(draws), extent[axis_at] // parts).reshape((-1,) + (1,) * (len(extent) - 1 - axis_at))
    return level


def gaussian(own_key, dims, deviation, bound, pieces=(), held_as=jnp.bfloat16):
    values = deviation * jax.random.normal(own_key, dims, jnp.float32)
    if pieces:
        values = values * steps_of(own_key, dims, pieces, -0.22, 0.18)
    return jnp.clip(values, -bound, bound).astype(held_as)


def setup_inputs(seed: int = 0) -> dict:
    key_of = jax.random.split(jax.random.key(seed), 15)
    return {
        "tokens": gaussian(key_of[0], (GROUPS, SEQ_TOK, MODEL_WIDTH), 1.0, 6.0, ((0, 4), (1, 8))),
        "seq_ids": draw_seq_ids(jax.random.fold_in(key_of[14], 71), 0),
        "positions": draw_positions(jax.random.fold_in(key_of[14], 71), 0),
        "block_ids": draw_block_ids(jax.random.fold_in(key_of[14], 71), 0),
        "gain_attn": jnp.clip(1.0 + 0.1 * jax.random.normal(key_of[4], (MODEL_WIDTH,), jnp.float32), 0.5, 1.5),
        "w_query": gaussian(key_of[5], (MODEL_WIDTH, QUERY_HEADS * HEAD_SIZE), (MODEL_WIDTH // 12) ** -0.5, 0.4375, ((0, 32),), jnp.float32),
        "key_weight_matrix": gaussian(key_of[6], (MODEL_WIDTH, KEY_VALUE_HEADS * HEAD_SIZE), (MODEL_WIDTH // 12) ** -0.5, 0.4375, ((0, 32),), jnp.float32),
        "value_weight_matrix": gaussian(key_of[7], (MODEL_WIDTH, KEY_VALUE_HEADS * HEAD_SIZE), MODEL_WIDTH ** -0.5, 0.125, ((0, 32),), jnp.float32),
        "w_out": gaussian(key_of[8], (MODEL_WIDTH, QUERY_HEADS * HEAD_SIZE), (max(1, QUERY_HEADS * HEAD_SIZE // 1024)) ** -0.5, 4.0, ((0, 32),), jnp.float32),
        "gain_mlp": jnp.clip(1.0 + 0.1 * jax.random.normal(key_of[9], (MODEL_WIDTH,), jnp.float32), 0.5, 1.5),
        "w_gate": gaussian(key_of[10], (MODEL_WIDTH, FF), MODEL_WIDTH ** -0.5, 0.125, ((0, 32),), jnp.float32),
        "w_up": gaussian(key_of[11], (MODEL_WIDTH, FF), MODEL_WIDTH ** -0.5, 0.125, ((0, 32),), jnp.float32),
        "w_down": gaussian(key_of[12], (MODEL_WIDTH, FF), (FF // 80) ** -0.5, 0.625, ((0, 32),), jnp.float32),
        "out_grad": gaussian(key_of[13], (GROUPS, SEQ_TOK, MODEL_WIDTH), 1.0, 6.0, ((0, 4), (1, 8))),
    }


eps_norm = 1e-05
rope_base = 10000000.0
attention_score_scale = 0.015625
residual_scale = 0.22
negative_filler = -1e+30

@jax.custom_vjp
def lower_precision(v):
    return lax.optimization_barrier(v.astype(jnp.bfloat16)).astype(jnp.float32)

@jax.custom_vjp
def lower_precision_backward(v):
    return v

def low_keep(v):
    return (lower_precision(v), None)

def low_pass(kept, grad):
    return (grad,)

def back_keep(v):
    return (v, None)

def back_low(kept, grad):
    return (lower_precision(grad),)
lower_precision.defvjp(low_keep, low_pass)
lower_precision_backward.defvjp(back_keep, back_low)

def rms_normed(values):
    return values * lax.rsqrt(lax.optimization_barrier(jnp.mean(values * values, axis=-1, keepdims=True)) + eps_norm)

def rope_tables(places):
    frequency = rope_base ** (-(jnp.arange(HEAD_SIZE // 2, dtype=jnp.float32) * 2.0) / HEAD_SIZE)
    angles = places.astype(jnp.float32)[:, None] * frequency[None, :]
    return (jnp.cos(angles)[:, None, :], jnp.sin(angles)[:, None, :])

def apply_rotation(values, cosine_table, sine_table):
    middle = values.shape[-1] // 2
    first_half = values[..., :middle]
    second = values[..., middle:]
    return jnp.concatenate([first_half * cosine_table - second * sine_table, second * cosine_table + first_half * sine_table], axis=-1)

def precise_product(left, right):
    return jnp.dot(left, right, precision=lax.Precision.HIGHEST, preferred_element_type=jnp.float32)

def layer(inputs, sequence_row_ids, place_row, block_row_index, gain_attn, w_query, key_weight_matrix, value_weight_matrix, w_out, gain_mlp, w_gate, w_up, w_down):
    total_row_count = inputs.shape[0]
    heads_per_group = QUERY_HEADS // KEY_VALUE_HEADS
    cosine_table, sine_table = rope_tables(place_row)
    normalized_input = lower_precision(rms_normed(inputs) * gain_attn[None, :])
    query_vectors = lower_precision_backward(precise_product(normalized_input, w_query)).reshape(total_row_count, QUERY_HEADS, HEAD_SIZE)
    key_entries = lower_precision_backward(precise_product(normalized_input, key_weight_matrix)).reshape(total_row_count, KEY_VALUE_HEADS, HEAD_SIZE)
    value_entries = lower_precision(lower_precision_backward(precise_product(normalized_input, value_weight_matrix))).reshape(total_row_count, KEY_VALUE_HEADS, HEAD_SIZE)
    query_vectors = lower_precision(apply_rotation(query_vectors, cosine_table, sine_table)).reshape(total_row_count, KEY_VALUE_HEADS, heads_per_group, HEAD_SIZE)
    key_entries = lower_precision(apply_rotation(key_entries, cosine_table, sine_table))
    block_row_count = math.gcd(total_row_count, 512)

    def block_attention_step(block_inputs):
        query_rows, seq_rows, blk_rows = block_inputs
        scores = jnp.einsum('tkgd,skd->kgts', query_rows, key_entries, precision=lax.Precision.HIGHEST) * attention_score_scale
        scores = lower_precision_backward(scores)
        allowed = (seq_rows[:, None] == sequence_row_ids[None, :]) & (block_row_index[None, :] <= blk_rows[:, None])
        scores = jnp.where(allowed[None, None], scores, negative_filler)
        row_max = lax.optimization_barrier(jnp.max(scores, axis=-1, keepdims=True))
        weights = jnp.exp(scores - row_max)
        weights = lower_precision(weights / lax.optimization_barrier(jnp.sum(weights, axis=-1, keepdims=True)))
        mixed = jnp.einsum('kgts,skd->tkgd', weights, value_entries, precision=lax.Precision.HIGHEST)
        return mixed.reshape(block_row_count, QUERY_HEADS * HEAD_SIZE)
    attention_result = lax.map(jax.checkpoint(block_attention_step), (query_vectors.reshape(total_row_count // block_row_count, block_row_count, KEY_VALUE_HEADS, heads_per_group, HEAD_SIZE), sequence_row_ids.reshape(total_row_count // block_row_count, block_row_count), block_row_index.reshape(total_row_count // block_row_count, block_row_count)))
    attention_result = lower_precision(lower_precision_backward(attention_result.reshape(total_row_count, QUERY_HEADS * HEAD_SIZE)))
    attn_branch = lower_precision_backward(precise_product(attention_result, w_out.T))
    hidden = inputs + residual_scale * attn_branch
    normed_two = lower_precision(rms_normed(hidden) * gain_mlp[None, :])
    gate = lower_precision_backward(precise_product(normed_two, w_gate))
    up_vals = lower_precision_backward(precise_product(normed_two, w_up))
    activation = lower_precision(jax.nn.silu(gate) * up_vals)
    mlp_branch = lower_precision_backward(precise_product(activation, w_down.T))
    return hidden + residual_scale * mlp_branch

def reference(tokens, seq_ids, positions, block_ids, gain_attn, w_query, key_weight_matrix, value_weight_matrix, w_out, gain_mlp, w_gate, w_up, w_down, out_grad):

    def forward(inputs, *params):
        rounded = tuple((lower_precision(weight) for weight in params))
        checked = jax.checkpoint(layer)

        def per_group(running, group):
            return (running, checked(group[0], group[1], group[2], group[3], *rounded))
        unused, result = lax.scan(per_group, jnp.zeros((), jnp.float32), (inputs, seq_ids, positions, block_ids))
        return result
    primals = (tokens.astype(jnp.float32), gain_attn, w_query, key_weight_matrix, value_weight_matrix, w_out, gain_mlp, w_gate, w_up, w_down)
    result, pullback = jax.vjp(forward, *primals)
    grads = pullback(out_grad.astype(jnp.float32))
    return (result.astype(jnp.bfloat16), grads[0], grads[1], grads[2], grads[3], grads[4], grads[5], grads[6], grads[7], grads[8], grads[9])
```

```python
import functools

import jax
import jax.numpy as jnp
from jax import lax
from jax.experimental import pallas as pl
from jax.experimental.pallas import tpu as pltpu
from jax.sharding import PartitionSpec as P

QUERY_HEADS = 32
KEY_VALUE_HEADS = 8
HD = 64
BLOCK = 256
EPS = 1e-05
ROPE_BASE = 10000000.0
SCALE = 0.015625
RES = 0.22
NEG = -1e30
bf16 = jnp.bfloat16
f32 = jnp.float32


def dg(a, b, ca, cb):
    return lax.dot_general(a, b, (((ca,), (cb,)), ((), ())), preferred_element_type=f32)


def attn_fwd_kernel(nh, tq, tk, q_ref, k_ref, v_ref, st_ref, en_ref, o_ref, ob_ref, l_ref):
    st = st_ref[...]
    en = en_ref[...]
    lo = jnp.min(st) // tk
    hi = (jnp.max(en) + tk - 1) // tk
    qs = [q_ref[h * HD : (h + 1) * HD, :] for h in range(nh)]

    def body(j, c):
        off = pl.multiple_of(j * tk, tk)
        kb = k_ref[pl.ds(off, tk), :]
        vb = v_ref[:, pl.ds(off, tk)]
        jj = off + lax.broadcasted_iota(jnp.int32, (tk, tq), 0)
        vis = (jj >= st) & (jj < en)
        out = []
        for h in range(nh):
            m, l, a = c[h]
            s = dg(kb, qs[h], 1, 0) * SCALE
            s = jnp.where(vis, s, NEG)
            mn = jnp.maximum(m, jnp.max(s, axis=0, keepdims=True))
            p = jnp.where(vis, jnp.exp(s - mn), 0.0)
            sh = jnp.exp(m - mn)
            l = l * sh + jnp.sum(p, axis=0, keepdims=True)
            a = a * sh + dg(vb, p.astype(bf16), 1, 0)
            out.append((mn, l, a))
        return tuple(out)

    init = tuple(
        (jnp.full((1, tq), NEG, f32), jnp.zeros((1, tq), f32), jnp.zeros((HD, tq), f32))
        for _ in range(nh)
    )
    res = lax.fori_loop(lo, hi, body, init)
    for h in range(nh):
        m, l, a = res[h]
        o = a / l
        o_ref[h * HD : (h + 1) * HD, :] = o
        ob_ref[h * HD : (h + 1) * HD, :] = o.astype(bf16)
        l_ref[h : h + 1, :] = m + jnp.log(l)


def attn_fwd(qT, k, vT, st, en, tq=256, tk=256):
    n, S = qT.shape
    nh = n // HD
    blk = lambda r: pl.BlockSpec((r, tq), lambda i: (0, i))
    full = lambda s: pl.BlockSpec(s, lambda i: (0, 0))
    return pl.pallas_call(
        functools.partial(attn_fwd_kernel, nh, tq, tk),
        grid=(S // tq,),
        in_specs=[blk(n), full((S, HD)), full((HD, S)), blk(1), blk(1)],
        out_specs=[blk(n), blk(n), blk(nh)],
        out_shape=[
            jax.ShapeDtypeStruct((n, S), f32),
            jax.ShapeDtypeStruct((n, S), bf16),
            jax.ShapeDtypeStruct((nh, S), f32),
        ],
        cost_estimate=pl.CostEstimate(
            flops=2 * S * S * n, bytes_accessed=8 * n * S, transcendentals=S * S * nh // 2
        ),
        name="attn_fwd",
    )(qT, k, vT, st, en)


def attn_bwd_kernel(
    nh, tq, tk, q_ref, do_ref, o_ref, lse_ref, st_ref, en_ref, k_ref, kT_ref, v_ref, dq_ref, dk_ref, dv_ref
):
    i = pl.program_id(0)

    @pl.when(i == 0)
    def _():
        dk_ref[...] = jnp.zeros_like(dk_ref)
        dv_ref[...] = jnp.zeros_like(dv_ref)

    st = st_ref[...]
    en = en_ref[...]
    lo = jnp.min(st) // tk
    hi = (jnp.max(en) + tk - 1) // tk
    qs = [q_ref[h * HD : (h + 1) * HD, :] for h in range(nh)]
    dos = [do_ref[h * HD : (h + 1) * HD, :] for h in range(nh)]
    dl = [
        jnp.sum(dos[h].astype(f32) * o_ref[h * HD : (h + 1) * HD, :], axis=0, keepdims=True)
        for h in range(nh)
    ]
    ls = [lse_ref[h : h + 1, :] for h in range(nh)]
    dq_ref[...] = jnp.zeros_like(dq_ref)

    def body(j, _):
        off = pl.multiple_of(j * tk, tk)
        kb = k_ref[pl.ds(off, tk), :]
        kT = kT_ref[:, pl.ds(off, tk)]
        vb = v_ref[pl.ds(off, tk), :]
        jj = off + lax.broadcasted_iota(jnp.int32, (tk, tq), 0)
        vis = (jj >= st) & (jj < en)
        dk = jnp.zeros((HD, tk), f32)
        dv = jnp.zeros((HD, tk), f32)
        for h in range(nh):
            s = dg(kb, qs[h], 1, 0) * SCALE
            p = jnp.exp(jnp.where(vis, s - ls[h], NEG))
            dp = dg(vb, dos[h], 1, 0)
            dsc = (p * (dp - dl[h])).astype(bf16)
            dq_ref[h * HD : (h + 1) * HD, :] += dg(kT, dsc, 1, 0)
            dk = dk + dg(qs[h], dsc, 1, 1)
            dv = dv + dg(dos[h], p.astype(bf16), 1, 1)
        dk_ref[:, pl.ds(off, tk)] += dk
        dv_ref[:, pl.ds(off, tk)] += dv
        return 0

    lax.fori_loop(lo, hi, body, 0)


def attn_bwd(qT, doT, oT, lse, st, en, k, kT, v, tq=256, tk=256):
    n, S = qT.shape
    nh = n // HD
    blk = lambda r: pl.BlockSpec((r, tq), lambda i: (0, i))
    full = lambda s: pl.BlockSpec(s, lambda i: (0, 0))
    return pl.pallas_call(
        functools.partial(attn_bwd_kernel, nh, tq, tk),
        grid=(S // tq,),
        in_specs=[
            blk(n), blk(n), blk(n), blk(nh), blk(1), blk(1),
            full((S, HD)), full((HD, S)), full((S, HD)),
        ],
        out_specs=[blk(n), full((HD, S)), full((HD, S))],
        out_shape=[
            jax.ShapeDtypeStruct((n, S), f32),
            jax.ShapeDtypeStruct((HD, S), f32),
            jax.ShapeDtypeStruct((HD, S), f32),
        ],
        cost_estimate=pl.CostEstimate(
            flops=5 * S * S * n, bytes_accessed=10 * n * S, transcendentals=S * S * nh // 2
        ),
        name="attn_bwd",
    )(qT, doT, oT, lse, st, en, k, kT, v)


def rms(v):
    inv = lax.rsqrt(jnp.mean(v * v, axis=-1, keepdims=True) + EPS)
    return v * inv, inv


def rms_back(x, inv, e):
    return inv * (e - x * jnp.mean(e * x, axis=-1, keepdims=True))


def rotate(v, cos, sin, sign):
    heads = v.shape[0] // HD
    v = v.reshape(heads, 2, HD // 2, v.shape[1])
    a, b = v[:, 0], v[:, 1]
    s = sign * sin
    return jnp.stack([a * cos - b * s, b * cos + a * s], axis=1).reshape(heads * HD, -1)


def local(
    tokens, seq_ids, positions, block_ids, gain_attn, w_query, w_key, w_value, w_out,
    gain_mlp, w_gate, w_up, w_down, out_grad,
):
    nc = lax.axis_size("ctx")
    nf = lax.axis_size("fsdp")
    T, E = tokens.shape[1:]
    R = w_query.shape[0]
    S = T * nc
    FFL = w_gate.shape[1] // nc
    nh = QUERY_HEADS // nc
    rep = nc // KEY_VALUE_HEADS
    QW = nh * HD
    KO, VO, OO = QW, QW + HD, QW + 2 * HD
    AW = 2 * QW + 2 * HD

    def cols(w):
        return w.astype(bf16).reshape(R, nc, -1)

    def kv_cols(w):
        return jnp.repeat(w.astype(bf16).reshape(R, KEY_VALUE_HEADS, HD), rep, axis=1)

    def spread(parts):
        w = jnp.transpose(jnp.concatenate(parts, axis=2), (1, 0, 2))
        w = lax.all_to_all(w, "ctx", 0, 0, tiled=True)
        w = lax.all_gather(w, "fsdp", axis=0)
        return jnp.transpose(w, (1, 0, 2, 3)).reshape(E, -1)

    def collect(g):
        g = g.astype(bf16).reshape(nc, nf, R, -1)
        g = jnp.transpose(g, (1, 0, 2, 3)).reshape(E, -1)
        g = lax.psum_scatter(g, "fsdp", scatter_dimension=0, tiled=True)
        return lax.all_to_all(g.reshape(nc, R, -1), "ctx", 0, 0, tiled=True)

    def gather(v):
        return lax.all_gather(v, "ctx", axis=0, tiled=True)

    def scatter(v):
        return lax.psum_scatter(v.astype(bf16), "ctx", scatter_dimension=0, tiled=True).astype(f32)

    both = ("ctx", "fsdp")
    g_attn, g_mlp = lax.all_gather(
        jnp.stack([gain_attn, gain_mlp]).astype(bf16), both, axis=1, tiled=True
    ).astype(f32)
    ids = lax.all_gather(
        jnp.concatenate([seq_ids, positions, block_ids], axis=0), "ctx", axis=1, tiled=True
    )
    row_tok = gather(tokens[0])
    wa = spread([cols(w_query), kv_cols(w_key), kv_cols(w_value), cols(w_out)])

    seq, pos, blk = ids[0], ids[1], ids[2]
    place = jnp.arange(S, dtype=jnp.int32)
    cut = jnp.sum((seq == 0).astype(jnp.int32))
    first = place - pos
    last = jnp.minimum(first + BLOCK * (blk + 1), jnp.where(seq == 0, cut, S))
    st, en = first[None], last[None]
    freq = ROPE_BASE ** (-(jnp.arange(HD // 2, dtype=f32) * 2.0) / HD)
    ang = freq[:, None] * pos.astype(f32)[None, :]
    cos, sin = jnp.cos(ang), jnp.sin(ang)

    x1r, _ = rms(row_tok.astype(f32))
    n1 = (x1r * g_attn[None]).astype(bf16)
    w_qkv, w_o = wa[:, :OO], wa[:, OO:]
    qkv = dg(w_qkv, n1, 0, 1)
    qkT = rotate(qkv[:VO], cos, sin, 1.0).astype(bf16)
    qT, kT = qkT[:QW], qkT[QW:]
    vT = qkv[VO:].astype(bf16)
    k, v = kT.T, vT.T
    oT, oTb, lse = attn_fwd(qT, k, vT, st, en)
    attn = scatter(dg(oTb, w_o, 0, 1))

    wm = spread([cols(w_gate), cols(w_up), cols(w_down)])
    w_gu, w_d = wm[:, : 2 * FFL], wm[:, 2 * FFL :]
    up_grad = out_grad[0].astype(f32)
    dm = gather((RES * up_grad).astype(bf16))

    tok = tokens[0].astype(f32)
    hidden = tok + RES * attn
    x2, r2 = rms(hidden)
    n2 = gather((x2 * g_mlp[None]).astype(bf16))
    gu = dg(n2, w_gu, 1, 0)
    gate, up = gu[:, :FFL], gu[:, FFL:]
    sg = jax.nn.sigmoid(gate)
    act = (gate * sg * up).astype(bf16)
    d_act = dg(dm, w_d, 1, 0)
    d_gate = (d_act * up * sg * (1.0 + gate * (1.0 - sg))).astype(bf16)
    d_up = (d_act * gate * sg).astype(bf16)
    d_gu = jnp.concatenate([d_gate, d_up], axis=1)
    dn2 = scatter(dg(d_gu, w_gu, 1, 1))
    mlp = scatter(dg(act, w_d, 1, 1))
    layer_out = (hidden + RES * mlp).astype(bf16)
    gm = collect(jnp.concatenate([dg(n2, d_gu, 0, 0), dg(dm, act, 0, 0)], axis=1))

    gg_mlp = jnp.sum(x2 * dn2, axis=0)
    dh = up_grad + rms_back(x2, r2, dn2 * g_mlp[None])
    da = gather((RES * dh).astype(bf16))
    doT = dg(w_o, da, 0, 1).astype(bf16)
    dqT, dkT, dvT = attn_bwd(qT, doT, oT, lse, st, en, k, kT, v)
    dqk = rotate(jnp.concatenate([dqT, dkT], axis=0) * SCALE, cos, sin, -1.0).astype(bf16)
    dqkv = jnp.concatenate([dqk, dvT.astype(bf16)], axis=0)
    dn1 = scatter(dg(dqkv, w_qkv, 0, 1))
    x1, r1 = rms(tok)
    gg_attn = jnp.sum(x1 * dn1, axis=0)
    input_grad = dh + rms_back(x1, r1, dn1 * g_attn[None])
    ga = collect(jnp.concatenate([dg(n1, dqkv, 0, 1), dg(da, oTb, 0, 1)], axis=1))
    gains = lax.psum_scatter(
        jnp.stack([gg_attn, gg_mlp], axis=1), both, scatter_dimension=0, tiled=True
    )

    def rows(g):
        return jnp.transpose(g.astype(f32), (1, 0, 2)).reshape(R, -1)

    def kv_rows(g):
        g = g.astype(f32).reshape(KEY_VALUE_HEADS, rep, R, HD)
        return jnp.transpose(jnp.sum(g, axis=1), (1, 0, 2)).reshape(R, -1)

    return (
        layer_out[None],
        input_grad[None],
        gains[:, 0],
        rows(ga[:, :, :KO]),
        kv_rows(ga[:, :, KO:VO]),
        kv_rows(ga[:, :, VO:OO]),
        rows(ga[:, :, OO:]),
        gains[:, 1],
        rows(gm[:, :, :FFL]),
        rows(gm[:, :, FFL : 2 * FFL]),
        rows(gm[:, :, 2 * FFL :]),
    )


def solution(mesh):
    w1, w2 = P(("ctx", "fsdp")), P(("ctx", "fsdp"), None)
    act, ids = P("fsdp", "ctx", None), P("fsdp", "ctx")
    return jax.shard_map(
        local,
        mesh=mesh,
        in_specs=(act, ids, ids, ids, w1, w2, w2, w2, w2, w1, w2, w2, w2, act),
        out_specs=(act, act, w1, w2, w2, w2, w2, w1, w2, w2, w2),
        check_vma=False,
    )
```

```python
import functools

import jax
import jax.numpy as jnp
from jax import lax
from jax.experimental import pallas as pl
from jax.experimental.pallas import tpu as pltpu
from jax.sharding import PartitionSpec as P

QUERY_HEADS = 32
KEY_VALUE_HEADS = 8
HD = 64
BLOCK = 256
EPS = 1e-05
ROPE_BASE = 10000000.0
SCALE = 0.015625
RES = 0.22
NEG = -1e30
bf16 = jnp.bfloat16
f32 = jnp.float32


def dg(a, b, ca, cb):
    return lax.dot_general(a, b, (((ca,), (cb,)), ((), ())), preferred_element_type=f32)


def attn_fwd_kernel(nh, tq, tk, q_ref, k_ref, v_ref, st_ref, en_ref, o_ref, ob_ref, l_ref):
    st = st_ref[...]
    en = en_ref[...]
    lo = jnp.min(st) // tk
    hi = (jnp.max(en) + tk - 1) // tk
    qs = [q_ref[h * HD : (h + 1) * HD, :] for h in range(nh)]

    def body(j, c):
        off = pl.multiple_of(j * tk, tk)
        kb = k_ref[pl.ds(off, tk), :]
        vb = v_ref[:, pl.ds(off, tk)]
        jj = off + lax.broadcasted_iota(jnp.int32, (tk, tq), 0)
        vis = (jj >= st) & (jj < en)
        out = []
        for h in range(nh):
            m, l, a = c[h]
            s = dg(kb, qs[h], 1, 0) * SCALE
            s = jnp.where(vis, s, NEG)
            mn = jnp.maximum(m, jnp.max(s, axis=0, keepdims=True))
            p = jnp.where(vis, jnp.exp(s - mn), 0.0)
            sh = jnp.exp(m - mn)
            l = l * sh + jnp.sum(p, axis=0, keepdims=True)
            a = a * sh + dg(vb, p.astype(bf16), 1, 0)
            out.append((mn, l, a))
        return tuple(out)

    init = tuple(
        (jnp.full((1, tq), NEG, f32), jnp.zeros((1, tq), f32), jnp.zeros((HD, tq), f32))
        for _ in range(nh)
    )
    res = lax.fori_loop(lo, hi, body, init)
    for h in range(nh):
        m, l, a = res[h]
        o = a / l
        o_ref[h * HD : (h + 1) * HD, :] = o
        ob_ref[h * HD : (h + 1) * HD, :] = o.astype(bf16)
        l_ref[h : h + 1, :] = m + jnp.log(l)


def attn_fwd(qT, k, vT, st, en, tq=256, tk=256):
    n, S = qT.shape
    nh = n // HD
    blk = lambda r: pl.BlockSpec((r, tq), lambda i: (0, i))
    full = lambda s: pl.BlockSpec(s, lambda i: (0, 0))
    return pl.pallas_call(
        functools.partial(attn_fwd_kernel, nh, tq, tk),
        grid=(S // tq,),
        in_specs=[blk(n), full((S, HD)), full((HD, S)), blk(1), blk(1)],
        out_specs=[blk(n), blk(n), blk(nh)],
        out_shape=[
            jax.ShapeDtypeStruct((n, S), f32),
            jax.ShapeDtypeStruct((n, S), bf16),
            jax.ShapeDtypeStruct((nh, S), f32),
        ],
        cost_estimate=pl.CostEstimate(
            flops=2 * S * S * n, bytes_accessed=8 * n * S, transcendentals=S * S * nh // 2
        ),
        name="attn_fwd",
    )(qT, k, vT, st, en)


def attn_bwd_kernel(
    nh, tq, tk, q_ref, do_ref, o_ref, lse_ref, st_ref, en_ref, k_ref, kT_ref, v_ref, dq_ref, dk_ref, dv_ref
):
    i = pl.program_id(0)

    @pl.when(i == 0)
    def _():
        dk_ref[...] = jnp.zeros_like(dk_ref)
        dv_ref[...] = jnp.zeros_like(dv_ref)

    st = st_ref[...]
    en = en_ref[...]
    lo = jnp.min(st) // tk
    hi = (jnp.max(en) + tk - 1) // tk
    qs = [q_ref[h * HD : (h + 1) * HD, :] for h in range(nh)]
    dos = [do_ref[h * HD : (h + 1) * HD, :] for h in range(nh)]
    dl = [
        jnp.sum(dos[h].astype(f32) * o_ref[h * HD : (h + 1) * HD, :], axis=0, keepdims=True)
        for h in range(nh)
    ]
    ls = [lse_ref[h : h + 1, :] for h in range(nh)]
    dq_ref[...] = jnp.zeros_like(dq_ref)

    def body(j, _):
        off = pl.multiple_of(j * tk, tk)
        kb = k_ref[pl.ds(off, tk), :]
        kT = kT_ref[:, pl.ds(off, tk)]
        vb = v_ref[pl.ds(off, tk), :]
        jj = off + lax.broadcasted_iota(jnp.int32, (tk, tq), 0)
        vis = (jj >= st) & (jj < en)
        dk = jnp.zeros((HD, tk), f32)
        dv = jnp.zeros((HD, tk), f32)
        for h in range(nh):
            s = dg(kb, qs[h], 1, 0) * SCALE
            p = jnp.exp(jnp.where(vis, s - ls[h], NEG))
            dp = dg(vb, dos[h], 1, 0)
            dsc = (p * (dp - dl[h])).astype(bf16)
            dq_ref[h * HD : (h + 1) * HD, :] += dg(kT, dsc, 1, 0)
            dk = dk + dg(qs[h], dsc, 1, 1)
            dv = dv + dg(dos[h], p.astype(bf16), 1, 1)
        dk_ref[:, pl.ds(off, tk)] += dk
        dv_ref[:, pl.ds(off, tk)] += dv
        return 0

    lax.fori_loop(lo, hi, body, 0)


def attn_bwd(qT, doT, oT, lse, st, en, k, kT, v, tq=256, tk=256):
    n, S = qT.shape
    nh = n // HD
    blk = lambda r: pl.BlockSpec((r, tq), lambda i: (0, i))
    full = lambda s: pl.BlockSpec(s, lambda i: (0, 0))
    return pl.pallas_call(
        functools.partial(attn_bwd_kernel, nh, tq, tk),
        grid=(S // tq,),
        in_specs=[
            blk(n), blk(n), blk(n), blk(nh), blk(1), blk(1),
            full((S, HD)), full((HD, S)), full((S, HD)),
        ],
        out_specs=[blk(n), full((HD, S)), full((HD, S))],
        out_shape=[
            jax.ShapeDtypeStruct((n, S), f32),
            jax.ShapeDtypeStruct((HD, S), f32),
            jax.ShapeDtypeStruct((HD, S), f32),
        ],
        cost_estimate=pl.CostEstimate(
            flops=5 * S * S * n, bytes_accessed=10 * n * S, transcendentals=S * S * nh // 2
        ),
        name="attn_bwd",
    )(qT, doT, oT, lse, st, en, k, kT, v)


MESH = pl.DeviceIdType.MESH
CH = 16


class Place:
    def __init__(self, nc, nf):
        self.nc, self.nf, self.nz = nc, nf, nc // 2
        self.c = lax.axis_index("ctx")
        self.f = lax.axis_index("fsdp")
        self.z = self.c // 2
        self.j = self.c % 2
        self.sib = self.z * 2 + (1 - self.j)
        self.low = self.z > 0
        self.high = self.z < self.nz - 1


def remote(src, dst, ss, rs, axis, idx):
    return pltpu.make_async_remote_copy(
        src_ref=src, dst_ref=dst, send_sem=ss, recv_sem=rs, device_id={axis: idx}, device_id_type=MESH
    )


def greet(p, line=True, ctx=False, fsdp=False):
    sem = pltpu.get_barrier_semaphore()
    count = 0

    def tell(axis, idx):
        pl.semaphore_signal(sem, inc=1, device_id={axis: idx}, device_id_type=MESH)

    if ctx:
        for k in range(1, p.nc):
            tell("ctx", lax.rem(p.c + k, p.nc))
        count = p.nc - 1
    elif line:
        tell("ctx", p.sib)

        @pl.when(p.low)
        def _():
            tell("ctx", p.c - 2)

        @pl.when(p.high)
        def _():
            tell("ctx", p.c + 2)

        count = 1 + p.low.astype(jnp.int32) + p.high.astype(jnp.int32)
    if fsdp:
        for k in range(1, p.nf):
            tell("fsdp", lax.rem(p.f + k, p.nf))
        count = count + p.nf - 1
    pl.semaphore_wait(sem, count)


def each(fn, start, size, step=CH):
    def body(r, _):
        fn(pl.ds(pl.multiple_of(start + r * step, step), step))
        return 0

    lax.fori_loop(0, size // step, body, 0)


class Gather:
    def __init__(self, p, own, full, rows, ss, rs, ls):
        self.p, self.own, self.full, self.rows, self.ss, self.rs, self.ls = p, own, full, rows, ss, rs, ls

    def slot(self, k):
        return self.full.at[k, self.rows]

    def copy(self, way, k, to, src=None):
        return remote(self.slot(k) if src is None else src, self.slot(k), self.ss.at[way, k], self.rs.at[k], "ctx", to)

    def first(self):
        p = self.p
        src = self.own.at[self.rows]

        @pl.when(p.high)
        def _():
            self.copy(0, p.c, p.c + 2, src).start()

        @pl.when(p.low)
        def _():
            self.copy(1, p.c, p.c - 2, src).start()

        self.copy(2, p.c, p.sib, src).start()
        pltpu.make_async_copy(src, self.slot(p.c), self.ls).start()

    def step(self, t):
        p = self.p

        @pl.when(p.z - t >= 0)
        def _():
            k = p.c - 2 * t
            self.copy(2, k, p.sib).wait_recv()

            @pl.when(p.high)
            def _():
                self.copy(0, k, p.c + 2).start()

            self.copy(2, k, p.sib).start()

        @pl.when(p.z + t < p.nz)
        def _():
            k = p.c + 2 * t
            self.copy(2, k, p.sib).wait_recv()

            @pl.when(p.low)
            def _():
                self.copy(1, k, p.c - 2).start()

            self.copy(2, k, p.sib).start()

    def finish(self):
        p = self.p
        src = self.own.at[self.rows]
        for y in range(p.nz):
            self.copy(2, 2 * y + 1 - p.j, p.sib).wait_recv()
        for y in range(p.nz):
            k = 2 * y + p.j
            self.copy(2, k, p.sib).wait_send()

            @pl.when(p.high & (y <= p.z))
            def _(k=k):
                self.copy(0, k, p.c + 2).wait_send()

            @pl.when(p.low & (y >= p.z))
            def _(k=k):
                self.copy(1, k, p.c - 2).wait_send()

        pltpu.make_async_copy(src, self.slot(p.c), self.ls).wait()

    def all_steps(self):
        return [self.first] + [functools.partial(self.step, t) for t in range(1, self.p.nz)]


class Scatter:
    def __init__(self, p, part, a, x, u, d, acc, start, size, sems):
        self.p, self.part, self.a, self.x, self.u, self.d, self.acc = p, part, a, x, u, d, acc
        self.start, self.size, self.rows, self.sems = start, size, pl.ds(start, size), sems

    def cross(self, y):
        p = self.p
        return remote(
            self.part.at[2 * y + 1 - p.j, self.rows], self.x.at[y, self.rows],
            self.sems.at[0, y], self.sems.at[1, y], "ctx", p.sib,
        )

    def load(self, y):
        return pltpu.make_async_copy(
            self.part.at[2 * y + self.p.j, self.rows], self.a.at[y, self.rows], self.sems.at[2, y]
        )

    def go_up(self, y):
        return remote(
            self.a.at[y, self.rows], self.u.at[y, self.rows], self.sems.at[3, y], self.sems.at[4, y], "ctx", self.p.c + 2
        )

    def go_down(self, y):
        return remote(
            self.a.at[y, self.rows], self.d.at[y, self.rows], self.sems.at[5, y], self.sems.at[6, y], "ctx", self.p.c - 2
        )

    def begin(self):
        nz = self.p.nz
        order = []
        for i in range(nz):
            order += [y for y in (nz - 1 - i, i) if y not in order]
        for y in order:
            self.cross(y).start()
            self.load(y).start()

    def add(self, y, extra):
        def fn(r):
            v = self.a[y, r].astype(f32) + self.x[y, r].astype(f32)
            if extra is not None:
                v = v + extra[y, r].astype(f32)
            self.a[y, r] = v.astype(bf16)

        each(fn, self.start, self.size)

    def step(self, i):
        p = self.p
        up, down = p.nz - 1 - i, i

        @pl.when(p.z < up)
        def _():
            self.load(up).wait()
            self.cross(up).wait_recv()

            @pl.when(p.low)
            def _():
                self.go_up(up).wait_recv()
                self.add(up, self.u)

            @pl.when(p.z == 0)
            def _():
                self.add(up, None)

            self.go_up(up).start()

        @pl.when(p.z > down)
        def _():
            self.load(down).wait()
            self.cross(down).wait_recv()

            @pl.when(p.high)
            def _():
                self.go_down(down).wait_recv()
                self.add(down, self.d)

            @pl.when(p.z == p.nz - 1)
            def _():
                self.add(down, None)

            self.go_down(down).start()

    def total(self):
        p = self.p
        z = p.z
        self.load(z).wait()
        self.cross(z).wait_recv()

        def both(r):
            self.acc[r] = self.a[z, r].astype(f32) + self.x[z, r].astype(f32)

        each(both, self.start, self.size)

        @pl.when(p.low)
        def _():
            self.go_up(z).wait_recv()

            def fn(r):
                self.acc[r] += self.u[z, r].astype(f32)

            each(fn, self.start, self.size)

        @pl.when(p.high)
        def _():
            self.go_down(z).wait_recv()

            def fn(r):
                self.acc[r] += self.d[z, r].astype(f32)

            each(fn, self.start, self.size)

    def finish(self):
        p = self.p
        for y in range(p.nz):
            self.cross(y).wait_send()

            @pl.when(p.z < y)
            def _(y=y):
                self.go_up(y).wait_send()

            @pl.when(p.z > y)
            def _(y=y):
                self.go_down(y).wait_send()

    def all_steps(self):
        return [functools.partial(self.step, i) for i in range(self.p.nz - 1)]


def interleave(first, second):
    for i in range(max(len(first), len(second))):
        if i < len(first):
            first[i]()
        if i < len(second):
            second[i]()


class Peers:
    def __init__(self, p, pick, ss, rs, keep, ls):
        self.p, self.pick, self.ss, self.rs, self.keep, self.ls = p, pick, ss, rs, keep, ls

    def copy(self, k):
        p = self.p
        to = lax.rem(p.f + k, p.nf)
        src, dst = self.pick(to)
        return remote(src, dst, self.ss.at[k], self.rs.at[k], "fsdp", to)

    def start(self):
        for k in range(1, self.p.nf):
            self.copy(k).start()
        if self.keep is not None:
            pltpu.make_async_copy(*self.keep, self.ls).start()

    def wait(self):
        for k in range(1, self.p.nf):
            self.copy(k).wait()
        if self.keep is not None:
            pltpu.make_async_copy(*self.keep, self.ls).wait()


DMA = pltpu.SemaphoreType.DMA


def gather_sems(nc):
    return [DMA((3, nc)), DMA((nc,)), DMA]


def scatter_scratch(nz, T, E):
    return [pltpu.VMEM((nz, T, E), bf16)] * 4 + [pltpu.VMEM((T, E), f32)]


def params(cid):
    return pltpu.CompilerParams(collective_id=cid, has_side_effects=True, vmem_limit_bytes=60 * 1024 * 1024)


ANY = pl.BlockSpec(memory_space=pl.ANY)
VM = pl.BlockSpec(memory_space=pltpu.VMEM)


def open_kernel(nc, nf, tok, ids, wl, row, ids_row, w, gss, grs, gls, iss, irs, ils, ass, ars, fss, frs, als):
    p = Place(nc, nf)
    greet(p, ctx=True, fsdp=True)
    T = tok.shape[0]
    g = Gather(p, tok, row, pl.ds(0, T), gss, grs, gls)

    def id_copy(k):
        to = lax.rem(p.c + k, nc)
        return remote(ids, ids_row.at[p.c], iss.at[k], irs.at[k], "ctx", to)

    def block(k):
        to = lax.rem(p.c + k, nc)
        return remote(wl.at[to], w.at[p.c, p.f], ass.at[k], ars.at[k], "ctx", to)

    def onward(c, k, m):
        to = lax.rem(p.f + m, nf)
        return remote(w.at[c, p.f], w.at[c, p.f], fss.at[k, m], frs.at[k, m], "fsdp", to)

    def source(k):
        return lax.rem(p.c + nc - k, nc)

    keep_ids = pltpu.make_async_copy(ids, ids_row.at[p.c], ils)
    keep_w = pltpu.make_async_copy(wl.at[p.c], w.at[p.c, p.f], als)
    keep_w.start()
    keep_ids.start()
    for k in range(1, nc):
        block(k).start()
        id_copy(k).start()
    g.first()
    keep_w.wait()

    def spread(k):
        for m in range(1, nf):
            onward(source(k), k, m).start()

    spread(0)
    for k in range(1, nc):
        block(k).wait_recv()
        spread(k)
    for t in range(1, p.nz):
        g.step(t)
    g.finish()
    keep_ids.wait()
    for k in range(1, nc):
        block(k).wait_send()
        id_copy(k).wait()
    for k in range(nc):
        for m in range(1, nf):
            onward(source(k), k, m).wait()


def open_call(nc, nf, tok, ids, wl):
    T, E = tok.shape
    _, R, A = wl.shape
    return pl.pallas_call(
        functools.partial(open_kernel, nc, nf),
        in_specs=[ANY, ANY, ANY],
        out_specs=[ANY, ANY, ANY],
        out_shape=[
            jax.ShapeDtypeStruct((nc, T, E), bf16),
            jax.ShapeDtypeStruct((nc,) + ids.shape, jnp.int32),
            jax.ShapeDtypeStruct((nc, nf, R, A), bf16),
        ],
        scratch_shapes=gather_sems(nc)
        + [DMA((nc,)), DMA((nc,)), DMA, DMA((nc,)), DMA((nc,)), DMA((nc, nf)), DMA((nc, nf)), DMA],
        compiler_params=params(1),
        name="open_row",
    )(tok, ids, wl)


def middle_kernel(
    nc, nf, parts, part, tok, og, g, wl, hid, n2, dm, w,
    a, x, u, d, acc, own, dmo, rsem, nss, nrs, nls, dss, drs, dls, fss, frs, fls,
):
    p = Place(nc, nf)
    greet(p, fsdp=True)
    T = tok.shape[0]
    size = T // parts
    rs = [Scatter(p, part, a, x, u, d, acc, q * size, size, rsem.at[q]) for q in range(parts)]
    ag = [
        Gather(p, own, n2, pl.ds(q * size, size), nss.at[q], nrs.at[q], nls.at[q]) for q in range(parts)
    ]
    dg_ = Gather(p, dmo, dm, pl.ds(0, T), dss, drs, dls)
    peers = Peers(p, lambda to: (wl, w.at[:, p.f]), fss, frs, (wl, w.at[:, p.f]), fls)

    rs[0].begin()

    def dm_rows(r):
        dmo[r] = (RES * og[r].astype(f32)).astype(bf16)

    each(dm_rows, 0, T)
    peers.start()
    for q in range(1, parts):
        rs[q].begin()

    def close(q):
        rs[q].total()

        def fn(r):
            h = tok[r].astype(f32) + RES * acc[r]
            hid[r] = h
            own[r] = (h * lax.rsqrt(jnp.mean(h * h, axis=-1, keepdims=True) + EPS) * g[...]).astype(bf16)

        each(fn, q * size, size)
        ag[q].first()

    pending = dg_.all_steps()
    for q in range(parts):
        interleave(pending, rs[q].all_steps())
        close(q)
        pending = ag[q].all_steps()[1:]
    for s in pending:
        s()
    for q in range(parts):
        ag[q].finish()
        rs[q].finish()
    dg_.finish()
    peers.wait()


def middle_call(nc, nf, parts, part, tok, og, g, wl):
    T, E = tok.shape
    _, R, M = wl.shape
    nz = nc // 2
    return pl.pallas_call(
        functools.partial(middle_kernel, nc, nf, parts),
        in_specs=[ANY, VM, VM, VM, ANY],
        out_specs=[VM, ANY, ANY, ANY],
        out_shape=[
            jax.ShapeDtypeStruct((T, E), f32),
            jax.ShapeDtypeStruct((nc, T, E), bf16),
            jax.ShapeDtypeStruct((nc, T, E), bf16),
            jax.ShapeDtypeStruct((nc, nf, R, M), bf16),
        ],
        scratch_shapes=scatter_scratch(nz, T, E)
        + [pltpu.VMEM((T, E), bf16), pltpu.VMEM((T, E), bf16), DMA((parts, 7, nz))]
        + [DMA((parts, 3, nc)), DMA((parts, nc)), DMA((parts,))]
        + gather_sems(nc)
        + [DMA((nf,)), DMA((nf,)), DMA],
        compiler_params=params(2),
        name="attn_to_mlp",
    )(part, tok, og, g, wl)


def turn_kernel(nc, nf, parts, fold, *refs):
    it = iter(refs)
    take = lambda n: [next(it) for _ in range(n)]
    (part,) = take(1)
    mpart = next(it) if fold else None
    hid, og, g, gw, dh, da = take(6)
    lay = next(it) if fold else None
    gg, y = take(2)
    a, x, u, d, acc, own, rsem = take(7)
    nss, nrs, nls, fss, frs, fls = take(6)
    p = Place(nc, nf)
    greet(p, fsdp=True)
    T, E = hid.shape
    size = T // parts
    rs = [Scatter(p, part, a, x, u, d, acc, q * size, size, rsem.at[q]) for q in range(parts)]
    ag = [
        Gather(p, own, da, pl.ds(q * size, size), nss.at[q], nrs.at[q], nls.at[q]) for q in range(parts)
    ]
    peers = Peers(p, lambda to: (gw.at[:, to], y.at[p.f]), fss, frs, (gw.at[:, p.f], y.at[p.f]), fls)
    for q in range(parts):
        rs[q].begin()
    peers.start()
    gg[...] = jnp.zeros_like(gg)
    if fold:
        a2, x2, u2, d2, msem = take(5)
        ms = Scatter(p, mpart, a2, x2, u2, d2, acc, 0, T, msem)

    def close(q):
        rs[q].total()

        def fn(r):
            h = hid[r]
            inv = lax.rsqrt(jnp.mean(h * h, axis=-1, keepdims=True) + EPS)
            xn = h * inv
            dn = acc[r]
            e = dn * g[...]
            v = og[r].astype(f32) + inv * (e - xn * jnp.mean(e * xn, axis=-1, keepdims=True))
            dh[r] = v
            own[r] = (RES * v).astype(bf16)
            gg[...] += jnp.sum((xn * dn).reshape(CH // 8, 8, E), axis=0)

        each(fn, q * size, size)
        ag[q].first()

    pending = []
    for q in range(parts):
        interleave(pending, rs[q].all_steps())
        if fold and q == parts - 1:
            ms.begin()
        close(q)
        pending = ag[q].all_steps()[1:]
    interleave(pending, ms.all_steps() if fold else [])
    if fold:
        ms.total()

        def out(r):
            lay[r] = (hid[r] + RES * acc[r]).astype(bf16)

        each(out, 0, T)
        ms.finish()
    for q in range(parts):
        ag[q].finish()
        rs[q].finish()
    peers.wait()


def turn_call(nc, nf, parts, part, mpart, hid, og, g, gw):
    T, E = hid.shape
    _, _, R, M = gw.shape
    nz = nc // 2
    fold = mpart is not None
    return pl.pallas_call(
        functools.partial(turn_kernel, nc, nf, parts, fold),
        in_specs=[ANY] * (1 + fold) + [VM, VM, VM, ANY],
        out_specs=[VM, ANY] + [VM] * fold + [VM, ANY],
        out_shape=[jax.ShapeDtypeStruct((T, E), f32), jax.ShapeDtypeStruct((nc, T, E), bf16)]
        + [jax.ShapeDtypeStruct((T, E), bf16)] * fold
        + [jax.ShapeDtypeStruct((8, E), f32), jax.ShapeDtypeStruct((nf, nc, R, M), bf16)],
        scratch_shapes=scatter_scratch(nz, T, E)
        + [pltpu.VMEM((T, E), bf16), DMA((parts, 7, nz))]
        + [DMA((parts, 3, nc)), DMA((parts, nc)), DMA((parts,))]
        + [DMA((nf,)), DMA((nf,)), DMA]
        + ([pltpu.VMEM((nz, T, E), bf16)] * 4 + [DMA((7, nz))]) * fold,
        compiler_params=params(3),
        name="mlp_to_attn",
    )(*([part, mpart] if fold else [part]), hid, og, g, gw)


def close_kernel(
    nc, nf, parts, part, tok, dh, g, gw, ggm, dx, gout, ggout,
    a, x, u, d, acc, y, zb, gg, gbuf, gsum, gfin, rsem, fss, frs, fls, css, crs, cls, s1, r1, s2, r2, l2,
):
    p = Place(nc, nf)
    greet(p, ctx=True, fsdp=True)
    T, E = tok.shape
    R = gw.shape[2]
    size = T // parts
    rs = [Scatter(p, part, a, x, u, d, acc, q * size, size, rsem.at[q]) for q in range(parts)]
    peers = Peers(p, lambda to: (gw.at[:, to], y.at[p.f]), fss, frs, (gw.at[:, p.f], y.at[p.f]), fls)
    for q in range(parts):
        rs[q].begin()
    peers.start()
    gg[...] = jnp.zeros_like(gg)

    def piece(k):
        to = lax.rem(p.c + k, nc)
        return remote(zb.at[to], gout.at[p.c], css.at[k], crs.at[k], "ctx", to)

    mine = pltpu.make_async_copy(zb.at[p.c], gout.at[p.c], cls)

    def grads():
        peers.wait()
        for c in range(nc):

            def fn(r):
                v = y[0, c, r].astype(f32)
                for m in range(1, nf):
                    v = v + y[m, c, r].astype(f32)
                zb[c, r] = v.astype(bf16)

            each(fn, 0, R)
        for k in range(1, nc):
            piece(k).start()
        mine.start()

    def close(q):
        rs[q].total()

        def fn(r):
            t = tok[r].astype(f32)
            inv = lax.rsqrt(jnp.mean(t * t, axis=-1, keepdims=True) + EPS)
            xn = t * inv
            dn = acc[r]
            e = dn * g[...]
            dx[r] = dh[r] + inv * (e - xn * jnp.mean(e * xn, axis=-1, keepdims=True))
            gg[...] += jnp.sum((xn * dn).reshape(CH // 8, 8, E), axis=0)

        each(fn, q * size, size)

    for q in range(parts):
        steps = rs[q].all_steps()
        for s in steps:
            s()
        if q == 0:
            grads()
        close(q)

    groups = E // 128
    sa = jnp.sum(gg[...], axis=0, keepdims=True)
    sm = jnp.sum(ggm[...], axis=0, keepdims=True)
    for i in range(groups):
        gbuf[p.f, i] = jnp.concatenate(
            [sa[:, i * 128 : (i + 1) * 128], sm[:, i * 128 : (i + 1) * 128], jnp.zeros((6, 128), f32)], axis=0
        )

    def over(k):
        to = lax.rem(p.f + k, nf)
        return remote(gbuf.at[p.f], gbuf.at[p.f], s1.at[k], r1.at[k], "fsdp", to)

    for k in range(1, nf):
        over(k).start()
    for k in range(1, nf):
        over(k).wait()
    v = gbuf[0]
    for m in range(1, nf):
        v = v + gbuf[m]
    gsum[...] = v
    per = 128 // R

    def along(k):
        to = lax.rem(p.c + k, nc)
        return remote(gsum.at[(to * nf + p.f) // per], gfin.at[p.c], s2.at[k], r2.at[k], "ctx", to)

    for k in range(1, nc):
        along(k).start()
    own = pltpu.make_async_copy(gsum.at[(p.c * nf + p.f) // per], gfin.at[p.c], l2)
    own.start()
    own.wait()
    for k in range(1, nc):
        along(k).wait()
    t = gfin[0]
    for m in range(1, nc):
        t = t + gfin[m]
    ggout[...] = t
    for k in range(1, nc):
        piece(k).wait()
    mine.wait()
    for q in range(parts):
        rs[q].finish()


def close_call(nc, nf, parts, part, tok, dh, g, gw, ggm):
    T, E = tok.shape
    _, _, R, A = gw.shape
    nz = nc // 2
    return pl.pallas_call(
        functools.partial(close_kernel, nc, nf, parts),
        in_specs=[ANY, VM, VM, VM, ANY, VM],
        out_specs=[VM, ANY, VM],
        out_shape=[
            jax.ShapeDtypeStruct((T, E), f32),
            jax.ShapeDtypeStruct((nc, R, A), bf16),
            jax.ShapeDtypeStruct((8, 128), f32),
        ],
        scratch_shapes=scatter_scratch(nz, T, E)
        + [
            pltpu.VMEM((nf, nc, R, A), bf16),
            pltpu.VMEM((nc, R, A), bf16),
            pltpu.VMEM((8, E), f32),
            pltpu.VMEM((nf, E // 128, 8, 128), f32),
            pltpu.VMEM((E // 128, 8, 128), f32),
            pltpu.VMEM((nc, 8, 128), f32),
            DMA((parts, 7, nz)),
        ]
        + [DMA((nf,)), DMA((nf,)), DMA, DMA((nc,)), DMA((nc,)), DMA]
        + [DMA((nf,)), DMA((nf,)), DMA((nc,)), DMA((nc,)), DMA],
        compiler_params=params(4),
        name="close_row",
    )(part, tok, dh, g, gw, ggm)


def rms(v):
    inv = lax.rsqrt(jnp.mean(v * v, axis=-1, keepdims=True) + EPS)
    return v * inv, inv


def rms_back(x, inv, e):
    return inv * (e - x * jnp.mean(e * x, axis=-1, keepdims=True))


def rotate(v, cos, sin, sign):
    heads = v.shape[0] // HD
    v = v.reshape(heads, 2, HD // 2, v.shape[1])
    a, b = v[:, 0], v[:, 1]
    s = sign * sin
    return jnp.stack([a * cos - b * s, b * cos + a * s], axis=1).reshape(heads * HD, -1)


def local(
    tokens, seq_ids, positions, block_ids, gain_attn, w_query, w_key, w_value, w_out,
    gain_mlp, w_gate, w_up, w_down, out_grad,
):
    nc = lax.axis_size("ctx")
    nf = lax.axis_size("fsdp")
    nz = nc // 2
    T, E = tokens.shape[1:]
    R = w_query.shape[0]
    S = T * nc
    FFL = w_gate.shape[1] // nc
    nh = QUERY_HEADS // nc
    rep = nc // KEY_VALUE_HEADS
    QW = nh * HD
    KO, VO, OO, GO = QW, QW + HD, QW + 2 * HD, 2 * QW + 2 * HD
    tok, og = tokens[0], out_grad[0]

    def cols(w):
        return w.astype(bf16).reshape(R, nc, -1)

    def kv_cols(w):
        return jnp.repeat(w.astype(bf16).reshape(R, KEY_VALUE_HEADS, HD), rep, axis=1)

    def blocks(parts):
        return jnp.transpose(jnp.concatenate(parts, axis=2), (1, 0, 2))

    def exchange(w):
        return lax.all_to_all(w, "ctx", 0, 0, tiled=True)

    gains = jnp.stack([gain_attn, gain_mlp], axis=1).astype(bf16)
    gains = jnp.broadcast_to(jnp.pad(gains, ((0, 0), (0, 126)))[:, None], (R, nc, 128))
    wl = blocks([cols(w_query), kv_cols(w_key), kv_cols(w_value), cols(w_out), gains])
    ids = jnp.pad(jnp.concatenate([seq_ids, positions, block_ids], axis=0), ((0, 5), (0, 0)))
    row_tok, ids, wa = open_call(nc, nf, tok, ids, wl)
    wa = wa.reshape(E, -1)
    g_attn, g_mlp = wa[:, GO].astype(f32)[None], wa[:, GO + 1].astype(f32)[None]

    wm = exchange(blocks([cols(w_gate), cols(w_up), cols(w_down)]))

    seq, pos, blk = (ids[:, i].reshape(S) for i in range(3))
    place = jnp.arange(S, dtype=jnp.int32)
    cut = jnp.sum((seq == 0).astype(jnp.int32))
    first = place - pos
    last = jnp.minimum(first + BLOCK * (blk + 1), jnp.where(seq == 0, cut, S))
    st, en = first[None], last[None]
    freq = ROPE_BASE ** (-(jnp.arange(HD // 2, dtype=f32) * 2.0) / HD)
    ang = freq[:, None] * pos.astype(f32)[None, :]
    cos, sin = jnp.cos(ang), jnp.sin(ang)

    x1r, _ = rms(row_tok.reshape(S, E).astype(f32))
    n1 = (x1r * g_attn).astype(bf16)
    w_qkv, w_o = wa[:, :OO], wa[:, OO:GO]
    qkv = dg(w_qkv, n1, 0, 1)
    qkT = rotate(qkv[:VO], cos, sin, 1.0).astype(bf16)
    qT, kT = qkT[:QW], qkT[QW:]
    vT = qkv[VO:].astype(bf16)
    k, v = kT.T, vT.T
    oT, oTb, lse = attn_fwd(qT, k, vT, st, en)
    attn = dg(oTb, w_o, 0, 1).astype(bf16).reshape(nc, T, E)

    hidden, n2, dm, wm = middle_call(nc, nf, 1, attn, tok, og, g_mlp, wm)
    n2, dm, wm = n2.reshape(S, E), dm.reshape(S, E), wm.reshape(E, -1)
    w_gu, w_d = wm[:, : 2 * FFL], wm[:, 2 * FFL :]
    gu = dg(n2, w_gu, 1, 0)
    gate, up = gu[:, :FFL], gu[:, FFL:]
    sg = jax.nn.sigmoid(gate)
    act = (gate * sg * up).astype(bf16)
    d_act = dg(dm, w_d, 1, 0)
    d_gate = (d_act * up * sg * (1.0 + gate * (1.0 - sg))).astype(bf16)
    d_up = (d_act * gate * sg).astype(bf16)
    d_gu = jnp.concatenate([d_gate, d_up], axis=1)
    dn2 = dg(d_gu, w_gu, 1, 1).astype(bf16).reshape(nc, T, E)
    mlp = dg(act, w_d, 1, 1).astype(bf16).reshape(nc, T, E)
    gm = jnp.concatenate([dg(n2, d_gu, 0, 0), dg(dm, act, 0, 0)], axis=1).astype(bf16)
    gm = gm.reshape(nc, nf, R, -1)

    if nz <= 4:
        dh, da, layer_out, ggm, gm = turn_call(nc, nf, 1, dn2, mlp, hidden, og, g_mlp, gm)
    else:
        dh, da, ggm, gm = turn_call(nc, nf, 1, dn2, None, hidden, og, g_mlp, gm)
        mlp = lax.psum_scatter(mlp.reshape(S, E), "ctx", scatter_dimension=0, tiled=True)
        layer_out = (hidden + RES * mlp.astype(f32)).astype(bf16)
    da = da.reshape(S, E)
    gm = exchange(jnp.sum(gm.astype(f32), axis=0).astype(bf16))

    doT = dg(w_o, da, 0, 1).astype(bf16)
    dqT, dkT, dvT = attn_bwd(qT, doT, oT, lse, st, en, k, kT, v)
    dqk = rotate(jnp.concatenate([dqT, dkT], axis=0) * SCALE, cos, sin, -1.0).astype(bf16)
    dqkv = jnp.concatenate([dqk, dvT.astype(bf16)], axis=0)
    dn1 = dg(dqkv, w_qkv, 0, 1).astype(bf16).reshape(nc, T, E)
    ga = jnp.concatenate([dg(n1, dqkv, 0, 1), dg(da, oTb, 0, 1)], axis=1).astype(bf16)
    input_grad, ga, gains = close_call(nc, nf, 1, dn1, tok, dh, g_attn, ga.reshape(nc, nf, R, -1), ggm)
    at = lax.rem((lax.axis_index("ctx") * nf + lax.axis_index("fsdp")) * R, 128)
    gains = lax.dynamic_slice_in_dim(gains, at, R, 1)

    def rows(g):
        return jnp.transpose(g.astype(f32), (1, 0, 2)).reshape(R, -1)

    def kv_rows(g):
        g = g.astype(f32).reshape(KEY_VALUE_HEADS, rep, R, HD)
        return jnp.transpose(jnp.sum(g, axis=1), (1, 0, 2)).reshape(R, -1)

    return (
        layer_out[None],
        input_grad[None],
        gains[0],
        rows(ga[:, :, :KO]),
        kv_rows(ga[:, :, KO:VO]),
        kv_rows(ga[:, :, VO:OO]),
        rows(ga[:, :, OO:]),
        gains[1],
        rows(gm[:, :, :FFL]),
        rows(gm[:, :, FFL : 2 * FFL]),
        rows(gm[:, :, 2 * FFL :]),
    )


def solution(mesh):
    w1, w2 = P(("ctx", "fsdp")), P(("ctx", "fsdp"), None)
    act, ids = P("fsdp", "ctx", None), P("fsdp", "ctx")
    return jax.shard_map(
        local,
        mesh=mesh,
        in_specs=(act, ids, ids, ids, w1, w2, w2, w2, w2, w1, w2, w2, w2, act),
        out_specs=(act, act, w1, w2, w2, w2, w2, w1, w2, w2, w2),
        check_vma=False,
    )
```

```python
import functools

import jax
import jax.numpy as jnp
from jax import lax
from jax.experimental import pallas as pl
from jax.experimental.pallas import tpu as pltpu
from jax.sharding import PartitionSpec as P

QUERY_HEADS = 32
KEY_VALUE_HEADS = 8
HD = 64
BLOCK = 256
EPS = 1e-05
ROPE_BASE = 10000000.0
SCALE = 0.015625
RES = 0.22
NEG = -1e30
bf16 = jnp.bfloat16
f32 = jnp.float32


def dg(a, b, ca, cb):
    return lax.dot_general(a, b, (((ca,), (cb,)), ((), ())), preferred_element_type=f32)


def attn_fwd_kernel(nh, tq, tk, q_ref, k_ref, v_ref, st_ref, en_ref, o_ref, ob_ref, l_ref):
    st = st_ref[...]
    en = en_ref[...]
    lo = jnp.min(st) // tk
    hi = (jnp.max(en) + tk - 1) // tk
    qs = [q_ref[h * HD : (h + 1) * HD, :] for h in range(nh)]

    def body(j, c):
        off = pl.multiple_of(j * tk, tk)
        kb = k_ref[pl.ds(off, tk), :]
        vb = v_ref[:, pl.ds(off, tk)]
        jj = off + lax.broadcasted_iota(jnp.int32, (tk, tq), 0)
        vis = (jj >= st) & (jj < en)
        out = []
        for h in range(nh):
            m, l, a = c[h]
            s = dg(kb, qs[h], 1, 0) * SCALE
            s = jnp.where(vis, s, NEG)
            mn = jnp.maximum(m, jnp.max(s, axis=0, keepdims=True))
            p = jnp.where(vis, jnp.exp(s - mn), 0.0)
            sh = jnp.exp(m - mn)
            l = l * sh + jnp.sum(p, axis=0, keepdims=True)
            a = a * sh + dg(vb, p.astype(bf16), 1, 0)
            out.append((mn, l, a))
        return tuple(out)

    init = tuple(
        (jnp.full((1, tq), NEG, f32), jnp.zeros((1, tq), f32), jnp.zeros((HD, tq), f32))
        for _ in range(nh)
    )
    res = lax.fori_loop(lo, hi, body, init)
    for h in range(nh):
        m, l, a = res[h]
        o = a / l
        o_ref[h * HD : (h + 1) * HD, :] = o
        ob_ref[h * HD : (h + 1) * HD, :] = o.astype(bf16)
        l_ref[h : h + 1, :] = m + jnp.log(l)


def attn_fwd(qT, k, vT, st, en, tq=256, tk=256):
    n, S = qT.shape
    nh = n // HD
    blk = lambda r: pl.BlockSpec((r, tq), lambda i: (0, i))
    full = lambda s: pl.BlockSpec(s, lambda i: (0, 0))
    return pl.pallas_call(
        functools.partial(attn_fwd_kernel, nh, tq, tk),
        grid=(S // tq,),
        in_specs=[blk(n), full((S, HD)), full((HD, S)), blk(1), blk(1)],
        out_specs=[blk(n), blk(n), blk(nh)],
        out_shape=[
            jax.ShapeDtypeStruct((n, S), f32),
            jax.ShapeDtypeStruct((n, S), bf16),
            jax.ShapeDtypeStruct((nh, S), f32),
        ],
        cost_estimate=pl.CostEstimate(
            flops=2 * S * S * n, bytes_accessed=8 * n * S, transcendentals=S * S * nh // 2
        ),
        name="attn_fwd",
    )(qT, k, vT, st, en)


def attn_bwd_kernel(
    nh, tq, tk, q_ref, do_ref, o_ref, lse_ref, st_ref, en_ref, k_ref, kT_ref, v_ref, dq_ref, dk_ref, dv_ref
):
    i = pl.program_id(0)

    @pl.when(i == 0)
    def _():
        dk_ref[...] = jnp.zeros_like(dk_ref)
        dv_ref[...] = jnp.zeros_like(dv_ref)

    st = st_ref[...]
    en = en_ref[...]
    lo = jnp.min(st) // tk
    hi = (jnp.max(en) + tk - 1) // tk
    qs = [q_ref[h * HD : (h + 1) * HD, :] for h in range(nh)]
    dos = [do_ref[h * HD : (h + 1) * HD, :] for h in range(nh)]
    dl = [
        jnp.sum(dos[h].astype(f32) * o_ref[h * HD : (h + 1) * HD, :], axis=0, keepdims=True)
        for h in range(nh)
    ]
    ls = [lse_ref[h : h + 1, :] for h in range(nh)]
    dq_ref[...] = jnp.zeros_like(dq_ref)

    def body(j, _):
        off = pl.multiple_of(j * tk, tk)
        kb = k_ref[pl.ds(off, tk), :]
        kT = kT_ref[:, pl.ds(off, tk)]
        vb = v_ref[pl.ds(off, tk), :]
        jj = off + lax.broadcasted_iota(jnp.int32, (tk, tq), 0)
        vis = (jj >= st) & (jj < en)
        dk = jnp.zeros((HD, tk), f32)
        dv = jnp.zeros((HD, tk), f32)
        for h in range(nh):
            s = dg(kb, qs[h], 1, 0) * SCALE
            p = jnp.exp(jnp.where(vis, s - ls[h], NEG))
            dp = dg(vb, dos[h], 1, 0)
            dsc = (p * (dp - dl[h])).astype(bf16)
            dq_ref[h * HD : (h + 1) * HD, :] += dg(kT, dsc, 1, 0)
            dk = dk + dg(qs[h], dsc, 1, 1)
            dv = dv + dg(dos[h], p.astype(bf16), 1, 1)
        dk_ref[:, pl.ds(off, tk)] += dk
        dv_ref[:, pl.ds(off, tk)] += dv
        return 0

    lax.fori_loop(lo, hi, body, 0)


def attn_bwd(qT, doT, oT, lse, st, en, k, kT, v, tq=256, tk=256):
    n, S = qT.shape
    nh = n // HD
    blk = lambda r: pl.BlockSpec((r, tq), lambda i: (0, i))
    full = lambda s: pl.BlockSpec(s, lambda i: (0, 0))
    return pl.pallas_call(
        functools.partial(attn_bwd_kernel, nh, tq, tk),
        grid=(S // tq,),
        in_specs=[
            blk(n), blk(n), blk(n), blk(nh), blk(1), blk(1),
            full((S, HD)), full((HD, S)), full((S, HD)),
        ],
        out_specs=[blk(n), full((HD, S)), full((HD, S))],
        out_shape=[
            jax.ShapeDtypeStruct((n, S), f32),
            jax.ShapeDtypeStruct((HD, S), f32),
            jax.ShapeDtypeStruct((HD, S), f32),
        ],
        cost_estimate=pl.CostEstimate(
            flops=5 * S * S * n, bytes_accessed=10 * n * S, transcendentals=S * S * nh // 2
        ),
        name="attn_bwd",
    )(qT, doT, oT, lse, st, en, k, kT, v)


MESH = pl.DeviceIdType.MESH
CH = 16


class Place:
    def __init__(self, nc, nf):
        self.nc, self.nf, self.nz = nc, nf, nc // 2
        self.c = lax.axis_index("ctx")
        self.f = lax.axis_index("fsdp")
        self.z = self.c // 2
        self.j = self.c % 2
        self.sib = self.z * 2 + (1 - self.j)
        self.low = self.z > 0
        self.high = self.z < self.nz - 1


def remote(src, dst, ss, rs, axis, idx):
    return pltpu.make_async_remote_copy(
        src_ref=src, dst_ref=dst, send_sem=ss, recv_sem=rs, device_id={axis: idx}, device_id_type=MESH
    )


def greet(p, line=True, ctx=False, fsdp=False):
    sem = pltpu.get_barrier_semaphore()
    count = 0

    def tell(axis, idx):
        pl.semaphore_signal(sem, inc=1, device_id={axis: idx}, device_id_type=MESH)

    if ctx:
        for k in range(1, p.nc):
            tell("ctx", lax.rem(p.c + k, p.nc))
        count = p.nc - 1
    elif line:
        tell("ctx", p.sib)

        @pl.when(p.low)
        def _():
            tell("ctx", p.c - 2)

        @pl.when(p.high)
        def _():
            tell("ctx", p.c + 2)

        count = 1 + p.low.astype(jnp.int32) + p.high.astype(jnp.int32)
    if fsdp:
        for k in range(1, p.nf):
            tell("fsdp", lax.rem(p.f + k, p.nf))
        count = count + p.nf - 1
    pl.semaphore_wait(sem, count)


def each(fn, start, size, step=CH):
    def body(r, _):
        fn(pl.ds(pl.multiple_of(start + r * step, step), step))
        return 0

    lax.fori_loop(0, size // step, body, 0)


class Gather:
    def __init__(self, p, own, full, rows, ss, rs, ls):
        self.p, self.own, self.full, self.rows, self.ss, self.rs, self.ls = p, own, full, rows, ss, rs, ls

    def slot(self, k):
        return self.full.at[k, self.rows]

    def copy(self, way, k, to, src=None):
        return remote(self.slot(k) if src is None else src, self.slot(k), self.ss.at[way, k], self.rs.at[k], "ctx", to)

    def first(self):
        p = self.p
        src = self.own.at[self.rows]

        @pl.when(p.high)
        def _():
            self.copy(0, p.c, p.c + 2, src).start()

        @pl.when(p.low)
        def _():
            self.copy(1, p.c, p.c - 2, src).start()

        self.copy(2, p.c, p.sib, src).start()
        pltpu.make_async_copy(src, self.slot(p.c), self.ls).start()

    def step(self, t):
        p = self.p

        @pl.when(p.z - t >= 0)
        def _():
            k = p.c - 2 * t
            self.copy(2, k, p.sib).wait_recv()

            @pl.when(p.high)
            def _():
                self.copy(0, k, p.c + 2).start()

            self.copy(2, k, p.sib).start()

        @pl.when(p.z + t < p.nz)
        def _():
            k = p.c + 2 * t
            self.copy(2, k, p.sib).wait_recv()

            @pl.when(p.low)
            def _():
                self.copy(1, k, p.c - 2).start()

            self.copy(2, k, p.sib).start()

    def finish(self):
        p = self.p
        src = self.own.at[self.rows]
        for y in range(p.nz):
            self.copy(2, 2 * y + 1 - p.j, p.sib).wait_recv()
        for y in range(p.nz):
            k = 2 * y + p.j
            self.copy(2, k, p.sib).wait_send()

            @pl.when(p.high & (y <= p.z))
            def _(k=k):
                self.copy(0, k, p.c + 2).wait_send()

            @pl.when(p.low & (y >= p.z))
            def _(k=k):
                self.copy(1, k, p.c - 2).wait_send()

        pltpu.make_async_copy(src, self.slot(p.c), self.ls).wait()

    def all_steps(self):
        return [self.first] + [functools.partial(self.step, t) for t in range(1, self.p.nz)]


class Scatter:
    def __init__(self, p, part, a, x, ud, start, size, sems):
        self.p, self.part, self.a, self.x, self.ud = p, part, a, x, ud
        self.start, self.size, self.rows, self.sems = start, size, pl.ds(start, size), sems

    def cross(self, y):
        p = self.p
        return remote(
            self.part.at[2 * y + 1 - p.j, self.rows], self.x.at[y, self.rows],
            self.sems.at[0, y], self.sems.at[1, y], "ctx", p.sib,
        )

    def load(self, y):
        return pltpu.make_async_copy(
            self.part.at[2 * y + self.p.j, self.rows], self.a.at[y, self.rows], self.sems.at[2, y]
        )

    def go_up(self, y):
        return remote(
            self.a.at[y, self.rows], self.ud.at[y, self.rows], self.sems.at[3, y], self.sems.at[4, y], "ctx", self.p.c + 2
        )

    def go_down(self, y, last=False):
        to = self.p.nz if last else y
        return remote(
            self.a.at[y, self.rows], self.ud.at[to, self.rows], self.sems.at[5, y], self.sems.at[6, y], "ctx", self.p.c - 2
        )

    def begin(self, cross=True, load=True):
        nz = self.p.nz
        order = []
        for i in range(nz):
            order += [y for y in (nz - 1 - i, i) if y not in order]
        for y in order:
            if cross:
                self.cross(y).start()
            if load:
                self.load(y).start()

    def ready(self, y):
        self.load(y).wait()
        self.cross(y).wait_recv()

    def add(self, y, extra):
        def fn(r):
            v = self.a[y, r].astype(f32) + self.x[y, r].astype(f32)
            if extra is not None:
                v = v + extra[y, r].astype(f32)
            self.a[y, r] = v.astype(bf16)

        each(fn, self.start, self.size)

    def edges(self):
        p = self.p

        @pl.when(p.z == 0)
        def _():
            for y in range(p.nz - 1, 0, -1):
                self.ready(y)
                self.add(y, None)
                self.go_up(y).start()

        @pl.when(p.z == p.nz - 1)
        def _():
            for y in range(p.nz - 1):
                self.ready(y)
                self.add(y, None)
                self.go_down(y, y == p.nz - 2).start()

    def step(self, t):
        p = self.p

        def upward():
            y = p.nz - 1 - t + p.z
            self.ready(y)
            self.go_up(y).wait_recv()
            self.add(y, self.ud)
            self.go_up(y).start()

        def downward():
            y = t - (p.nz - 1 - p.z)
            self.ready(y)
            self.go_down(y).wait_recv()
            self.add(y, self.ud)
            self.go_down(y, t == p.nz - 2).start()

        half = p.nz // 2
        goes_up = p.low & p.high & (p.z <= t)
        goes_down = p.low & p.high & (p.nz - 1 - p.z <= t)
        pl.when(goes_up & (p.z < half))(upward)
        pl.when(goes_down)(downward)
        pl.when(goes_up & (p.z >= half))(upward)

    def total(self, fn):
        p = self.p
        z = p.z
        self.ready(z)
        pl.when(p.low)(lambda: self.go_up(z).wait_recv())
        pl.when(p.high)(lambda: self.go_down(z, True).wait_recv())

        def run(low, high):
            def body(r):
                v = self.a[z, r].astype(f32) + self.x[z, r].astype(f32)
                if low:
                    v = v + self.ud[z, r].astype(f32)
                if high:
                    v = v + self.ud[p.nz, r].astype(f32)
                fn(r, v)

            each(body, self.start, self.size)

        pl.when(p.low & p.high)(lambda: run(True, True))
        pl.when(p.z == 0)(lambda: run(False, p.nz > 1))
        pl.when(p.z == p.nz - 1)(lambda: run(True, False))

    def finish(self):
        p = self.p
        for y in range(p.nz):
            self.cross(y).wait_send()

            @pl.when(p.z < y)
            def _(y=y):
                self.go_up(y).wait_send()

            @pl.when(p.z > y)
            def _(y=y):
                self.go_down(y).wait_send()

    def all_steps(self):
        return [functools.partial(self.step, i) for i in range(1, self.p.nz - 1)]


def interleave(first, second):
    for i in range(max(len(first), len(second))):
        if i < len(first):
            first[i]()
        if i < len(second):
            second[i]()


class Peers:
    def __init__(self, p, pick, ss, rs, keep, ls):
        self.p, self.pick, self.ss, self.rs, self.keep, self.ls = p, pick, ss, rs, keep, ls

    def copy(self, k):
        p = self.p
        to = lax.rem(p.f + k, p.nf)
        src, dst = self.pick(to)
        return remote(src, dst, self.ss.at[k], self.rs.at[k], "fsdp", to)

    def start(self):
        for k in range(1, self.p.nf):
            self.copy(k).start()
        if self.keep is not None:
            pltpu.make_async_copy(*self.keep, self.ls).start()

    def wait(self):
        for k in range(1, self.p.nf):
            self.copy(k).wait()
        if self.keep is not None:
            pltpu.make_async_copy(*self.keep, self.ls).wait()


DMA = pltpu.SemaphoreType.DMA


def gather_sems(nc):
    return [DMA((3, nc)), DMA((nc,)), DMA]


def scatter_scratch(nz, T, E):
    return [pltpu.VMEM((nz, T, E), bf16)] * 2 + [pltpu.VMEM((nz + 1, T, E), bf16)]


def params(cid):
    return pltpu.CompilerParams(collective_id=cid, has_side_effects=True, vmem_limit_bytes=60 * 1024 * 1024)


ANY = pl.BlockSpec(memory_space=pl.ANY)
VM = pl.BlockSpec(memory_space=pltpu.VMEM)


def open_kernel(nc, nf, tok, ids, wl, row, ids_row, w, gss, grs, gls, iss, irs, ils, ass, ars, fss, frs, als):
    p = Place(nc, nf)
    greet(p, ctx=True, fsdp=True)
    T = tok.shape[0]
    g = Gather(p, tok, row, pl.ds(0, T), gss, grs, gls)

    def id_copy(k):
        to = lax.rem(p.c + k, nc)
        return remote(ids, ids_row.at[p.c], iss.at[k], irs.at[k], "ctx", to)

    def block(k):
        to = lax.rem(p.c + k, nc)
        return remote(wl.at[to], w.at[p.c, p.f], ass.at[k], ars.at[k], "ctx", to)

    def onward(c, k, m):
        to = lax.rem(p.f + m, nf)
        return remote(w.at[c, p.f], w.at[c, p.f], fss.at[k, m], frs.at[k, m], "fsdp", to)

    def source(k):
        return lax.rem(p.c + nc - k, nc)

    keep_ids = pltpu.make_async_copy(ids, ids_row.at[p.c], ils)
    keep_w = pltpu.make_async_copy(wl.at[p.c], w.at[p.c, p.f], als)
    keep_w.start()
    keep_ids.start()
    for k in range(1, nc):
        block(k).start()
        id_copy(k).start()
    g.first()
    keep_w.wait()

    def spread(k):
        for m in range(1, nf):
            onward(source(k), k, m).start()

    spread(0)
    for k in range(1, nc):
        block(k).wait_recv()
        spread(k)
    for t in range(1, p.nz):
        g.step(t)
    g.finish()
    keep_ids.wait()
    for k in range(1, nc):
        block(k).wait_send()
        id_copy(k).wait()
    for k in range(nc):
        for m in range(1, nf):
            onward(source(k), k, m).wait()


def open_call(nc, nf, tok, ids, wl):
    T, E = tok.shape
    _, R, A = wl.shape
    return pl.pallas_call(
        functools.partial(open_kernel, nc, nf),
        in_specs=[ANY, ANY, ANY],
        out_specs=[ANY, ANY, ANY],
        out_shape=[
            jax.ShapeDtypeStruct((nc, T, E), bf16),
            jax.ShapeDtypeStruct((nc,) + ids.shape, jnp.int32),
            jax.ShapeDtypeStruct((nc, nf, R, A), bf16),
        ],
        scratch_shapes=gather_sems(nc)
        + [DMA((nc,)), DMA((nc,)), DMA, DMA((nc,)), DMA((nc,)), DMA((nc, nf)), DMA((nc, nf)), DMA],
        compiler_params=params(1),
        name="open_row",
    )(tok, ids, wl)


def middle_kernel(
    nc, nf, parts, part, tok, og, g, wl, hid, n2, dm, w,
    a, x, ud, own, dmo, rsem, nss, nrs, nls, dss, drs, dls, fss, frs, fls,
):
    p = Place(nc, nf)
    greet(p, fsdp=True)
    T = tok.shape[0]
    size = T // parts
    rs = [Scatter(p, part, a, x, ud, q * size, size, rsem.at[q]) for q in range(parts)]
    ag = [
        Gather(p, own, n2, pl.ds(q * size, size), nss.at[q], nrs.at[q], nls.at[q]) for q in range(parts)
    ]
    dmg = Gather(p, dmo, dm, pl.ds(0, T), dss, drs, dls)
    peers = Peers(p, lambda to: (wl, w.at[:, p.f]), fss, frs, (wl, w.at[:, p.f]), fls)
    for q in range(parts):
        rs[q].begin()

    def dm_rows(r):
        dmo[r] = (RES * og[r].astype(f32)).astype(bf16)

    each(dm_rows, 0, T)
    dmg.first()
    rs[0].edges()
    peers.start()

    def rows(r, v):
        h = tok[r].astype(f32) + RES * v
        hid[r] = h
        own[r] = (h * lax.rsqrt(jnp.mean(h * h, axis=-1, keepdims=True) + EPS) * g[...]).astype(bf16)

    pending = dmg.all_steps()[1:]
    for q in range(parts):
        interleave(pending, rs[q].all_steps())
        if q + 1 < parts:
            rs[q + 1].edges()
        rs[q].total(rows)
        ag[q].first()
        pending = ag[q].all_steps()[1:]
    for s in pending:
        s()
    for q in range(parts):
        ag[q].finish()
        rs[q].finish()
    dmg.finish()
    peers.wait()


def middle_call(nc, nf, parts, part, tok, og, g, wl):
    T, E = tok.shape
    _, R, M = wl.shape
    nz = nc // 2
    return pl.pallas_call(
        functools.partial(middle_kernel, nc, nf, parts),
        in_specs=[ANY, VM, VM, VM, ANY],
        out_specs=[VM, ANY, ANY, ANY],
        out_shape=[
            jax.ShapeDtypeStruct((T, E), f32),
            jax.ShapeDtypeStruct((nc, T, E), bf16),
            jax.ShapeDtypeStruct((nc, T, E), bf16),
            jax.ShapeDtypeStruct((nc, nf, R, M), bf16),
        ],
        scratch_shapes=scatter_scratch(nz, T, E)
        + [pltpu.VMEM((T, E), bf16), pltpu.VMEM((T, E), bf16), DMA((parts, 7, nz))]
        + [DMA((parts, 3, nc)), DMA((parts, nc)), DMA((parts,))]
        + gather_sems(nc)
        + [DMA((nf,)), DMA((nf,)), DMA],
        compiler_params=params(2),
        name="attn_to_mlp",
    )(part, tok, og, g, wl)


def turn_kernel(nc, nf, fold, *refs):
    it = iter(refs)
    take = lambda n: [next(it) for _ in range(n)]
    part, n2, dm, dgu, act = take(5)
    wd = next(it) if fold else None
    hid, og, g, dh, da = take(5)
    lay = next(it) if fold else None
    gg, y, gbuf = take(3)
    mpart = next(it) if fold else None
    a, x, ud, own, rsem = take(5)
    nss, nrs, nls, fss, frs, fls = take(6)
    dguv, actv, nb, db, nt, go, lsem, ssem = take(8)
    p = Place(nc, nf)
    greet(p, fsdp=True)
    T, E = hid.shape
    S, F2 = dgu.shape
    F = act.shape[1]
    R = E // (nc * nf)
    B = nf * R
    rs = Scatter(p, part, a, x, ud, 0, T, rsem)
    ag = Gather(p, own, da, pl.ds(0, T), nss, nrs, nls)
    rs.begin()
    big = [pltpu.make_async_copy(dgu, dguv, lsem.at[4]), pltpu.make_async_copy(act, actv, lsem.at[5])]
    if fold:
        x2, ud2, wdv, mp, msem, wsem, psem = take(7)
        ms = Scatter(p, mpart, a, x2, ud2, 0, T, msem)
        big.append(pltpu.make_async_copy(wd, wdv, wsem))
    for cp in big:
        cp.start()

    def column(b, slot):
        at = pl.ds(pl.multiple_of(b * B, B), B)
        return (
            pltpu.make_async_copy(n2.at[:, at], nb.at[slot], lsem.at[slot]),
            pltpu.make_async_copy(dm.at[:, at], db.at[slot], lsem.at[2 + slot]),
        )

    def keep(b, slot):
        return pltpu.make_async_copy(go.at[slot], gbuf.at[b], ssem.at[slot])

    def peer(b, k):
        to = lax.rem(p.f + k, nf)
        at = pl.ds(pl.multiple_of(to * R, R), R)
        return remote(gbuf.at[b, at], y.at[p.f, b], fss.at[k, b], frs.at[k, b], "fsdp", to)

    def mine(b):
        at = pl.ds(pl.multiple_of(p.f * R, R), R)
        return pltpu.make_async_copy(gbuf.at[b, at], y.at[p.f, b], fls.at[b])

    def send(b):
        keep(b, b % 2).wait()
        for k in range(1, nf):
            peer(b, k).start()
        mine(b).start()

    def grads(b, _):
        slot = b % 2

        @pl.when(b + 1 < nc)
        def _():
            for cp in column(b + 1, 1 - slot):
                cp.start()

        now = column(b, slot)
        for src, val, base, width, cp in ((nb, dguv, 0, F2, now[0]), (db, actv, F2, F, now[1])):
            cp.wait()
            nt[...] = src[slot].T
            step = min(512, width)

            def dots(i, _, val=val, base=base, step=step):
                at = pl.multiple_of(i * step, step)
                v = jnp.dot(nt[...], val[:, pl.ds(at, step)], preferred_element_type=f32)
                go[slot, :, pl.ds(pl.multiple_of(base + at, step), step)] = v.astype(bf16)
                return 0

            lax.fori_loop(0, width // step, dots, 0)
        keep(b, slot).start()

        @pl.when(b > 0)
        def _():
            send(b - 1)

        return 0

    def mlp(b, _):
        slot = b % 2
        out = pltpu.make_async_copy(mp.at[slot], mpart.at[b], psem.at[slot])

        @pl.when(b > 1)
        def _():
            out.wait()

        tok = actv[pl.ds(pl.multiple_of(b * T, T), T), :]

        def dots(i, _):
            at = pl.ds(pl.multiple_of(i * 512, 512), 512)
            mp[slot, :, at] = dg(tok, wdv[at, :], 1, 1).astype(bf16)
            return 0

        lax.fori_loop(0, E // 512, dots, 0)
        out.start()
        return 0

    for cp in column(0, 0):
        cp.start()
    gg[...] = jnp.zeros_like(gg)
    rs.edges()
    for cp in big:
        cp.wait()
    if fold:
        lax.fori_loop(0, nc, mlp, 0)
        for slot in range(2):
            pltpu.make_async_copy(mp.at[slot], mpart.at[slot], psem.at[slot]).wait()
        ms.begin(load=False)
    steps = rs.all_steps()
    bounds = [nc * i // (len(steps) + 1) for i in range(len(steps) + 2)]
    for i in range(len(steps) + 1):
        lax.fori_loop(bounds[i], bounds[i + 1], grads, 0)
        if i < len(steps):
            steps[i]()
    send(nc - 1)

    def rows(r, dn):
        h = hid[r]
        inv = lax.rsqrt(jnp.mean(h * h, axis=-1, keepdims=True) + EPS)
        xn = h * inv
        e = dn * g[...]
        v = og[r].astype(f32) + inv * (e - xn * jnp.mean(e * xn, axis=-1, keepdims=True))
        dh[r] = v
        own[r] = (RES * v).astype(bf16)
        gg[...] += jnp.sum((xn * dn).reshape(CH // 8, 8, E), axis=0)

    rs.total(rows)
    ag.first()
    rs.finish()
    if fold:
        ms.begin(cross=False)
        ms.edges()
    interleave(ag.all_steps()[1:], ms.all_steps() if fold else [])
    if fold:

        def out(r, v):
            lay[r] = (hid[r] + RES * v).astype(bf16)

        ms.total(out)
        ms.finish()
    ag.finish()
    for b in range(nc):
        for k in range(1, nf):
            peer(b, k).wait()
        mine(b).wait()


def turn_call(nc, nf, fold, part, n2, dm, dgu, act, wd, hid, og, g):
    T, E = hid.shape
    S, F2 = dgu.shape
    F = act.shape[1]
    M = F2 + F
    R = E // (nc * nf)
    B = nf * R
    nz = nc // 2
    VMEM = pltpu.VMEM
    return pl.pallas_call(
        functools.partial(turn_kernel, nc, nf, fold),
        in_specs=[ANY] * (5 + fold) + [VM, VM, VM],
        out_specs=[VM, ANY] + [VM] * fold + [VM, ANY, ANY] + [ANY] * fold,
        out_shape=[jax.ShapeDtypeStruct((T, E), f32), jax.ShapeDtypeStruct((nc, T, E), bf16)]
        + [jax.ShapeDtypeStruct((T, E), bf16)] * fold
        + [
            jax.ShapeDtypeStruct((8, E), f32),
            jax.ShapeDtypeStruct((nf, nc, R, M), bf16),
            jax.ShapeDtypeStruct((nc, B, M), bf16),
        ]
        + [jax.ShapeDtypeStruct((nc, T, E), bf16)] * fold,
        scratch_shapes=scatter_scratch(nz, T, E)
        + [VMEM((T, E), bf16), DMA((7, nz))]
        + gather_sems(nc)
        + [DMA((nf, nc)), DMA((nf, nc)), DMA((nc,))]
        + [VMEM((S, F2), bf16), VMEM((S, F), bf16), VMEM((2, S, B), bf16), VMEM((2, S, B), bf16)]
        + [VMEM((B, S), bf16), VMEM((2, B, M), bf16), DMA((6,)), DMA((2,))]
        + [
            VMEM((nz, T, E), bf16), VMEM((nz + 1, T, E), bf16), VMEM((E, F), bf16), VMEM((2, T, E), bf16),
            DMA((7, nz)), DMA, DMA((2,)),
        ]
        * fold,
        compiler_params=params(3),
        name="mlp_to_attn",
    )(part, n2, dm, dgu, act, *([wd] if fold else []), hid, og, g)


def close_kernel(
    nc, nf, parts, part, tok, dh, g, gw, ggm, dx, gout, ggout,
    a, x, ud, y, zb, gg, gbuf, gsum, gfin, rsem, fss, frs, fls, css, crs, cls, s1, r1, s2, r2, l2,
):
    p = Place(nc, nf)
    greet(p, ctx=True, fsdp=True)
    T, E = tok.shape
    R = gw.shape[2]
    size = T // parts
    rs = [Scatter(p, part, a, x, ud, q * size, size, rsem.at[q]) for q in range(parts)]
    peers = Peers(p, lambda to: (gw.at[:, to], y.at[p.f]), fss, frs, (gw.at[:, p.f], y.at[p.f]), fls)
    for q in range(parts):
        rs[q].begin()
    peers.start()
    gg[...] = jnp.zeros_like(gg)

    def piece(k):
        to = lax.rem(p.c + k, nc)
        return remote(zb.at[to], gout.at[p.c], css.at[k], crs.at[k], "ctx", to)

    mine = pltpu.make_async_copy(zb.at[p.c], gout.at[p.c], cls)

    def grads():
        peers.wait()
        for c in range(nc):

            def fn(r):
                v = y[0, c, r].astype(f32)
                for m in range(1, nf):
                    v = v + y[m, c, r].astype(f32)
                zb[c, r] = v.astype(bf16)

            each(fn, 0, R)
        for k in range(1, nc):
            piece(k).start()
        mine.start()

    def rows(r, dn):
        t = tok[r].astype(f32)
        inv = lax.rsqrt(jnp.mean(t * t, axis=-1, keepdims=True) + EPS)
        xn = t * inv
        e = dn * g[...]
        dx[r] = dh[r] + inv * (e - xn * jnp.mean(e * xn, axis=-1, keepdims=True))
        gg[...] += jnp.sum((xn * dn).reshape(CH // 8, 8, E), axis=0)

    for q in range(parts):
        rs[q].edges()
    for q in range(parts):
        for s in rs[q].all_steps():
            s()
        if q == 0:
            grads()
        rs[q].total(rows)

    groups = E // 128
    sa = jnp.sum(gg[...], axis=0, keepdims=True)
    sm = jnp.sum(ggm[...], axis=0, keepdims=True)
    for i in range(groups):
        gbuf[p.f, i] = jnp.concatenate(
            [sa[:, i * 128 : (i + 1) * 128], sm[:, i * 128 : (i + 1) * 128], jnp.zeros((6, 128), f32)], axis=0
        )

    def over(k):
        to = lax.rem(p.f + k, nf)
        return remote(gbuf.at[p.f], gbuf.at[p.f], s1.at[k], r1.at[k], "fsdp", to)

    for k in range(1, nf):
        over(k).start()
    for k in range(1, nf):
        over(k).wait()
    v = gbuf[0]
    for m in range(1, nf):
        v = v + gbuf[m]
    gsum[...] = v
    per = 128 // R

    def along(k):
        to = lax.rem(p.c + k, nc)
        return remote(gsum.at[(to * nf + p.f) // per], gfin.at[p.c], s2.at[k], r2.at[k], "ctx", to)

    for k in range(1, nc):
        along(k).start()
    own = pltpu.make_async_copy(gsum.at[(p.c * nf + p.f) // per], gfin.at[p.c], l2)
    own.start()
    own.wait()
    for k in range(1, nc):
        along(k).wait()
    t = gfin[0]
    for m in range(1, nc):
        t = t + gfin[m]
    ggout[...] = t
    for k in range(1, nc):
        piece(k).wait()
    mine.wait()
    for q in range(parts):
        rs[q].finish()


def close_call(nc, nf, parts, part, tok, dh, g, gw, ggm):
    T, E = tok.shape
    _, _, R, A = gw.shape
    nz = nc // 2
    return pl.pallas_call(
        functools.partial(close_kernel, nc, nf, parts),
        in_specs=[ANY, VM, VM, VM, ANY, VM],
        out_specs=[VM, ANY, VM],
        out_shape=[
            jax.ShapeDtypeStruct((T, E), f32),
            jax.ShapeDtypeStruct((nc, R, A), bf16),
            jax.ShapeDtypeStruct((8, 128), f32),
        ],
        scratch_shapes=scatter_scratch(nz, T, E)
        + [
            pltpu.VMEM((nf, nc, R, A), bf16),
            pltpu.VMEM((nc, R, A), bf16),
            pltpu.VMEM((8, E), f32),
            pltpu.VMEM((nf, E // 128, 8, 128), f32),
            pltpu.VMEM((E // 128, 8, 128), f32),
            pltpu.VMEM((nc, 8, 128), f32),
            DMA((parts, 7, nz)),
        ]
        + [DMA((nf,)), DMA((nf,)), DMA, DMA((nc,)), DMA((nc,)), DMA]
        + [DMA((nf,)), DMA((nf,)), DMA((nc,)), DMA((nc,)), DMA],
        compiler_params=params(4),
        name="close_row",
    )(part, tok, dh, g, gw, ggm)


def rms(v):
    inv = lax.rsqrt(jnp.mean(v * v, axis=-1, keepdims=True) + EPS)
    return v * inv, inv


def rms_back(x, inv, e):
    return inv * (e - x * jnp.mean(e * x, axis=-1, keepdims=True))


def rotate(v, cos, sin, sign):
    heads = v.shape[0] // HD
    v = v.reshape(heads, 2, HD // 2, v.shape[1])
    a, b = v[:, 0], v[:, 1]
    s = sign * sin
    return jnp.stack([a * cos - b * s, b * cos + a * s], axis=1).reshape(heads * HD, -1)


PB, PD = 1, 2


def local(
    tokens, seq_ids, positions, block_ids, gain_attn, w_query, w_key, w_value, w_out,
    gain_mlp, w_gate, w_up, w_down, out_grad,
):
    nc = lax.axis_size("ctx")
    nf = lax.axis_size("fsdp")
    nz = nc // 2
    T, E = tokens.shape[1:]
    R = w_query.shape[0]
    S = T * nc
    FFL = w_gate.shape[1] // nc
    nh = QUERY_HEADS // nc
    rep = nc // KEY_VALUE_HEADS
    QW = nh * HD
    KO, VO, OO, GO = QW, QW + HD, QW + 2 * HD, 2 * QW + 2 * HD
    tok, og = tokens[0], out_grad[0]

    def cols(w):
        return w.astype(bf16).reshape(R, nc, -1)

    def kv_cols(w):
        return jnp.repeat(w.astype(bf16).reshape(R, KEY_VALUE_HEADS, HD), rep, axis=1)

    def blocks(parts):
        return jnp.transpose(jnp.concatenate(parts, axis=2), (1, 0, 2))

    def exchange(w):
        return lax.all_to_all(w, "ctx", 0, 0, tiled=True)

    gains = jnp.stack([gain_attn, gain_mlp], axis=1).astype(bf16)
    gains = jnp.broadcast_to(jnp.pad(gains, ((0, 0), (0, 126)))[:, None], (R, nc, 128))
    wl = blocks([cols(w_query), kv_cols(w_key), kv_cols(w_value), cols(w_out), gains])
    ids = jnp.pad(jnp.concatenate([seq_ids, positions, block_ids], axis=0), ((0, 5), (0, 0)))
    row_tok, ids, wa = open_call(nc, nf, tok, ids, wl)
    wa = wa.reshape(E, -1)
    g_attn, g_mlp = wa[:, GO].astype(f32)[None], wa[:, GO + 1].astype(f32)[None]

    wm = blocks([cols(w_gate), cols(w_up), cols(w_down)])
    row_tok, wm = lax.optimization_barrier((row_tok, wm))
    wm = exchange(wm)

    seq, pos, blk = (ids[:, i].reshape(S) for i in range(3))
    place = jnp.arange(S, dtype=jnp.int32)
    cut = jnp.sum((seq == 0).astype(jnp.int32))
    first = place - pos
    last = jnp.minimum(first + BLOCK * (blk + 1), jnp.where(seq == 0, cut, S))
    st, en = first[None], last[None]
    freq = ROPE_BASE ** (-(jnp.arange(HD // 2, dtype=f32) * 2.0) / HD)
    ang = freq[:, None] * pos.astype(f32)[None, :]
    cos, sin = jnp.cos(ang), jnp.sin(ang)

    x1r, _ = rms(row_tok.reshape(S, E).astype(f32))
    n1 = (x1r * g_attn).astype(bf16)
    w_qkv, w_o = wa[:, :OO], wa[:, OO:GO]
    qkv = dg(w_qkv, n1, 0, 1)
    qkT = rotate(qkv[:VO], cos, sin, 1.0).astype(bf16)
    qT, kT = qkT[:QW], qkT[QW:]
    vT = qkv[VO:].astype(bf16)
    k, v = kT.T, vT.T
    oT, oTb, lse = attn_fwd(qT, k, vT, st, en)
    attn = dg(oTb, w_o, 0, 1).astype(bf16).reshape(nc, T, E)

    hidden, n2, dm, wm = middle_call(nc, nf, PB, attn, tok, og, g_mlp, wm)
    n2, dm, wm = n2.reshape(S, E), dm.reshape(S, E), wm.reshape(E, -1)
    w_gu, w_d = wm[:, : 2 * FFL], wm[:, 2 * FFL :]
    gu = dg(n2, w_gu, 1, 0)
    gate, up = gu[:, :FFL], gu[:, FFL:]
    sg = jax.nn.sigmoid(gate)
    act = (gate * sg * up).astype(bf16)
    d_act = dg(dm, w_d, 1, 0)
    d_gate = (d_act * up * sg * (1.0 + gate * (1.0 - sg))).astype(bf16)
    d_up = (d_act * gate * sg).astype(bf16)
    d_gu = jnp.concatenate([d_gate, d_up], axis=1)
    dn2 = dg(d_gu, w_gu, 1, 1).astype(bf16).reshape(nc, T, E)
    if nz <= 4:
        dh, da, layer_out, ggm, gm = turn_call(nc, nf, True, dn2, n2, dm, d_gu, act, w_d, hidden, og, g_mlp)[:5]
    else:
        dh, da, ggm, gm = turn_call(nc, nf, False, dn2, n2, dm, d_gu, act, None, hidden, og, g_mlp)[:4]
        mlp = dg(act, w_d, 1, 1).astype(bf16)
        mlp = lax.psum_scatter(mlp, "ctx", scatter_dimension=0, tiled=True)
        layer_out = (hidden + RES * mlp.astype(f32)).astype(bf16)
    da = da.reshape(S, E)
    gm = exchange(jnp.sum(gm.astype(f32), axis=0).astype(bf16))

    doT = dg(w_o, da, 0, 1).astype(bf16)
    dqT, dkT, dvT = attn_bwd(qT, doT, oT, lse, st, en, k, kT, v)
    dqk = rotate(jnp.concatenate([dqT, dkT], axis=0) * SCALE, cos, sin, -1.0).astype(bf16)
    dqkv = jnp.concatenate([dqk, dvT.astype(bf16)], axis=0)
    dn1 = dg(dqkv, w_qkv, 0, 1).astype(bf16).reshape(nc, T, E)
    ga = jnp.concatenate([dg(dqkv, n1, 1, 0), dg(oTb, da, 1, 0)], axis=0).astype(bf16).T
    input_grad, ga, gains = close_call(nc, nf, PD, dn1, tok, dh, g_attn, ga.reshape(nc, nf, R, -1), ggm)
    at = lax.rem((lax.axis_index("ctx") * nf + lax.axis_index("fsdp")) * R, 128)
    gains = lax.dynamic_slice_in_dim(gains, at, R, 1)

    def rows(g):
        return jnp.transpose(g.astype(f32), (1, 0, 2)).reshape(R, -1)

    def kv_rows(g):
        g = g.astype(f32).reshape(KEY_VALUE_HEADS, rep, R, HD)
        return jnp.transpose(jnp.sum(g, axis=1), (1, 0, 2)).reshape(R, -1)

    return (
        layer_out[None],
        input_grad[None],
        gains[0],
        rows(ga[:, :, :KO]),
        kv_rows(ga[:, :, KO:VO]),
        kv_rows(ga[:, :, VO:OO]),
        rows(ga[:, :, OO:]),
        gains[1],
        rows(gm[:, :, :FFL]),
        rows(gm[:, :, FFL : 2 * FFL]),
        rows(gm[:, :, 2 * FFL :]),
    )


def solution(mesh):
    w1, w2 = P(("ctx", "fsdp")), P(("ctx", "fsdp"), None)
    act, ids = P("fsdp", "ctx", None), P("fsdp", "ctx")
    return jax.shard_map(
        local,
        mesh=mesh,
        in_specs=(act, ids, ids, ids, w1, w2, w2, w2, w2, w1, w2, w2, w2, act),
        out_specs=(act, act, w1, w2, w2, w2, w2, w1, w2, w2, w2),
        check_vma=False,
    )
```

```python
import functools

import jax
import jax.numpy as jnp
from jax import lax
from jax.experimental import pallas as pl
from jax.experimental.pallas import tpu as pltpu
from jax.sharding import PartitionSpec as P

QUERY_HEADS = 32
KEY_VALUE_HEADS = 8
HD = 64
BLOCK = 256
EPS = 1e-05
ROPE_BASE = 10000000.0
SCALE = 0.015625
RES = 0.22
NEG = -1e30
bf16 = jnp.bfloat16
f32 = jnp.float32


def dg(a, b, ca, cb):
    return lax.dot_general(a, b, (((ca,), (cb,)), ((), ())), preferred_element_type=f32)


def lanes(v, heads):
    return jnp.concatenate([v[h * HD : (h + 1) * HD, :] for h in range(heads)], axis=1)


def turned_back(v, cos, sin):
    half = HD // 2
    out = []
    for h in range(v.shape[0] // HD):
        a, b = v[h * HD : h * HD + half, :], v[h * HD + half : (h + 1) * HD, :]
        out += [a * cos + b * sin, b * cos - a * sin]
    return jnp.concatenate(out, axis=0)


def key_blocks(st, en, tk):
    return jnp.min(st) // tk, (jnp.max(en) + tk - 1) // tk


def attn_fwd_kernel(nh, tq, tk, q_ref, k_ref, v_ref, st_ref, en_ref, o_ref, ob_ref, l_ref, a_ref):
    lo, hi = key_blocks(st_ref[...], en_ref[...], tk)
    q = lanes(q_ref[...] * jnp.asarray(SCALE, bf16), nh)
    st = jnp.concatenate([st_ref[...]] * nh, axis=1)
    en = jnp.concatenate([en_ref[...]] * nh, axis=1)
    W = nh * tq
    a_ref[...] = jnp.zeros_like(a_ref)

    def body(j, c):
        m, l = c
        off = pl.multiple_of(j * tk, tk)
        jj = off + lax.broadcasted_iota(jnp.int32, (tk, W), 0)
        s = dg(k_ref[pl.ds(off, tk), :], q, 1, 0)
        s = jnp.where((jj >= st) & (jj < en), s, NEG)
        mn = jnp.maximum(m, jnp.max(s, axis=0, keepdims=True))
        p = jnp.exp(s - mn)
        sh = jnp.exp(m - mn)
        l = l * sh + jnp.sum(p, axis=0, keepdims=True)
        a_ref[...] = a_ref[...] * sh + dg(v_ref[:, pl.ds(off, tk)], p.astype(bf16), 1, 0)
        return mn, l

    m, l = lax.fori_loop(lo, hi, body, (jnp.full((1, W), 0.1 * NEG, f32), jnp.zeros((1, W), f32)))
    o = a_ref[...] / l
    ls = m + jnp.log(l)
    for h in range(nh):
        oh = o[:, h * tq : (h + 1) * tq]
        o_ref[h * HD : (h + 1) * HD, :] = oh
        ob_ref[h * HD : (h + 1) * HD, :] = oh.astype(bf16)
        l_ref[h : h + 1, :] = ls[:, h * tq : (h + 1) * tq]


def attn_fwd(qT, k, vT, st, en, tq=256, tk=256):
    n, S = qT.shape
    nh = n // HD
    blk = lambda r: pl.BlockSpec((r, tq), lambda i: (0, i))
    full = lambda s: pl.BlockSpec(s, lambda i: (0, 0))
    return pl.pallas_call(
        functools.partial(attn_fwd_kernel, nh, tq, tk),
        grid=(S // tq,),
        in_specs=[blk(n), full((S, HD)), full((HD, S)), blk(1), blk(1)],
        out_specs=[blk(n), blk(n), blk(nh)],
        out_shape=[
            jax.ShapeDtypeStruct((n, S), f32),
            jax.ShapeDtypeStruct((n, S), bf16),
            jax.ShapeDtypeStruct((nh, S), f32),
        ],
        scratch_shapes=[pltpu.VMEM((HD, nh * tq), f32)],
        cost_estimate=pl.CostEstimate(
            flops=2 * S * S * n, bytes_accessed=8 * n * S, transcendentals=S * S * nh // 2
        ),
        name="attn_fwd",
    )(qT, k, vT, st, en)


def attn_bwd_kernel(
    nh, tq, tk, q_ref, da_ref, wo_ref, o_ref, lse_ref, st_ref, en_ref, cos_ref, sin_ref, k_ref, kT_ref, v_ref,
    out_ref, dk_ref, dv_ref, acc,
):
    i = pl.program_id(0)
    n = nh * HD

    @pl.when(i == 0)
    def _():
        dk_ref[...] = jnp.zeros_like(dk_ref)
        dv_ref[...] = jnp.zeros_like(dv_ref)

    here = pl.ds(pl.multiple_of(i * tq, tq), tq)
    lo, hi = key_blocks(st_ref[...], en_ref[...], tk)
    q = lanes(q_ref[...] * jnp.asarray(SCALE, bf16), nh)
    do = lanes(dg(wo_ref[...], da_ref[...], 1, 1).astype(bf16), nh)
    o = lanes(o_ref[...], nh)
    dl = jnp.sum(do.astype(f32) * o, axis=0, keepdims=True)
    ls = jnp.concatenate([lse_ref[h : h + 1, :] for h in range(nh)], axis=1)
    st = jnp.concatenate([st_ref[...]] * nh, axis=1)
    en = jnp.concatenate([en_ref[...]] * nh, axis=1)
    acc[...] = jnp.zeros_like(acc)

    def body(j, _):
        off = pl.multiple_of(j * tk, tk)
        at = pl.ds(off, tk)
        jj = off + lax.broadcasted_iota(jnp.int32, (tk, nh * tq), 0)
        s = dg(k_ref[at, :], q, 1, 0)
        dp = dg(v_ref[at, :], do, 1, 0)
        p = jnp.exp(jnp.where((jj >= st) & (jj < en), s - ls, NEG))
        ds = (p * (dp - dl)).astype(bf16)
        acc[...] += dg(kT_ref[:, at], ds, 1, 0)
        dk_ref[:, at] += dg(q, ds, 1, 1)
        dv_ref[:, at] += dg(do, p.astype(bf16), 1, 1)
        return 0

    lax.fori_loop(lo, hi, body, 0)
    dq = jnp.concatenate([acc[:, h * tq : (h + 1) * tq] for h in range(nh)], axis=0) * SCALE
    out_ref[pl.ds(0, n), here] = turned_back(dq, cos_ref[:, here], sin_ref[:, here]).astype(bf16)

    @pl.when(i == pl.num_programs(0) - 1)
    def _():
        out_ref[pl.ds(n, HD), :] = turned_back(dk_ref[...], cos_ref[...], sin_ref[...]).astype(bf16)
        out_ref[pl.ds(n + HD, HD), :] = dv_ref[...].astype(bf16)


def attn_bwd(qT, da, woT, oT, lse, st, en, cos, sin, k, kT, v, tq=256, tk=256):
    n, S = qT.shape
    E = da.shape[1]
    nh = n // HD
    blk = lambda r: pl.BlockSpec((r, tq), lambda i: (0, i))
    full = lambda s: pl.BlockSpec(s, lambda i: (0, 0))
    return pl.pallas_call(
        functools.partial(attn_bwd_kernel, nh, tq, tk),
        grid=(S // tq,),
        in_specs=[
            blk(n), pl.BlockSpec((tq, E), lambda i: (i, 0)), full((n, E)), blk(n), blk(nh), blk(1), blk(1),
            full((HD // 2, S)), full((HD // 2, S)), full((S, HD)), full((HD, S)), full((S, HD)),
        ],
        out_specs=full((n + 2 * HD, S)),
        out_shape=jax.ShapeDtypeStruct((n + 2 * HD, S), bf16),
        scratch_shapes=[pltpu.VMEM((HD, S), f32), pltpu.VMEM((HD, S), f32), pltpu.VMEM((HD, nh * tq), f32)],
        cost_estimate=pl.CostEstimate(
            flops=5 * S * S * n, bytes_accessed=10 * n * S, transcendentals=S * S * nh // 2
        ),
        name="attn_bwd",
    )(qT, da, woT, oT, lse, st, en, cos, sin, k, kT, v)


MESH = pl.DeviceIdType.MESH
CH = 16


class Place:
    def __init__(self, nc, nf):
        self.nc, self.nf, self.nz = nc, nf, nc // 2
        self.c = lax.axis_index("ctx")
        self.f = lax.axis_index("fsdp")
        self.z = self.c // 2
        self.j = self.c % 2
        self.sib = self.z * 2 + (1 - self.j)
        self.low = self.z > 0
        self.high = self.z < self.nz - 1


def remote(src, dst, ss, rs, axis, idx):
    return pltpu.make_async_remote_copy(
        src_ref=src, dst_ref=dst, send_sem=ss, recv_sem=rs, device_id={axis: idx}, device_id_type=MESH
    )


def greet(p, line=True, ctx=False, fsdp=False):
    sem = pltpu.get_barrier_semaphore()
    count = 0

    def tell(axis, idx):
        pl.semaphore_signal(sem, inc=1, device_id={axis: idx}, device_id_type=MESH)

    if ctx:
        for k in range(1, p.nc):
            tell("ctx", lax.rem(p.c + k, p.nc))
        count = p.nc - 1
    elif line:
        tell("ctx", p.sib)

        @pl.when(p.low)
        def _():
            tell("ctx", p.c - 2)

        @pl.when(p.high)
        def _():
            tell("ctx", p.c + 2)

        count = 1 + p.low.astype(jnp.int32) + p.high.astype(jnp.int32)
    if fsdp:
        for k in range(1, p.nf):
            tell("fsdp", lax.rem(p.f + k, p.nf))
        count = count + p.nf - 1
    pl.semaphore_wait(sem, count)


def each(fn, start, size, step=CH):
    def body(r, _):
        fn(pl.ds(pl.multiple_of(start + r * step, step), step))
        return 0

    lax.fori_loop(0, size // step, body, 0)


class Gather:
    def __init__(self, p, own, full, rows, ss, rs, ls):
        self.p, self.own, self.full, self.rows, self.ss, self.rs, self.ls = p, own, full, rows, ss, rs, ls

    def slot(self, k):
        return self.full.at[k, self.rows]

    def copy(self, way, k, to, src=None):
        return remote(self.slot(k) if src is None else src, self.slot(k), self.ss.at[way, k], self.rs.at[k], "ctx", to)

    def first(self):
        p = self.p
        src = self.own.at[self.rows]

        @pl.when(p.high)
        def _():
            self.copy(0, p.c, p.c + 2, src).start()

        @pl.when(p.low)
        def _():
            self.copy(1, p.c, p.c - 2, src).start()

        self.copy(2, p.c, p.sib, src).start()
        pltpu.make_async_copy(src, self.slot(p.c), self.ls).start()

    def step(self, t):
        p = self.p

        @pl.when(p.z - t >= 0)
        def _():
            k = p.c - 2 * t
            self.copy(2, k, p.sib).wait_recv()

            @pl.when(p.high)
            def _():
                self.copy(0, k, p.c + 2).start()

            self.copy(2, k, p.sib).start()

        @pl.when(p.z + t < p.nz)
        def _():
            k = p.c + 2 * t
            self.copy(2, k, p.sib).wait_recv()

            @pl.when(p.low)
            def _():
                self.copy(1, k, p.c - 2).start()

            self.copy(2, k, p.sib).start()

    def finish(self):
        p = self.p
        src = self.own.at[self.rows]
        for y in range(p.nz):
            self.copy(2, 2 * y + 1 - p.j, p.sib).wait_recv()
        for y in range(p.nz):
            k = 2 * y + p.j
            self.copy(2, k, p.sib).wait_send()

            @pl.when(p.high & (y <= p.z))
            def _(k=k):
                self.copy(0, k, p.c + 2).wait_send()

            @pl.when(p.low & (y >= p.z))
            def _(k=k):
                self.copy(1, k, p.c - 2).wait_send()

        pltpu.make_async_copy(src, self.slot(p.c), self.ls).wait()

    def all_steps(self):
        return [self.first] + [functools.partial(self.step, t) for t in range(1, self.p.nz)]


class Scatter:
    def __init__(self, p, a, x, ud, T, sems, part=None, make=None, stage=None):
        self.p, self.a, self.x, self.ud, self.T, self.sems = p, a, x, ud, T, sems
        self.part, self.make, self.stage = part, make, stage

    def cross(self, y, slot=0):
        p = self.p
        src = self.part.at[2 * y + 1 - p.j] if self.part is not None else self.stage.at[slot]
        return remote(src, self.x.at[y], self.sems.at[0, y], self.sems.at[1, y], "ctx", p.sib)

    def load(self, y):
        return pltpu.make_async_copy(self.part.at[2 * y + self.p.j], self.a.at[y], self.sems.at[2, y])

    def go_up(self, y):
        return remote(self.a.at[y], self.ud.at[y], self.sems.at[3, y], self.sems.at[4, y], "ctx", self.p.c + 2)

    def go_down(self, y, last=False):
        to = self.p.nz if last else y
        return remote(self.a.at[y], self.ud.at[to], self.sems.at[5, y], self.sems.at[6, y], "ctx", self.p.c - 2)

    def begin(self, cross=True, load=True):
        nz = self.p.nz
        order = []
        for i in range(nz):
            order += [y for y in (nz - 1 - i, i) if y not in order]
        for y in order:
            if cross:
                self.cross(y).start()
            if load:
                self.load(y).start()

    def turn(self, i):
        p = self.p
        upper = p.z // (p.nz // 2)
        return upper * i + (1 - upper) * (p.nz - 1 - i)

    def compute(self, between=None):
        p = self.p
        for i in range(p.nz):
            y, slot = self.turn(i), i % 2
            if i > 1:
                self.cross(self.turn(i - 2), slot).wait_send()
            self.make(2 * y + 1 - p.j, self.stage.at[slot])
            self.cross(y, slot).start()
            self.make(2 * y + p.j, self.a.at[y])
            if i > 0:
                pl.when(p.z == 0)(functools.partial(self.edge, self.turn(i - 1), True, False))
                pl.when(p.z == p.nz - 1)(functools.partial(self.edge, self.turn(i - 1), False, i == p.nz - 1))
            if between is not None:
                between(i)

    def edge(self, y, up, last):
        self.ready(y)
        self.add(y, None)
        if up:
            self.go_up(y).start()
        else:
            self.go_down(y, last).start()

    def ready(self, y):
        if self.part is not None:
            self.load(y).wait()
        self.cross(y).wait_recv()

    def add(self, y, extra):
        def fn(r):
            v = self.a[y, r].astype(f32) + self.x[y, r].astype(f32)
            if extra is not None:
                v = v + extra[y, r].astype(f32)
            self.a[y, r] = v.astype(bf16)

        each(fn, 0, self.T)

    def edges(self):
        p = self.p

        @pl.when(p.z == 0)
        def _():
            for y in range(p.nz - 1, 0, -1):
                self.edge(y, True, False)

        @pl.when(p.z == p.nz - 1)
        def _():
            for y in range(p.nz - 1):
                self.edge(y, False, y == p.nz - 2)

    def step(self, t):
        p = self.p

        def upward():
            y = p.nz - 1 - t + p.z
            self.ready(y)
            self.go_up(y).wait_recv()
            self.add(y, self.ud)
            self.go_up(y).start()

        def downward():
            y = t - (p.nz - 1 - p.z)
            self.ready(y)
            self.go_down(y).wait_recv()
            self.add(y, self.ud)
            self.go_down(y, t == p.nz - 2).start()

        half = p.nz // 2
        goes_up = p.low & p.high & (p.z <= t)
        goes_down = p.low & p.high & (p.nz - 1 - p.z <= t)
        pl.when(goes_up & (p.z < half))(upward)
        pl.when(goes_down)(downward)
        pl.when(goes_up & (p.z >= half))(upward)

    def total(self, fn):
        p = self.p
        z = p.z
        self.ready(z)
        pl.when(p.low)(lambda: self.go_up(z).wait_recv())
        pl.when(p.high)(lambda: self.go_down(z, True).wait_recv())

        def run(low, high):
            def body(r):
                v = self.a[z, r].astype(f32) + self.x[z, r].astype(f32)
                if low:
                    v = v + self.ud[z, r].astype(f32)
                if high:
                    v = v + self.ud[p.nz, r].astype(f32)
                fn(r, v)

            each(body, 0, self.T)

        pl.when(p.low & p.high)(lambda: run(True, True))
        pl.when(p.z == 0)(lambda: run(False, p.nz > 1))
        pl.when(p.z == p.nz - 1)(lambda: run(True, False))

    def finish(self, staged=True):
        p = self.p
        for y in range(p.nz):
            if self.part is not None:
                self.cross(y).wait_send()

            @pl.when(p.z < y)
            def _(y=y):
                self.go_up(y).wait_send()

            @pl.when(p.z > y)
            def _(y=y):
                self.go_down(y).wait_send()

        if self.part is None and staged:
            for i in range(max(p.nz - 2, 0), p.nz):
                self.cross(self.turn(i), i % 2).wait_send()

    def all_steps(self):
        return [functools.partial(self.step, i) for i in range(1, self.p.nz - 1)]


def strips(fn, width, step):
    def body(i, _):
        fn(pl.ds(pl.multiple_of(i * step, step), step))
        return 0

    lax.fori_loop(0, width // step, body, 0)


def interleave(first, second):
    for i in range(max(len(first), len(second))):
        if i < len(first):
            first[i]()
        if i < len(second):
            second[i]()


class Peers:
    def __init__(self, p, pick, ss, rs, keep, ls):
        self.p, self.pick, self.ss, self.rs, self.keep, self.ls = p, pick, ss, rs, keep, ls

    def copy(self, k):
        p = self.p
        to = lax.rem(p.f + k, p.nf)
        src, dst = self.pick(to)
        return remote(src, dst, self.ss.at[k], self.rs.at[k], "fsdp", to)

    def start(self):
        for k in range(1, self.p.nf):
            self.copy(k).start()
        if self.keep is not None:
            pltpu.make_async_copy(*self.keep, self.ls).start()

    def wait(self):
        for k in range(1, self.p.nf):
            self.copy(k).wait()
        if self.keep is not None:
            pltpu.make_async_copy(*self.keep, self.ls).wait()


DMA = pltpu.SemaphoreType.DMA


def gather_sems(nc):
    return [DMA((3, nc)), DMA((nc,)), DMA]


def scatter_scratch(nz, T, E):
    return [pltpu.VMEM((nz, T, E), bf16)] * 2 + [pltpu.VMEM((nz + 1, T, E), bf16)]


def params(cid):
    return pltpu.CompilerParams(collective_id=cid, has_side_effects=True, vmem_limit_bytes=62 * 1024 * 1024)


ANY = pl.BlockSpec(memory_space=pl.ANY)
VM = pl.BlockSpec(memory_space=pltpu.VMEM)


def open_kernel(nc, nf, tok, ids, wl, row, ids_row, w, gss, grs, gls, iss, irs, ils, ass, ars, fss, frs, als):
    p = Place(nc, nf)
    greet(p, ctx=True, fsdp=True)
    T = tok.shape[0]
    g = Gather(p, tok, row, pl.ds(0, T), gss, grs, gls)

    def id_copy(k):
        to = lax.rem(p.c + k, nc)
        return remote(ids, ids_row.at[p.c], iss.at[k], irs.at[k], "ctx", to)

    def block(k):
        to = lax.rem(p.c + k, nc)
        return remote(wl.at[to], w.at[p.c, p.f], ass.at[k], ars.at[k], "ctx", to)

    def onward(c, k, m):
        to = lax.rem(p.f + m, nf)
        return remote(w.at[c, p.f], w.at[c, p.f], fss.at[k, m], frs.at[k, m], "fsdp", to)

    def source(k):
        return lax.rem(p.c + nc - k, nc)

    keep_ids = pltpu.make_async_copy(ids, ids_row.at[p.c], ils)
    keep_w = pltpu.make_async_copy(wl.at[p.c], w.at[p.c, p.f], als)
    keep_w.start()
    keep_ids.start()
    for k in range(1, nc):
        block(k).start()
        id_copy(k).start()
    g.first()
    keep_w.wait()

    def spread(k):
        for m in range(1, nf):
            onward(source(k), k, m).start()

    spread(0)
    for k in range(1, nc):
        block(k).wait_recv()
        spread(k)
    for t in range(1, p.nz):
        g.step(t)
    g.finish()
    keep_ids.wait()
    for k in range(1, nc):
        block(k).wait_send()
        id_copy(k).wait()
    for k in range(nc):
        for m in range(1, nf):
            onward(source(k), k, m).wait()


def open_call(nc, nf, tok, ids, wl):
    T, E = tok.shape
    _, R, A = wl.shape
    return pl.pallas_call(
        functools.partial(open_kernel, nc, nf),
        in_specs=[ANY, ANY, ANY],
        out_specs=[ANY, ANY, ANY],
        out_shape=[
            jax.ShapeDtypeStruct((nc, T, E), bf16),
            jax.ShapeDtypeStruct((nc,) + ids.shape, jnp.int32),
            jax.ShapeDtypeStruct((nc, nf, R, A), bf16),
        ],
        scratch_shapes=gather_sems(nc)
        + [DMA((nc,)), DMA((nc,)), DMA, DMA((nc,)), DMA((nc,)), DMA((nc, nf)), DMA((nc, nf)), DMA],
        compiler_params=params(1),
        name="open_row",
    )(tok, ids, wl)


def middle_kernel(
    nc, nf, oT, wo, tok, og, g, wl, hid, n2, dm, w,
    a, x, ud, stage, oblk, own, dmo, rsem, nss, nrs, nls, dss, drs, dls, fss, frs, fls,
):
    p = Place(nc, nf)
    greet(p, fsdp=True)
    T, E = tok.shape

    def make(d, ref):
        oblk[...] = oT[:, pl.ds(pl.multiple_of(d * T, T), T)].T

        def fn(r):
            ref[:, r] = dg(oblk[...], wo[r, :], 1, 1).astype(bf16)

        strips(fn, E, 512)

    rs = Scatter(p, a, x, ud, T, rsem, make=make, stage=stage)
    ag = Gather(p, own, n2, pl.ds(0, T), nss, nrs, nls)
    dmg = Gather(p, dmo, dm, pl.ds(0, T), dss, drs, dls)
    peers = Peers(p, lambda to: (wl, w.at[:, p.f]), fss, frs, (wl, w.at[:, p.f]), fls)
    peers.start()

    def dm_rows(r):
        dmo[r] = (RES * og[r].astype(f32)).astype(bf16)

    each(dm_rows, 0, T)
    dmg.first()
    rs.compute()

    def rows(r, v):
        h = tok[r].astype(f32) + RES * v
        hid[r] = h
        own[r] = (h * lax.rsqrt(jnp.mean(h * h, axis=-1, keepdims=True) + EPS) * g[...]).astype(bf16)

    interleave(dmg.all_steps()[1:], rs.all_steps())
    rs.total(rows)
    ag.first()
    for s in ag.all_steps()[1:]:
        s()
    ag.finish()
    rs.finish()
    dmg.finish()
    peers.wait()


def middle_call(nc, nf, oT, wo, tok, og, g, wl):
    T, E = tok.shape
    _, R, M = wl.shape
    nz = nc // 2
    return pl.pallas_call(
        functools.partial(middle_kernel, nc, nf),
        in_specs=[VM, VM, VM, VM, VM, ANY],
        out_specs=[VM, ANY, ANY, ANY],
        out_shape=[
            jax.ShapeDtypeStruct((T, E), f32),
            jax.ShapeDtypeStruct((nc, T, E), bf16),
            jax.ShapeDtypeStruct((nc, T, E), bf16),
            jax.ShapeDtypeStruct((nc, nf, R, M), bf16),
        ],
        scratch_shapes=scatter_scratch(nz, T, E)
        + [pltpu.VMEM((2, T, E), bf16), pltpu.VMEM((T, oT.shape[0]), bf16)]
        + [pltpu.VMEM((T, E), bf16), pltpu.VMEM((T, E), bf16), DMA((7, nz))]
        + gather_sems(nc)
        + gather_sems(nc)
        + [DMA((nf,)), DMA((nf,)), DMA],
        compiler_params=params(2),
        name="attn_to_mlp",
    )(oT, wo, tok, og, g, wl)


def turn_kernel(nc, nf, fold, *refs):
    it = iter(refs)
    take = lambda n: [next(it) for _ in range(n)]
    n2, dm, dga, dup, act, wm = take(6)
    hid, og, g, dh, da = take(5)
    lay = next(it) if fold else None
    gg, gs, y, gbuf = take(4)
    mpart = next(it) if fold else None
    a, x, ud, own, rsem = take(5)
    nss, nrs, nls, fss, frs, fls = take(6)
    dguv, actv, wide, nt, go, mp, lsem, ssem = take(8)
    p = Place(nc, nf)
    nz = p.nz
    greet(p, fsdp=True)
    T, E = hid.shape
    S, F = act.shape
    F2 = 2 * F
    R = E // (nc * nf)
    B = nf * R

    def fetch(src, dst, i):
        return pltpu.make_async_copy(src, dst, lsem.at[4 + i])

    big = [
        fetch(wm.at[:, pl.ds(0, F2)], wide.at[pl.ds(0, E), pl.ds(0, F2)], 0),
        fetch(dga, dguv.at[:, pl.ds(0, F)], 1),
        fetch(dup, dguv.at[:, pl.ds(F, F)], 2),
        fetch(act, actv, 3),
    ]

    def make(d, ref):
        tok = dguv[pl.ds(pl.multiple_of(d * T, T), T), :]

        def fn(r):
            ref[:, r] = dg(tok, wide[r, pl.ds(0, F2)], 1, 1).astype(bf16)

        strips(fn, E, 512)

    rs = Scatter(p, a, x, ud, T, rsem, make=make, stage=mp)
    ag = Gather(p, own, da, pl.ds(0, T), nss, nrs, nls)
    if fold:
        x2, ud2, wdv, msem, psem = take(5)
        ms = Scatter(p, a, x2, ud2, T, msem, part=mpart)
        big.append(fetch(wm.at[:, pl.ds(F2, F)], wdv, 4))
    for cp in big:
        cp.start()

    def spot(i):
        return pl.ds(pl.multiple_of(i * B, B), B)

    def column(b, slot):
        at = spot(b)
        return (
            pltpu.make_async_copy(n2.at[:, at], wide.at[pl.ds(0, S), spot(slot)], lsem.at[slot]),
            pltpu.make_async_copy(dm.at[:, at], wide.at[pl.ds(0, S), spot(2 + slot)], lsem.at[2 + slot]),
        )

    def keep(b, slot):
        return pltpu.make_async_copy(go.at[slot], gbuf.at[b], ssem.at[slot])

    def peer(b, k):
        to = lax.rem(p.f + k, nf)
        at = pl.ds(pl.multiple_of(to * R, R), R)
        return remote(gbuf.at[b, at], y.at[p.f, b], fss.at[k, b], frs.at[k, b], "fsdp", to)

    def terms(b, slot):
        at = pl.ds(pl.multiple_of(p.f * R, R), R)
        srcs = [gbuf.at[b, at]] + [y.at[lax.rem(p.f + k, nf), b] for k in range(1, nf)]
        return [
            pltpu.make_async_copy(src, go.at[slot, pl.ds(i * R, R)], fls.at[slot, i]) for i, src in enumerate(srcs)
        ]

    def stored(b, slot):
        return pltpu.make_async_copy(go.at[slot, pl.ds(0, R)], gs.at[b], ssem.at[slot])

    def sums(first, last):
        for b in range(first, last):
            slot = b % 2
            for k in range(1, nf):
                peer(b, k).wait()
            if b > 1:
                stored(b - 2, slot).wait()
            cps = terms(b, slot)
            for cp in cps:
                cp.start()
            for cp in cps:
                cp.wait()

            def fn(r, slot=slot):
                v = go[slot, r].astype(f32)
                for i in range(1, nf):
                    v = v + go[slot, pl.ds(r.start + i * R, CH)].astype(f32)
                go[slot, r] = v.astype(bf16)

            each(fn, 0, R)
            stored(b, slot).start()

    def send(b):
        keep(b, b % 2).wait()
        for k in range(1, nf):
            peer(b, k).start()

    def grads(b, _):
        slot = b % 2

        @pl.when(b + 1 < nc)
        def _():
            for cp in column(b + 1, 1 - slot):
                cp.start()

        now = column(b, slot)
        for at, val, base, width, cp in ((slot, dguv, 0, F2, now[0]), (2 + slot, actv, F2, F, now[1])):
            cp.wait()
            nt[...] = wide[pl.ds(0, S), spot(at)].T
            step = min(512, width)

            def dots(i, _, val=val, base=base, step=step):
                at = pl.multiple_of(i * step, step)
                v = jnp.dot(nt[...], val[:, pl.ds(at, step)], preferred_element_type=f32)
                go[slot, :, pl.ds(pl.multiple_of(base + at, step), step)] = v.astype(bf16)
                return 0

            lax.fori_loop(0, width // step, dots, 0)
        keep(b, slot).start()

        @pl.when(b > 0)
        def _():
            send(b - 1)

        return 0

    def mlp(b, _):
        slot = b % 2
        out = pltpu.make_async_copy(mp.at[slot], mpart.at[b], psem.at[slot])

        @pl.when(b > 1)
        def _():
            out.wait()

        tok = actv[pl.ds(pl.multiple_of(b * T, T), T), :]

        def dots(i, _):
            at = pl.ds(pl.multiple_of(i * 512, 512), 512)
            mp[slot, :, at] = dg(tok, wdv[at, :], 1, 1).astype(bf16)
            return 0

        lax.fori_loop(0, E // 512, dots, 0)
        out.start()
        return 0

    gg[...] = jnp.zeros_like(gg)
    for cp in big[:3]:
        cp.wait()
    rs.compute()
    for cp in column(0, 0):
        cp.start()
    for cp in big[3:]:
        cp.wait()
    steps = rs.all_steps()
    bounds = [nc * i // (len(steps) + 1) for i in range(len(steps) + 2)]
    for i in range(len(steps) + 1):
        lax.fori_loop(bounds[i], bounds[i + 1], grads, 0)
        if i < len(steps):
            steps[i]()
    send(nc - 1)
    if fold:
        for i in range(max(nz - 2, 0), nz):
            rs.cross(rs.turn(i), i % 2).wait_send()
        lax.fori_loop(0, nc, mlp, 0)
        for slot in range(2):
            pltpu.make_async_copy(mp.at[slot], mpart.at[slot], psem.at[slot]).wait()
        ms.begin(load=False)

    def rows(r, dn):
        h = hid[r]
        inv = lax.rsqrt(jnp.mean(h * h, axis=-1, keepdims=True) + EPS)
        xn = h * inv
        e = dn * g[...]
        v = og[r].astype(f32) + inv * (e - xn * jnp.mean(e * xn, axis=-1, keepdims=True))
        dh[r] = v
        own[r] = (RES * v).astype(bf16)
        gg[...] += jnp.sum((xn * dn).reshape(CH // 8, 8, E), axis=0)

    rs.total(rows)
    ag.first()
    rs.finish(not fold)
    if fold:
        ms.begin(cross=False)
        ms.edges()
    sums(0, nc // 4)
    more = ms.all_steps() if fold else []
    done = nc // 4
    for i, s in enumerate(ag.all_steps()[1:]):
        s()
        if i < len(more):
            more[i]()
        upto = min(nc - 1, done + max(1, nc // 4))
        sums(done, upto)
        done = upto
    if fold:

        def out(r, v):
            lay[r] = (hid[r] + RES * v).astype(bf16)

        ms.total(out)
        ms.finish()
    ag.finish()
    sums(done, nc)
    for b in range(nc - 2, nc):
        stored(b, b % 2).wait()


def turn_call(nc, nf, fold, n2, dm, dga, dup, act, wm, hid, og, g):
    T, E = hid.shape
    S, F = act.shape
    F2, M = 2 * F, 3 * F
    R = E // (nc * nf)
    B = nf * R
    nz = nc // 2
    VMEM = pltpu.VMEM
    return pl.pallas_call(
        functools.partial(turn_kernel, nc, nf, fold),
        in_specs=[ANY] * 6 + [VM, VM, VM],
        out_specs=[VM, ANY] + [VM] * fold + [VM, ANY, ANY, ANY] + [ANY] * fold,
        out_shape=[jax.ShapeDtypeStruct((T, E), f32), jax.ShapeDtypeStruct((nc, T, E), bf16)]
        + [jax.ShapeDtypeStruct((T, E), bf16)] * fold
        + [
            jax.ShapeDtypeStruct((8, E), f32),
            jax.ShapeDtypeStruct((nc, R, M), bf16),
            jax.ShapeDtypeStruct((nf, nc, R, M), bf16),
            jax.ShapeDtypeStruct((nc, B, M), bf16),
        ]
        + [jax.ShapeDtypeStruct((nc, T, E), bf16)] * fold,
        scratch_shapes=scatter_scratch(nz, T, E)
        + [VMEM((T, E), bf16), DMA((7, nz))]
        + gather_sems(nc)
        + [DMA((nf, nc)), DMA((nf, nc)), DMA((2, nf))]
        + [VMEM((S, F2), bf16), VMEM((S, F), bf16), VMEM((max(E, S), max(F2, 4 * B)), bf16)]
        + [VMEM((B, S), bf16), VMEM((2, B, M), bf16), VMEM((2, T, E), bf16), DMA((9,)), DMA((2,))]
        + [VMEM((nz, T, E), bf16), VMEM((nz + 1, T, E), bf16), VMEM((E, F), bf16), DMA((7, nz)), DMA((2,))] * fold,
        compiler_params=params(3),
        name="mlp_to_attn",
    )(n2, dm, dga, dup, act, wm, hid, og, g)


def close_kernel(
    nc, nf, dqkv, wq, oT, n1, da, tok, dh, g, ggm, dx, gout, ggout,
    a, x, ud, stage, dblk, wqv, big, gt, gb, y, zb, gg, gbuf, gsum, gfin, rsem, lsem,
    fss, frs, fls, css, crs, cls, s1, r1, s2, r2, l2,
):
    p = Place(nc, nf)
    greet(p, ctx=True, fsdp=True)
    T, E = tok.shape
    Q = dqkv.shape[0]
    H = oT.shape[0]
    R = E // (nc * nf)
    B = nf * R
    weights = pltpu.make_async_copy(wq.at[:, pl.ds(0, Q)], wqv, lsem.at[4])
    weights.start()

    def column(b, slot):
        at = pl.ds(pl.multiple_of(b * B, B), B)
        return (
            pltpu.make_async_copy(n1.at[:, at], big.at[0, slot], lsem.at[slot]),
            pltpu.make_async_copy(da.at[:, at], big.at[1, slot], lsem.at[2 + slot]),
        )

    for cp in column(0, 0):
        cp.start()

    def make(d, ref):
        dblk[...] = dqkv[:, pl.ds(pl.multiple_of(d * T, T), T)].T

        def fn(r):
            ref[:, r] = dg(dblk[...], wqv[r, :], 1, 1).astype(bf16)

        strips(fn, E, 512)

    rs = Scatter(p, a, x, ud, T, rsem, make=make, stage=stage)

    def pieces(to):
        return gb.at[:, pl.ds(pl.multiple_of(to * R, R), R)], y.at[p.f]

    peers = Peers(p, pieces, fss, frs, pieces(p.f), fls)
    gg[...] = jnp.zeros_like(gg)

    def piece(k):
        to = lax.rem(p.c + k, nc)
        return remote(zb.at[to], gout.at[p.c], css.at[k], crs.at[k], "ctx", to)

    mine = pltpu.make_async_copy(zb.at[p.c], gout.at[p.c], cls)

    def grads():
        peers.wait()
        for c in range(nc):

            def fn(r):
                v = y[0, c, r].astype(f32)
                for m in range(1, nf):
                    v = v + y[m, c, r].astype(f32)
                zb[c, r] = v.astype(bf16)

            each(fn, 0, R)
        for k in range(1, nc):
            piece(k).start()
        mine.start()

    def rows(r, dn):
        t = tok[r].astype(f32)
        inv = lax.rsqrt(jnp.mean(t * t, axis=-1, keepdims=True) + EPS)
        xn = t * inv
        e = dn * g[...]
        dx[r] = dh[r] + inv * (e - xn * jnp.mean(e * xn, axis=-1, keepdims=True))
        gg[...] += jnp.sum((xn * dn).reshape(CH // 8, 8, E), axis=0)

    weights.wait()
    rs.compute()

    def products(b, _):
        slot = b % 2

        @pl.when(b + 1 < nc)
        def _():
            for cp in column(b + 1, 1 - slot):
                cp.start()

        for cp in column(b, slot):
            cp.wait()
        gt[pl.ds(0, Q), :] = dg(dqkv[...], big[0, slot], 1, 0)
        gt[pl.ds(Q, H), :] = dg(oT[...], big[1, slot], 1, 0)
        gb[b] = gt[...].T.astype(bf16)
        return 0

    lax.fori_loop(0, nc, products, 0)
    peers.start()
    for s in rs.all_steps():
        s()
    grads()
    rs.total(rows)

    groups = E // 128
    sa = jnp.sum(gg[...], axis=0, keepdims=True)
    sm = jnp.sum(ggm[...], axis=0, keepdims=True)
    for i in range(groups):
        gbuf[p.f, i] = jnp.concatenate(
            [sa[:, i * 128 : (i + 1) * 128], sm[:, i * 128 : (i + 1) * 128], jnp.zeros((6, 128), f32)], axis=0
        )

    def over(k):
        to = lax.rem(p.f + k, nf)
        return remote(gbuf.at[p.f], gbuf.at[p.f], s1.at[k], r1.at[k], "fsdp", to)

    for k in range(1, nf):
        over(k).start()
    for k in range(1, nf):
        over(k).wait()
    v = gbuf[0]
    for m in range(1, nf):
        v = v + gbuf[m]
    gsum[...] = v
    per = 128 // R

    def along(k):
        to = lax.rem(p.c + k, nc)
        return remote(gsum.at[(to * nf + p.f) // per], gfin.at[p.c], s2.at[k], r2.at[k], "ctx", to)

    for k in range(1, nc):
        along(k).start()
    own = pltpu.make_async_copy(gsum.at[(p.c * nf + p.f) // per], gfin.at[p.c], l2)
    own.start()
    own.wait()
    for k in range(1, nc):
        along(k).wait()
    t = gfin[0]
    for m in range(1, nc):
        t = t + gfin[m]
    ggout[...] = t
    for k in range(1, nc):
        piece(k).wait()
    mine.wait()
    rs.finish()


def close_call(nc, nf, dqkv, wq, oT, n1, da, tok, dh, g, ggm):
    T, E = tok.shape
    S = n1.shape[0]
    Q, H = dqkv.shape[0], oT.shape[0]
    A = Q + H
    R = E // (nc * nf)
    nz = nc // 2
    VMEM = pltpu.VMEM
    return pl.pallas_call(
        functools.partial(close_kernel, nc, nf),
        in_specs=[VM, ANY, VM, ANY, ANY, VM, VM, VM, VM],
        out_specs=[VM, ANY, VM],
        out_shape=[
            jax.ShapeDtypeStruct((T, E), f32),
            jax.ShapeDtypeStruct((nc, R, A), bf16),
            jax.ShapeDtypeStruct((8, 128), f32),
        ],
        scratch_shapes=scatter_scratch(nz, T, E)
        + [VMEM((2, T, E), bf16), VMEM((T, Q), bf16), VMEM((E, Q), bf16), VMEM((2, 2, S, nf * R), bf16)]
        + [VMEM((A, nf * R), f32), VMEM((nc, nf * R, A), bf16)]
        + [
            VMEM((nf, nc, R, A), bf16),
            VMEM((nc, R, A), bf16),
            VMEM((8, E), f32),
            VMEM((nf, E // 128, 8, 128), f32),
            VMEM((E // 128, 8, 128), f32),
            VMEM((nc, 8, 128), f32),
            DMA((7, nz)),
            DMA((5,)),
        ]
        + [DMA((nf,)), DMA((nf,)), DMA, DMA((nc,)), DMA((nc,)), DMA]
        + [DMA((nf,)), DMA((nf,)), DMA((nc,)), DMA((nc,)), DMA],
        compiler_params=params(4),
        name="close_row",
    )(dqkv, wq, oT, n1, da, tok, dh, g, ggm)


def rms(v):
    inv = lax.rsqrt(jnp.mean(v * v, axis=-1, keepdims=True) + EPS)
    return v * inv, inv


def rms_back(x, inv, e):
    return inv * (e - x * jnp.mean(e * x, axis=-1, keepdims=True))


def rotate(v, cos, sin, sign):
    heads = v.shape[0] // HD
    v = v.reshape(heads, 2, HD // 2, v.shape[1])
    a, b = v[:, 0], v[:, 1]
    s = sign * sin
    return jnp.stack([a * cos - b * s, b * cos + a * s], axis=1).reshape(heads * HD, -1)


def local(
    tokens, seq_ids, positions, block_ids, gain_attn, w_query, w_key, w_value, w_out,
    gain_mlp, w_gate, w_up, w_down, out_grad,
):
    nc = lax.axis_size("ctx")
    nf = lax.axis_size("fsdp")
    nz = nc // 2
    T, E = tokens.shape[1:]
    R = w_query.shape[0]
    S = T * nc
    FFL = w_gate.shape[1] // nc
    nh = QUERY_HEADS // nc
    rep = nc // KEY_VALUE_HEADS
    QW = nh * HD
    KO, VO, OO, GO = QW, QW + HD, QW + 2 * HD, 2 * QW + 2 * HD
    tok, og = tokens[0], out_grad[0]

    def cols(w):
        return w.astype(bf16).reshape(R, nc, -1)

    def kv_cols(w):
        return jnp.repeat(w.astype(bf16).reshape(R, KEY_VALUE_HEADS, HD), rep, axis=1)

    def blocks(parts):
        return jnp.transpose(jnp.concatenate(parts, axis=2), (1, 0, 2))

    def exchange(w):
        return lax.all_to_all(w, "ctx", 0, 0, tiled=True)

    gains = jnp.stack([gain_attn, gain_mlp], axis=1).astype(bf16)
    gains = jnp.broadcast_to(jnp.pad(gains, ((0, 0), (0, 126)))[:, None], (R, nc, 128))
    wl = blocks([cols(w_query), kv_cols(w_key), kv_cols(w_value), cols(w_out), gains])
    ids = jnp.pad(jnp.concatenate([seq_ids, positions, block_ids], axis=0), ((0, 5), (0, 0)))
    row_tok, ids, wa = open_call(nc, nf, tok, ids, wl)
    wa = wa.reshape(E, -1)
    g_attn, g_mlp = wa[:, GO].astype(f32)[None], wa[:, GO + 1].astype(f32)[None]

    wm = blocks([cols(w_gate), cols(w_up), cols(w_down)])
    row_tok, wm = lax.optimization_barrier((row_tok, wm))
    wm = exchange(wm)

    seq, pos, blk = (ids[:, i].reshape(S) for i in range(3))
    place = jnp.arange(S, dtype=jnp.int32)
    cut = jnp.sum((seq == 0).astype(jnp.int32))
    first = place - pos
    last = jnp.minimum(first + BLOCK * (blk + 1), jnp.where(seq == 0, cut, S))
    st, en = first[None], last[None]
    freq = ROPE_BASE ** (-(jnp.arange(HD // 2, dtype=f32) * 2.0) / HD)
    ang = freq[:, None] * pos.astype(f32)[None, :]
    cos, sin = jnp.cos(ang), jnp.sin(ang)

    x1r, _ = rms(row_tok.reshape(S, E).astype(f32))
    n1 = (x1r * g_attn).astype(bf16)
    w_qkv, w_o = wa[:, :OO], wa[:, OO:GO]
    qkv = dg(w_qkv, n1, 0, 1)
    qkT = rotate(qkv[:VO], cos, sin, 1.0).astype(bf16)
    qT, kT = qkT[:QW], qkT[QW:]
    vT = qkv[VO:].astype(bf16)
    k, v = kT.T, vT.T
    oT, oTb, lse = attn_fwd(qT, k, vT, st, en)

    hidden, n2, dm, wm = middle_call(nc, nf, oTb, w_o, tok, og, g_mlp, wm)
    n2, dm, wm = n2.reshape(S, E), dm.reshape(S, E), wm.reshape(E, -1)
    w_gu, w_d = wm[:, : 2 * FFL], wm[:, 2 * FFL :]
    gu = dg(n2, w_gu, 1, 0)
    gate, up = gu[:, :FFL], gu[:, FFL:]
    sg = jax.nn.sigmoid(gate)
    act = (gate * sg * up).astype(bf16)
    d_act = dg(dm, w_d, 1, 0)
    d_gate = (d_act * up * sg * (1.0 + gate * (1.0 - sg))).astype(bf16)
    d_up = (d_act * gate * sg).astype(bf16)
    turn = (n2, dm, d_gate, d_up, act, wm, hidden, og, g_mlp)
    if nz <= 4:
        dh, da, layer_out, ggm, gm = turn_call(nc, nf, True, *turn)[:5]
    else:
        dh, da, ggm, gm = turn_call(nc, nf, False, *turn)[:4]
        mlp = dg(act, w_d, 1, 1).astype(bf16)
        mlp = lax.psum_scatter(mlp, "ctx", scatter_dimension=0, tiled=True)
        layer_out = (hidden + RES * mlp.astype(f32)).astype(bf16)
    da = da.reshape(S, E)
    gm = exchange(gm)

    dqkv = attn_bwd(qT, da, w_o.T, oT, lse, st, en, cos, sin, k, kT, v)
    input_grad, ga, gains = close_call(nc, nf, dqkv, wa, oTb, n1, da, tok, dh, g_attn, ggm)
    at = lax.rem((lax.axis_index("ctx") * nf + lax.axis_index("fsdp")) * R, 128)
    gains = lax.dynamic_slice_in_dim(gains, at, R, 1)

    def rows(g):
        return jnp.transpose(g.astype(f32), (1, 0, 2)).reshape(R, -1)

    def kv_rows(g):
        g = g.astype(f32).reshape(KEY_VALUE_HEADS, rep, R, HD)
        return jnp.transpose(jnp.sum(g, axis=1), (1, 0, 2)).reshape(R, -1)

    return (
        layer_out[None],
        input_grad[None],
        gains[0],
        rows(ga[:, :, :KO]),
        kv_rows(ga[:, :, KO:VO]),
        kv_rows(ga[:, :, VO:OO]),
        rows(ga[:, :, OO:]),
        gains[1],
        rows(gm[:, :, :FFL]),
        rows(gm[:, :, FFL : 2 * FFL]),
        rows(gm[:, :, 2 * FFL :]),
    )


def solution(mesh):
    w1, w2 = P(("ctx", "fsdp")), P(("ctx", "fsdp"), None)
    act, ids = P("fsdp", "ctx", None), P("fsdp", "ctx")
    return jax.shard_map(
        local,
        mesh=mesh,
        in_specs=(act, ids, ids, ids, w1, w2, w2, w2, w2, w1, w2, w2, w2, act),
        out_specs=(act, act, w1, w2, w2, w2, w2, w1, w2, w2, w2),
        check_vma=False,
    )
```

```python
import functools

import jax
import jax.numpy as jnp
from jax import lax
from jax.experimental import pallas as pl
from jax.experimental.pallas import tpu as pltpu
from jax.sharding import PartitionSpec as P

QUERY_HEADS = 32
KEY_VALUE_HEADS = 8
HD = 64
BLOCK = 256
EPS = 1e-05
ROPE_BASE = 10000000.0
SCALE = 0.015625
RES = 0.22
NEG = -1e30
bf16 = jnp.bfloat16
f32 = jnp.float32


def dg(a, b, ca, cb):
    return lax.dot_general(a, b, (((ca,), (cb,)), ((), ())), preferred_element_type=f32)


def lanes(v, heads):
    return jnp.concatenate([v[h * HD : (h + 1) * HD, :] for h in range(heads)], axis=1)


def turned_back(v, cos, sin):
    half = HD // 2
    out = []
    for h in range(v.shape[0] // HD):
        a, b = v[h * HD : h * HD + half, :], v[h * HD + half : (h + 1) * HD, :]
        out += [a * cos + b * sin, b * cos - a * sin]
    return jnp.concatenate(out, axis=0)


def key_blocks(st, en, tk):
    return jnp.min(st) // tk, (jnp.max(en) + tk - 1) // tk


def attn_fwd_kernel(nh, tq, tk, q_ref, k_ref, v_ref, st_ref, en_ref, o_ref, ob_ref, l_ref, a_ref):
    lo, hi = key_blocks(st_ref[...], en_ref[...], tk)
    q = lanes(q_ref[...] * jnp.asarray(SCALE, bf16), nh)
    st = jnp.concatenate([st_ref[...]] * nh, axis=1)
    en = jnp.concatenate([en_ref[...]] * nh, axis=1)
    W = nh * tq
    a_ref[...] = jnp.zeros_like(a_ref)

    def body(j, c):
        m, l = c
        off = pl.multiple_of(j * tk, tk)
        jj = off + lax.broadcasted_iota(jnp.int32, (tk, W), 0)
        s = dg(k_ref[pl.ds(off, tk), :], q, 1, 0)
        s = jnp.where((jj >= st) & (jj < en), s, NEG)
        mn = jnp.maximum(m, jnp.max(s, axis=0, keepdims=True))
        p = jnp.exp(s - mn)
        sh = jnp.exp(m - mn)
        l = l * sh + jnp.sum(p, axis=0, keepdims=True)
        a_ref[...] = a_ref[...] * sh + dg(v_ref[:, pl.ds(off, tk)], p.astype(bf16), 1, 0)
        return mn, l

    m, l = lax.fori_loop(lo, hi, body, (jnp.full((1, W), 0.1 * NEG, f32), jnp.zeros((1, W), f32)))
    o = a_ref[...] / l
    ls = m + jnp.log(l)
    for h in range(nh):
        oh = o[:, h * tq : (h + 1) * tq]
        o_ref[h * HD : (h + 1) * HD, :] = oh
        ob_ref[h * HD : (h + 1) * HD, :] = oh.astype(bf16)
        l_ref[h : h + 1, :] = ls[:, h * tq : (h + 1) * tq]


def attn_fwd(qT, k, vT, st, en, tq=256, tk=256):
    n, S = qT.shape
    nh = n // HD
    blk = lambda r: pl.BlockSpec((r, tq), lambda i: (0, i))
    full = lambda s: pl.BlockSpec(s, lambda i: (0, 0))
    return pl.pallas_call(
        functools.partial(attn_fwd_kernel, nh, tq, tk),
        grid=(S // tq,),
        in_specs=[blk(n), full((S, HD)), full((HD, S)), blk(1), blk(1)],
        out_specs=[blk(n), blk(n), blk(nh)],
        out_shape=[
            jax.ShapeDtypeStruct((n, S), f32),
            jax.ShapeDtypeStruct((n, S), bf16),
            jax.ShapeDtypeStruct((nh, S), f32),
        ],
        scratch_shapes=[pltpu.VMEM((HD, nh * tq), f32)],
        cost_estimate=pl.CostEstimate(
            flops=2 * S * S * n, bytes_accessed=8 * n * S, transcendentals=S * S * nh // 2
        ),
        name="attn_fwd",
    )(qT, k, vT, st, en)


def attn_bwd_kernel(
    nh, tq, tk, q_ref, da_ref, wo_ref, o_ref, lse_ref, st_ref, en_ref, cos_ref, sin_ref, k_ref, kT_ref, v_ref,
    out_ref, dk_ref, dv_ref, acc,
):
    i = pl.program_id(0)
    n = nh * HD

    @pl.when(i == 0)
    def _():
        dk_ref[...] = jnp.zeros_like(dk_ref)
        dv_ref[...] = jnp.zeros_like(dv_ref)

    here = pl.ds(pl.multiple_of(i * tq, tq), tq)
    lo, hi = key_blocks(st_ref[...], en_ref[...], tk)
    q = lanes(q_ref[...] * jnp.asarray(SCALE, bf16), nh)
    do = lanes(dg(wo_ref[...], da_ref[...], 1, 1).astype(bf16), nh)
    o = lanes(o_ref[...], nh)
    dl = jnp.sum(do.astype(f32) * o, axis=0, keepdims=True)
    ls = jnp.concatenate([lse_ref[h : h + 1, :] for h in range(nh)], axis=1)
    st = jnp.concatenate([st_ref[...]] * nh, axis=1)
    en = jnp.concatenate([en_ref[...]] * nh, axis=1)
    acc[...] = jnp.zeros_like(acc)

    def body(j, _):
        off = pl.multiple_of(j * tk, tk)
        at = pl.ds(off, tk)
        jj = off + lax.broadcasted_iota(jnp.int32, (tk, nh * tq), 0)
        s = dg(k_ref[at, :], q, 1, 0)
        dp = dg(v_ref[at, :], do, 1, 0)
        p = jnp.exp(jnp.where((jj >= st) & (jj < en), s - ls, NEG))
        ds = (p * (dp - dl)).astype(bf16)
        acc[...] += dg(kT_ref[:, at], ds, 1, 0)
        dk_ref[:, at] += dg(q, ds, 1, 1)
        dv_ref[:, at] += dg(do, p.astype(bf16), 1, 1)
        return 0

    lax.fori_loop(lo, hi, body, 0)
    dq = jnp.concatenate([acc[:, h * tq : (h + 1) * tq] for h in range(nh)], axis=0) * SCALE
    out_ref[pl.ds(0, n), here] = turned_back(dq, cos_ref[:, here], sin_ref[:, here]).astype(bf16)

    @pl.when(i == pl.num_programs(0) - 1)
    def _():
        out_ref[pl.ds(n, HD), :] = turned_back(dk_ref[...], cos_ref[...], sin_ref[...]).astype(bf16)
        out_ref[pl.ds(n + HD, HD), :] = dv_ref[...].astype(bf16)


def attn_bwd(qT, da, woT, oT, lse, st, en, cos, sin, k, kT, v, tq=256, tk=256):
    n, S = qT.shape
    E = da.shape[1]
    nh = n // HD
    blk = lambda r: pl.BlockSpec((r, tq), lambda i: (0, i))
    full = lambda s: pl.BlockSpec(s, lambda i: (0, 0))
    return pl.pallas_call(
        functools.partial(attn_bwd_kernel, nh, tq, tk),
        grid=(S // tq,),
        in_specs=[
            blk(n), pl.BlockSpec((tq, E), lambda i: (i, 0)), full((n, E)), blk(n), blk(nh), blk(1), blk(1),
            full((HD // 2, S)), full((HD // 2, S)), full((S, HD)), full((HD, S)), full((S, HD)),
        ],
        out_specs=full((n + 2 * HD, S)),
        out_shape=jax.ShapeDtypeStruct((n + 2 * HD, S), bf16),
        scratch_shapes=[pltpu.VMEM((HD, S), f32), pltpu.VMEM((HD, S), f32), pltpu.VMEM((HD, nh * tq), f32)],
        cost_estimate=pl.CostEstimate(
            flops=5 * S * S * n, bytes_accessed=10 * n * S, transcendentals=S * S * nh // 2
        ),
        name="attn_bwd",
    )(qT, da, woT, oT, lse, st, en, cos, sin, k, kT, v)


MESH = pl.DeviceIdType.MESH
CH = 16


class Place:
    def __init__(self, nc, nf):
        self.nc, self.nf, self.nz = nc, nf, nc // 2
        self.c = lax.axis_index("ctx")
        self.f = lax.axis_index("fsdp")
        self.z = self.c // 2
        self.j = self.c % 2
        self.sib = self.z * 2 + (1 - self.j)
        self.low = self.z > 0
        self.high = self.z < self.nz - 1


def remote(src, dst, ss, rs, axis, idx):
    return pltpu.make_async_remote_copy(
        src_ref=src, dst_ref=dst, send_sem=ss, recv_sem=rs, device_id={axis: idx}, device_id_type=MESH
    )


def greet(p, line=True, ctx=False, fsdp=False):
    sem = pltpu.get_barrier_semaphore()
    count = 0

    def tell(axis, idx):
        pl.semaphore_signal(sem, inc=1, device_id={axis: idx}, device_id_type=MESH)

    if ctx:
        for k in range(1, p.nc):
            tell("ctx", lax.rem(p.c + k, p.nc))
        count = p.nc - 1
    elif line:
        tell("ctx", p.sib)

        @pl.when(p.low)
        def _():
            tell("ctx", p.c - 2)

        @pl.when(p.high)
        def _():
            tell("ctx", p.c + 2)

        count = 1 + p.low.astype(jnp.int32) + p.high.astype(jnp.int32)
    if fsdp:
        for k in range(1, p.nf):
            tell("fsdp", lax.rem(p.f + k, p.nf))
        count = count + p.nf - 1
    pl.semaphore_wait(sem, count)


def each(fn, start, size, step=CH):
    def body(r, _):
        fn(pl.ds(pl.multiple_of(start + r * step, step), step))
        return 0

    lax.fori_loop(0, size // step, body, 0)


class Gather:
    def __init__(self, p, own, full, rows, ss, rs, ls):
        self.p, self.own, self.full, self.rows, self.ss, self.rs, self.ls = p, own, full, rows, ss, rs, ls

    def slot(self, k):
        return self.full.at[k, self.rows]

    def copy(self, way, k, to, src=None):
        return remote(self.slot(k) if src is None else src, self.slot(k), self.ss.at[way, k], self.rs.at[k], "ctx", to)

    def first(self):
        p = self.p
        src = None if self.own is None else self.own.at[self.rows]

        @pl.when(p.high)
        def _():
            self.copy(0, p.c, p.c + 2, src).start()

        @pl.when(p.low)
        def _():
            self.copy(1, p.c, p.c - 2, src).start()

        self.copy(2, p.c, p.sib, src).start()
        if src is not None:
            pltpu.make_async_copy(src, self.slot(p.c), self.ls).start()

    def step(self, t):
        p = self.p

        @pl.when(p.z - t >= 0)
        def _():
            k = p.c - 2 * t
            self.copy(2, k, p.sib).wait_recv()

            @pl.when(p.high)
            def _():
                self.copy(0, k, p.c + 2).start()

            self.copy(2, k, p.sib).start()

        @pl.when(p.z + t < p.nz)
        def _():
            k = p.c + 2 * t
            self.copy(2, k, p.sib).wait_recv()

            @pl.when(p.low)
            def _():
                self.copy(1, k, p.c - 2).start()

            self.copy(2, k, p.sib).start()

    def arrived(self, k):
        self.copy(2, k, self.p.sib).wait_recv()

    def finish(self, arrived=False):
        p = self.p
        if not arrived:
            for y in range(p.nz):
                self.arrived(2 * y + 1 - p.j)
        for y in range(p.nz):
            k = 2 * y + p.j
            self.copy(2, k, p.sib).wait_send()

            @pl.when(p.high & (y <= p.z))
            def _(k=k):
                self.copy(0, k, p.c + 2).wait_send()

            @pl.when(p.low & (y >= p.z))
            def _(k=k):
                self.copy(1, k, p.c - 2).wait_send()

        if self.own is not None:
            pltpu.make_async_copy(self.own.at[self.rows], self.slot(p.c), self.ls).wait()

    def all_steps(self):
        return [self.first] + [functools.partial(self.step, t) for t in range(1, self.p.nz)]


class Scatter:
    def __init__(self, p, a, x, ud, T, sems, part=None, make=None, stage=None):
        self.p, self.a, self.x, self.ud, self.T, self.sems = p, a, x, ud, T, sems
        self.part, self.make, self.stage = part, make, stage
        self.size = T // CUTS

    def cross(self, y, slot=0):
        p = self.p
        src = self.part.at[2 * y + 1 - p.j] if self.part is not None else self.stage.at[slot]
        return remote(src, self.x.at[y], self.sems.at[0, y, 0], self.sems.at[1, y, 0], "ctx", p.sib)

    def load(self, y):
        return pltpu.make_async_copy(self.part.at[2 * y + self.p.j], self.a.at[y], self.sems.at[2, y, 0])

    def go_up(self, y, h):
        at = pl.ds(h * self.size, self.size)
        ss, rs = self.sems.at[3, y, h], self.sems.at[4, y, h]
        return remote(self.a.at[y, at], self.ud.at[y, at], ss, rs, "ctx", self.p.c + 2)

    def go_down(self, y, h, last=False):
        at = pl.ds(h * self.size, self.size)
        ss, rs = self.sems.at[5, y, h], self.sems.at[6, y, h]
        return remote(self.a.at[y, at], self.ud.at[self.p.nz if last else y, at], ss, rs, "ctx", self.p.c - 2)

    def begin(self, cross=True, load=True):
        nz = self.p.nz
        order = []
        for i in range(nz):
            order += [y for y in (nz - 1 - i, i) if y not in order]
        for y in order:
            if cross:
                self.cross(y).start()
            if load:
                self.load(y).start()

    def turn(self, i):
        p = self.p
        upper = p.z // (p.nz // 2)
        return upper * i + (1 - upper) * (p.nz - 1 - i)

    def compute(self):
        p = self.p
        for i in range(p.nz):
            y, slot = self.turn(i), i % 2
            if i > 1:
                self.cross(self.turn(i - 2), slot).wait_send()
            self.make(2 * y + 1 - p.j, self.stage.at[slot])
            self.cross(y, slot).start()
            self.make(2 * y + p.j, self.a.at[y])
            if i < p.nz - 1:
                pl.when(p.z == 0)(functools.partial(self.edge, y, True, False))
                pl.when(p.z == p.nz - 1)(functools.partial(self.edge, y, False, i == p.nz - 2))

    def edge(self, y, up, last):
        self.ready(y)
        for h in range(CUTS):
            self.add(y, h, None)
            if up:
                self.go_up(y, h).start()
            else:
                self.go_down(y, h, last).start()

    def ready(self, y):
        if self.part is not None:
            self.load(y).wait()
        self.cross(y).wait_recv()

    def add(self, y, h, extra):
        def fn(r):
            v = self.a[y, r].astype(f32) + self.x[y, r].astype(f32)
            if extra is not None:
                v = v + extra[y, r].astype(f32)
            self.a[y, r] = v.astype(bf16)

        each(fn, h * self.size, self.size)

    def edges(self):
        p = self.p

        @pl.when(p.z == 0)
        def _():
            for y in range(p.nz - 1, 0, -1):
                self.edge(y, True, False)

        @pl.when(p.z == p.nz - 1)
        def _():
            for y in range(p.nz - 1):
                self.edge(y, False, y == p.nz - 2)

    def step(self, t, h):
        p = self.p

        def upward():
            y = p.nz - 1 - t + p.z
            if h == 0:
                self.ready(y)
            self.go_up(y, h).wait_recv()
            self.add(y, h, self.ud)
            self.go_up(y, h).start()

        def downward():
            y = t - (p.nz - 1 - p.z)
            if h == 0:
                self.ready(y)
            self.go_down(y, h).wait_recv()
            self.add(y, h, self.ud)
            self.go_down(y, h, t == p.nz - 2).start()

        half = p.nz // 2
        goes_up = p.low & p.high & (p.z <= t)
        goes_down = p.low & p.high & (p.nz - 1 - p.z <= t)
        pl.when(goes_up & (p.z < half))(upward)
        pl.when(goes_down)(downward)
        pl.when(goes_up & (p.z >= half))(upward)

    def total(self, fn, after=None):
        p = self.p
        z = p.z
        self.ready(z)
        for h in range(CUTS):
            pl.when(p.low)(lambda: self.go_up(z, h).wait_recv())
            pl.when(p.high)(lambda: self.go_down(z, h, True).wait_recv())

            def run(low, high):
                def body(r):
                    v = self.a[z, r].astype(f32) + self.x[z, r].astype(f32)
                    if low:
                        v = v + self.ud[z, r].astype(f32)
                    if high:
                        v = v + self.ud[p.nz, r].astype(f32)
                    fn(r, v)

                each(body, h * self.size, self.size)

            pl.when(p.low & p.high)(lambda: run(True, True))
            pl.when(p.z == 0)(lambda: run(False, p.nz > 1))
            pl.when(p.z == p.nz - 1)(lambda: run(True, False))
            if after is not None:
                after(h)

    def finish(self, staged=True):
        p = self.p
        for y in range(p.nz):
            if self.part is not None:
                self.cross(y).wait_send()

            @pl.when(p.z < y)
            def _(y=y):
                for h in range(CUTS):
                    self.go_up(y, h).wait_send()

            @pl.when(p.z > y)
            def _(y=y):
                for h in range(CUTS):
                    self.go_down(y, h).wait_send()

        if self.part is None and staged:
            self.sent()

    def sent(self):
        for i in range(max(self.p.nz - 2, 0), self.p.nz):
            self.cross(self.turn(i), i % 2).wait_send()

    def all_steps(self):
        return [functools.partial(self.step, i, h) for i in range(1, self.p.nz - 1) for h in range(CUTS)]


class Gathers:
    def __init__(self, p, own, full, T, ss, rs, ls):
        n = T // CUTS
        self.all = [Gather(p, own, full, pl.ds(h * n, n), ss.at[h], rs.at[h], ls.at[h]) for h in range(CUTS)]

    def first(self, h):
        self.all[h].first()

    def step(self, t):
        for g in self.all:
            g.step(t)

    def all_steps(self):
        return [functools.partial(g.step, t) for t in range(1, self.all[0].p.nz) for g in self.all]

    def arrived(self, k):
        for g in self.all:
            g.arrived(k)

    def finish(self, arrived=False):
        for g in self.all:
            g.finish(arrived)


CUTS = 2


def interleave(first, second):
    for i in range(max(len(first), len(second))):
        if i < len(first):
            first[i]()
        if i < len(second):
            second[i]()


def strips(fn, width, step):
    def body(i, _):
        fn(pl.ds(pl.multiple_of(i * step, step), step))
        return 0

    lax.fori_loop(0, width // step, body, 0)


def interleave(first, second):
    for i in range(max(len(first), len(second))):
        if i < len(first):
            first[i]()
        if i < len(second):
            second[i]()


class Peers:
    def __init__(self, p, pick, ss, rs, keep, ls):
        self.p, self.pick, self.ss, self.rs, self.keep, self.ls = p, pick, ss, rs, keep, ls

    def copy(self, k):
        p = self.p
        to = lax.rem(p.f + k, p.nf)
        src, dst = self.pick(to)
        return remote(src, dst, self.ss.at[k], self.rs.at[k], "fsdp", to)

    def start(self):
        for k in range(1, self.p.nf):
            self.copy(k).start()
        if self.keep is not None:
            pltpu.make_async_copy(*self.keep, self.ls).start()

    def wait(self):
        for k in range(1, self.p.nf):
            self.copy(k).wait()
        if self.keep is not None:
            pltpu.make_async_copy(*self.keep, self.ls).wait()


DMA = pltpu.SemaphoreType.DMA


def gather_sems(nc):
    return [DMA((3, nc)), DMA((nc,)), DMA]


def gathers_sems(nc):
    return [DMA((CUTS, 3, nc)), DMA((CUTS, nc)), DMA((CUTS,))]


def scatter_scratch(nz, T, E):
    return [pltpu.VMEM((nz, T, E), bf16)] * 2 + [pltpu.VMEM((nz + 1, T, E), bf16)]


def params(cid):
    return pltpu.CompilerParams(collective_id=cid, has_side_effects=True, vmem_limit_bytes=62 * 1024 * 1024)


ANY = pl.BlockSpec(memory_space=pl.ANY)
VM = pl.BlockSpec(memory_space=pltpu.VMEM)


def open_kernel(
    nc, nf, tok, ids, gains, wq, wk, wv, wo, wg, wu, wd, row, ids_row, w, wm,
    qv, kv, vv, ov, gv, bigv, wl, wmv, lsem, msem,
    gss, grs, gls, iss, irs, ils, ass, ars, fss, frs, als,
):
    p = Place(nc, nf)
    T = tok.shape[0]
    R, QW = wq.shape[0], wq.shape[1] // nc
    F = wg.shape[1] // nc
    rep = nc * HD // wk.shape[1]
    small = [
        pltpu.make_async_copy(src, dst, lsem.at[i])
        for i, (src, dst) in enumerate(((wq, qv), (wk, kv), (wv, vv), (wo, ov), (gains, gv)))
    ]
    large = [pltpu.make_async_copy(src, bigv.at[i], lsem.at[5 + i]) for i, src in enumerate((wg, wu, wd))]
    for cp in small + large:
        cp.start()
    greet(p, ctx=True, fsdp=True)
    g = Gather(p, tok, row, pl.ds(0, T), gss, grs, gls)
    g.first()

    def id_copy(k):
        to = lax.rem(p.c + k, nc)
        return remote(ids, ids_row.at[p.c], iss.at[k], irs.at[k], "ctx", to)

    def block(k):
        to = lax.rem(p.c + k, nc)
        return remote(wl.at[to], w.at[p.c, p.f], ass.at[k], ars.at[k], "ctx", to)

    def onward(c, k, m):
        to = lax.rem(p.f + m, nf)
        return remote(w.at[c, p.f], w.at[c, p.f], fss.at[k, m], frs.at[k, m], "fsdp", to)

    def source(k):
        return lax.rem(p.c + nc - k, nc)

    for cp in small:
        cp.wait()
    for c in range(nc):
        h = c // rep
        at = 0
        for src, i, width in ((qv, c, QW), (kv, h, HD), (vv, h, HD), (ov, c, QW)):
            wl[c, :, pl.ds(at, width)] = src[:, i * width : (i + 1) * width].astype(bf16)
            at += width
        wl[c, :, pl.ds(at, 128)] = gv[...]
    keep_ids = pltpu.make_async_copy(ids, ids_row.at[p.c], ils)
    keep_w = pltpu.make_async_copy(wl.at[p.c], w.at[p.c, p.f], als)
    keep_w.start()
    keep_ids.start()
    for k in range(1, nc):
        block(k).start()
        id_copy(k).start()
    keep_w.wait()

    def spread(k):
        for m in range(1, nf):
            onward(source(k), k, m).start()

    spread(0)
    for i, cp in enumerate(large):
        cp.wait()

        def cast(c, _, i=i):
            wmv[c, :, pl.ds(i * F, F)] = bigv[i, :, pl.ds(pl.multiple_of(c * F, F), F)].astype(bf16)
            return 0

        lax.fori_loop(0, nc, cast, 0)
    keep_m = pltpu.make_async_copy(wmv, wm, msem)
    keep_m.start()
    for k in range(1, nc):
        block(k).wait_recv()
        spread(k)
    for t in range(1, p.nz):
        g.step(t)
    g.finish()
    keep_ids.wait()
    keep_m.wait()
    for k in range(1, nc):
        block(k).wait_send()
        id_copy(k).wait()
    for k in range(nc):
        for m in range(1, nf):
            onward(source(k), k, m).wait()


def open_call(nc, nf, tok, ids, gains, wq, wk, wv, wo, wg, wu, wd):
    T, E = tok.shape
    R = wq.shape[0]
    A = 2 * wq.shape[1] // nc + 2 * HD + 128
    M = 3 * wg.shape[1] // nc
    VMEM = pltpu.VMEM
    return pl.pallas_call(
        functools.partial(open_kernel, nc, nf),
        in_specs=[ANY] * 10,
        out_specs=[ANY] * 4,
        out_shape=[
            jax.ShapeDtypeStruct((nc, T, E), bf16),
            jax.ShapeDtypeStruct((nc,) + ids.shape, jnp.int32),
            jax.ShapeDtypeStruct((nc, nf, R, A), bf16),
            jax.ShapeDtypeStruct((nc, R, M), bf16),
        ],
        scratch_shapes=[VMEM(v.shape, f32) for v in (wq, wk, wv, wo)]
        + [VMEM((R, 128), bf16), VMEM((3,) + wg.shape, f32), VMEM((nc, R, A), bf16), VMEM((nc, R, M), bf16)]
        + [DMA((8,)), DMA]
        + gather_sems(nc)
        + [DMA((nc,)), DMA((nc,)), DMA, DMA((nc,)), DMA((nc,)), DMA((nc, nf)), DMA((nc, nf)), DMA],
        compiler_params=params(1),
        name="open_row",
    )(tok, ids, gains, wq, wk, wv, wo, wg, wu, wd)


def finish_kernel(F, QW, gm, ga, gg, gu, gd, gq, go):
    gg[...] = gm[0, :, pl.ds(0, F)].astype(f32)
    gu[...] = gm[0, :, pl.ds(F, F)].astype(f32)
    gd[...] = gm[0, :, pl.ds(2 * F, F)].astype(f32)
    gq[...] = ga[0, :, pl.ds(0, QW)].astype(f32)
    go[...] = ga[0, :, pl.ds(QW + 2 * HD, QW)].astype(f32)


def finish_call(gm, ga):
    nc, R, M = gm.shape
    A = ga.shape[2]
    F, QW = M // 3, (A - 2 * HD) // 2
    out = lambda n: pl.BlockSpec((R, n), lambda c: (0, c))
    widths = (F, F, F, QW, QW)
    return pl.pallas_call(
        functools.partial(finish_kernel, F, QW),
        grid=(nc,),
        in_specs=[pl.BlockSpec((1, R, M), lambda c: (c, 0, 0)), pl.BlockSpec((1, R, A), lambda c: (c, 0, 0))],
        out_specs=[out(n) for n in widths],
        out_shape=[jax.ShapeDtypeStruct((R, nc * n), f32) for n in widths],
        name="finish_rows",
    )(gm, ga)


def middle_kernel(nc, nf, fold, *refs):
    it = iter(refs)
    take = lambda n: [next(it) for _ in range(n)]
    oT, wo, tok, og, g, wl = take(6)
    hid, n2, dm, w = take(4)
    outs = take(3) if fold else None
    a, x, ud, stage, oblk, own, dmo, rsem = take(8)
    nss, nrs, nls, dss, drs, dls, fss, frs, fls = take(9)
    p = Place(nc, nf)
    greet(p, fsdp=True)
    T, E = tok.shape
    M = wl.shape[2]
    F, F2 = M // 3, 2 * M // 3
    R = wl.shape[1]
    S = nc * T

    def make(d, ref):
        oblk[...] = oT[:, pl.ds(pl.multiple_of(d * T, T), T)].T

        def fn(r):
            ref[:, r] = dg(oblk[...], wo[r, :], 1, 1).astype(bf16)

        strips(fn, E, 512)

    rs = Scatter(p, a, x, ud, T, rsem, make=make, stage=stage)
    dmg = Gathers(p, dmo, dm, T, dss, drs, dls)
    if fold:
        n2v, wguv, wdv, dact, dmb, out, osem, dsem, csem, wsem = take(10)
        ag = Gathers(p, None, n2v, T, nss, nrs, nls)
        low, high = wl.at[:, :, pl.ds(0, F2)], wl.at[:, :, pl.ds(F2, F)]
        last = Peers(p, lambda to: (high, wdv.at[:, p.f]), fss.at[0], frs.at[0], (high, wdv.at[:, p.f]), fls.at[0])
        firsts = Peers(p, lambda to: (low, wguv.at[:, p.f]), fss.at[1], frs.at[1], (low, wguv.at[:, p.f]), fls.at[1])
        last.start()
        firsts.start()
        saves = [
            pltpu.make_async_copy(wdv, w.at[:, :, :, pl.ds(F2, F)], wsem.at[0]),
            pltpu.make_async_copy(wguv, w.at[:, :, :, pl.ds(0, F2)], wsem.at[1]),
        ]
    else:
        ag = Gathers(p, own, n2, T, nss, nrs, nls)
        every = Peers(p, lambda to: (wl, w.at[:, p.f]), fss.at[0], frs.at[0], (wl, w.at[:, p.f]), fls.at[0])
        every.start()

    def dm_rows(r):
        dmo[r] = (RES * og[r].astype(f32)).astype(bf16)

    each(dm_rows, 0, T)
    for h in range(CUTS):
        dmg.first(h)
    rs.compute()

    def rows(r, v):
        h = tok[r].astype(f32) + RES * v
        hid[r] = h
        v = (h * lax.rsqrt(jnp.mean(h * h, axis=-1, keepdims=True) + EPS) * g[...]).astype(bf16)
        if fold:
            n2v[p.c, r] = v
        else:
            own[r] = v

    interleave(dmg.all_steps(), rs.all_steps())
    rs.total(rows, ag.first)
    dmg.finish()
    steps = [functools.partial(ag.step, t) for t in range(1, p.nz)]
    if not fold:
        for s in steps:
            s()
        ag.finish()
        rs.finish()
        every.wait()
        return

    def dm_load(k, slot):
        return pltpu.make_async_copy(dm.at[k], dmb.at[slot], dsem.at[slot])

    def back(k, _):
        slot = k % 2

        @pl.when(k + 1 < nc)
        def _():
            dm_load(k + 1, 1 - slot).start()

        dm_load(k, slot).wait()

        def fn(at):
            v = jnp.dot(dmb[slot], wdv[:, :, :, at].reshape(E, -1), preferred_element_type=f32)
            dact[pl.ds(pl.multiple_of(k * T, T), T), at] = v

        strips(fn, F, min(512, F))
        return 0

    dm_load(0, 0).start()
    last.wait()
    saves[0].start()
    lax.fori_loop(0, nc, back, 0)

    def results(k, slot):
        rows_ = pl.ds(pl.multiple_of(k * T, T), T)
        return [pltpu.make_async_copy(out.at[slot, i], outs[i].at[rows_], osem.at[slot, i]) for i in range(3)]

    def block(q, _):
        dist, sign, slot = q // 4, (q // 2) % 2, q % 2
        y = p.z + (2 * sign - 1) * dist

        @pl.when((y >= 0) & (y < nc // 2) & (dist + 1 - sign > 0))
        def _():
            k = 2 * y + p.j + slot * (1 - 2 * p.j)
            pl.when(slot == 1)(lambda: ag.arrived(k))
            pltpu.make_async_copy(n2v.at[k], n2.at[k], csem.at[k]).start()

            @pl.when(dist > 0)
            def _():
                for cp in results(k, slot):
                    cp.wait()

            def fn(at):
                up_at = pl.ds(pl.multiple_of(at.start + F, 128), at.size)
                gate = jnp.dot(n2v[k], wguv[:, :, :, at].reshape(E, -1), preferred_element_type=f32)
                up = jnp.dot(n2v[k], wguv[:, :, :, up_at].reshape(E, -1), preferred_element_type=f32)
                d = dact[pl.ds(pl.multiple_of(k * T, T), T), at]
                sg = 1.0 / (1.0 + jnp.exp(-gate))
                silu = gate * sg
                out[slot, 0, :, at] = (d * up * sg * (1.0 + gate * (1.0 - sg))).astype(bf16)
                out[slot, 1, :, at] = (d * silu).astype(bf16)
                out[slot, 2, :, at] = (silu * up).astype(bf16)

            strips(fn, F, min(STRIP, F))
            for cp in results(k, slot):
                cp.start()

        return 0

    nz = nc // 2
    for t, s in enumerate(steps, 1):
        s()
        if t == 2:
            firsts.wait()
            saves[1].start()
            lax.fori_loop(0, 8, block, 0)
    lax.fori_loop(8, 4 * nz, block, 0)
    ag.finish(True)
    rs.finish()
    for slot in range(2):
        for cp in results(0, slot):
            cp.wait()
    for cp in saves:
        cp.wait()
    for k in range(nc):
        pltpu.make_async_copy(n2v.at[k], n2.at[k], csem.at[k]).wait()


STRIP = 512


def middle_call(nc, nf, fold, oT, wo, tok, og, g, wl):
    T, E = tok.shape
    _, R, M = wl.shape
    nz = nc // 2
    F, S = M // 3, nc * T
    VMEM = pltpu.VMEM
    return pl.pallas_call(
        functools.partial(middle_kernel, nc, nf, fold),
        in_specs=[VM, VM, VM, VM, VM, ANY],
        out_specs=[VM, ANY, ANY, ANY] + [ANY] * 3 * fold,
        out_shape=[
            jax.ShapeDtypeStruct((T, E), f32),
            jax.ShapeDtypeStruct((nc, T, E), bf16),
            jax.ShapeDtypeStruct((nc, T, E), bf16),
            jax.ShapeDtypeStruct((nc, nf, R, M), bf16),
        ]
        + [jax.ShapeDtypeStruct((S, F), bf16)] * 3 * fold,
        scratch_shapes=scatter_scratch(nz, T, E)
        + [VMEM((2, T, E), bf16), VMEM((T, oT.shape[0]), bf16)]
        + [VMEM((8, 128) if fold else (T, E), bf16), VMEM((T, E), bf16), DMA((7, nz, CUTS))]
        + gathers_sems(nc)
        + gathers_sems(nc)
        + [DMA((2, nf)), DMA((2, nf)), DMA((2,))]
        + [
            VMEM((nc, T, E), bf16), VMEM((nc, nf, R, 2 * F), bf16), VMEM((nc, nf, R, F), bf16), VMEM((S, F), f32),
            VMEM((2, T, E), bf16), VMEM((2, 3, T, F), bf16), DMA((2, 3)), DMA((2,)), DMA((nc,)), DMA((2,)),
        ]
        * fold,
        compiler_params=params(2),
        name="attn_to_mlp",
    )(oT, wo, tok, og, g, wl)


EARLY, MLP_LATE = 8, True


def turn_kernel(nc, nf, fold, *refs):
    it = iter(refs)
    take = lambda n: [next(it) for _ in range(n)]
    n2, dm, dga, dup, act, wm = take(6)
    hid, og, g, dh, da = take(5)
    lay = next(it) if fold else None
    gg, gs, y, gbuf = take(4)
    mpart = next(it) if fold else None
    a, x, ud, own, rsem = take(5)
    nss, nrs, nls, fss, frs, fls = take(6)
    dguv, actv, wide, nt, go, mp, lsem, ssem = take(8)
    p = Place(nc, nf)
    nz = p.nz
    greet(p, fsdp=True)
    T, E = hid.shape
    S, F = act.shape
    F2 = 2 * F
    R = E // (nc * nf)
    B = nf * R

    def fetch(src, dst, i):
        return pltpu.make_async_copy(src, dst, lsem.at[4 + i])

    big = [
        fetch(wm.at[:, pl.ds(0, F2)], wide.at[pl.ds(0, E), pl.ds(0, F2)], 0),
        fetch(dga, dguv.at[:, pl.ds(0, F)], 1),
        fetch(dup, dguv.at[:, pl.ds(F, F)], 2),
        fetch(act, actv, 3),
    ]

    def make(d, ref):
        tok = dguv[pl.ds(pl.multiple_of(d * T, T), T), :]

        def fn(r):
            ref[:, r] = dg(tok, wide[r, pl.ds(0, F2)], 1, 1).astype(bf16)

        strips(fn, E, 512)

    rs = Scatter(p, a, x, ud, T, rsem, make=make, stage=mp)
    ag = Gathers(p, own, da, T, nss, nrs, nls)
    if fold:
        x2, ud2, wdv, msem, psem = take(5)
        ms = Scatter(p, a, x2, ud2, T, msem, part=mpart)
        big.append(fetch(wm.at[:, pl.ds(F2, F)], wdv, 4))
    for cp in big:
        cp.start()

    def spot(i):
        return pl.ds(pl.multiple_of(i * B, B), B)

    def column(b, slot):
        at = spot(b)
        return (
            pltpu.make_async_copy(n2.at[:, at], wide.at[pl.ds(0, S), spot(slot)], lsem.at[slot]),
            pltpu.make_async_copy(dm.at[:, at], wide.at[pl.ds(0, S), spot(2 + slot)], lsem.at[2 + slot]),
        )

    def keep(b, slot):
        return pltpu.make_async_copy(go.at[slot], gbuf.at[b], ssem.at[slot])

    def peer(b, k):
        to = lax.rem(p.f + k, nf)
        at = pl.ds(pl.multiple_of(to * R, R), R)
        return remote(gbuf.at[b, at], y.at[p.f, b], fss.at[k, b], frs.at[k, b], "fsdp", to)

    def terms(b, slot):
        at = pl.ds(pl.multiple_of(p.f * R, R), R)
        srcs = [gbuf.at[b, at]] + [y.at[lax.rem(p.f + k, nf), b] for k in range(1, nf)]
        return [
            pltpu.make_async_copy(src, go.at[slot, pl.ds(i * R, R)], fls.at[slot, i]) for i, src in enumerate(srcs)
        ]

    def stored(b, slot):
        return pltpu.make_async_copy(go.at[slot, pl.ds(0, R)], gs.at[b], ssem.at[slot])

    def sums(first, last):
        for b in range(first, last):
            slot = b % 2
            for k in range(1, nf):
                peer(b, k).wait()
            if b > 1:
                stored(b - 2, slot).wait()
            cps = terms(b, slot)
            for cp in cps:
                cp.start()
            for cp in cps:
                cp.wait()

            def fn(r, slot=slot):
                v = go[slot, r].astype(f32)
                for i in range(1, nf):
                    v = v + go[slot, pl.ds(r.start + i * R, CH)].astype(f32)
                go[slot, r] = v.astype(bf16)

            each(fn, 0, R)
            stored(b, slot).start()

    def send(b):
        keep(b, b % 2).wait()
        for k in range(1, nf):
            peer(b, k).start()

    def grads(b, _):
        slot = b % 2

        @pl.when(b + 1 < nc)
        def _():
            for cp in column(b + 1, 1 - slot):
                cp.start()

        now = column(b, slot)
        for at, val, base, width, cp in ((slot, dguv, 0, F2, now[0]), (2 + slot, actv, F2, F, now[1])):
            cp.wait()
            nt[...] = wide[pl.ds(0, S), spot(at)].T
            step = min(512, width)

            def dots(i, _, val=val, base=base, step=step):
                at = pl.multiple_of(i * step, step)
                v = jnp.dot(nt[...], val[:, pl.ds(at, step)], preferred_element_type=f32)
                go[slot, :, pl.ds(pl.multiple_of(base + at, step), step)] = v.astype(bf16)
                return 0

            lax.fori_loop(0, width // step, dots, 0)
        keep(b, slot).start()

        @pl.when(b > 0)
        def _():
            send(b - 1)

        return 0

    def mlp(b, _):
        slot = b % 2
        out = pltpu.make_async_copy(mp.at[slot], mpart.at[b], psem.at[slot])

        @pl.when(b > 1)
        def _():
            out.wait()

        tok = actv[pl.ds(pl.multiple_of(b * T, T), T), :]

        def dots(i, _):
            at = pl.ds(pl.multiple_of(i * 512, 512), 512)
            mp[slot, :, at] = dg(tok, wdv[at, :], 1, 1).astype(bf16)
            return 0

        lax.fori_loop(0, E // 512, dots, 0)
        out.start()
        return 0

    gg[...] = jnp.zeros_like(gg)
    for cp in big[:3]:
        cp.wait()
    rs.compute()
    for cp in column(0, 0):
        cp.start()
    for cp in big[3:]:
        cp.wait()
    steps = rs.all_steps()
    early = EARLY * nc // 8 if fold else nc
    bounds = [early * i // (len(steps) + 1) for i in range(len(steps) + 2)]
    for i in range(len(steps) + 1):
        lax.fori_loop(bounds[i], bounds[i + 1], grads, 0)
        if i < len(steps):
            steps[i]()
    if fold:
        rs.sent()

    def mlp_terms():
        if fold:
            lax.fori_loop(0, nc, mlp, 0)
            for slot in range(2):
                pltpu.make_async_copy(mp.at[slot], mpart.at[slot], psem.at[slot]).wait()
            ms.begin(load=False)

    def rows(r, dn):
        h = hid[r]
        inv = lax.rsqrt(jnp.mean(h * h, axis=-1, keepdims=True) + EPS)
        xn = h * inv
        e = dn * g[...]
        v = og[r].astype(f32) + inv * (e - xn * jnp.mean(e * xn, axis=-1, keepdims=True))
        dh[r] = v
        own[r] = (RES * v).astype(bf16)
        gg[...] += jnp.sum((xn * dn).reshape(CH // 8, 8, E), axis=0)

    if not MLP_LATE:
        mlp_terms()
    rs.total(rows, ag.first)
    if MLP_LATE:
        mlp_terms()
    rs.finish(not fold)
    if fold:
        ms.begin(cross=False)
        ms.edges()
    more = ms.all_steps() if fold else []
    made, done = early, 0
    late = ag.all_steps()
    for i, s in enumerate(late):
        upto = min(nc, made + max(1, nc // 8))
        lax.fori_loop(made, upto, grads, 0)
        if made < nc and upto == nc:
            send(nc - 1)
        made = upto
        s()
        if i < len(more):
            more[i]()
    if early == nc:
        send(nc - 1)
    sums(0, nc // 2)
    done = nc // 2
    if fold:

        def out(r, v):
            lay[r] = (hid[r] + RES * v).astype(bf16)

        ms.total(out)
        ms.finish()
    ag.finish()
    sums(done, nc)
    for b in range(nc - 2, nc):
        stored(b, b % 2).wait()


def turn_call(nc, nf, fold, n2, dm, dga, dup, act, wm, hid, og, g):
    T, E = hid.shape
    S, F = act.shape
    F2, M = 2 * F, 3 * F
    R = E // (nc * nf)
    B = nf * R
    nz = nc // 2
    VMEM = pltpu.VMEM
    return pl.pallas_call(
        functools.partial(turn_kernel, nc, nf, fold),
        in_specs=[ANY] * 6 + [VM, VM, VM],
        out_specs=[VM, ANY] + [VM] * fold + [VM, ANY, ANY, ANY] + [ANY] * fold,
        out_shape=[jax.ShapeDtypeStruct((T, E), f32), jax.ShapeDtypeStruct((nc, T, E), bf16)]
        + [jax.ShapeDtypeStruct((T, E), bf16)] * fold
        + [
            jax.ShapeDtypeStruct((8, E), f32),
            jax.ShapeDtypeStruct((nc, R, M), bf16),
            jax.ShapeDtypeStruct((nf, nc, R, M), bf16),
            jax.ShapeDtypeStruct((nc, B, M), bf16),
        ]
        + [jax.ShapeDtypeStruct((nc, T, E), bf16)] * fold,
        scratch_shapes=scatter_scratch(nz, T, E)
        + [VMEM((T, E), bf16), DMA((7, nz, CUTS))]
        + gathers_sems(nc)
        + [DMA((nf, nc)), DMA((nf, nc)), DMA((2, nf))]
        + [VMEM((S, F2), bf16), VMEM((S, F), bf16), VMEM((max(E, S), max(F2, 4 * B)), bf16)]
        + [VMEM((B, S), bf16), VMEM((2, B, M), bf16), VMEM((2, T, E), bf16), DMA((9,)), DMA((2,))]
        + [VMEM((nz, T, E), bf16), VMEM((nz + 1, T, E), bf16), VMEM((E, F), bf16), DMA((7, nz, CUTS)), DMA((2,))] * fold,
        compiler_params=params(3),
        name="mlp_to_attn",
    )(n2, dm, dga, dup, act, wm, hid, og, g)


def close_kernel(
    nc, nf, dqkv, wq, oT, n1, da, tok, dh, g, ggm, dx, gout, ggout,
    a, x, ud, stage, dblk, wqv, big, gt, gb, y, zb, gg, gbuf, gsum, gfin, rsem, lsem,
    fss, frs, fls, css, crs, cls, s1, r1, s2, r2, l2,
):
    p = Place(nc, nf)
    greet(p, ctx=True, fsdp=True)
    T, E = tok.shape
    Q = dqkv.shape[0]
    H = oT.shape[0]
    R = E // (nc * nf)
    B = nf * R
    weights = pltpu.make_async_copy(wq.at[:, pl.ds(0, Q)], wqv, lsem.at[4])
    weights.start()

    def column(b, slot):
        at = pl.ds(pl.multiple_of(b * B, B), B)
        return (
            pltpu.make_async_copy(n1.at[:, at], big.at[0, slot], lsem.at[slot]),
            pltpu.make_async_copy(da.at[:, at], big.at[1, slot], lsem.at[2 + slot]),
        )

    for cp in column(0, 0):
        cp.start()

    def make(d, ref):
        dblk[...] = dqkv[:, pl.ds(pl.multiple_of(d * T, T), T)].T

        def fn(r):
            ref[:, r] = dg(dblk[...], wqv[r, :], 1, 1).astype(bf16)

        strips(fn, E, 512)

    rs = Scatter(p, a, x, ud, T, rsem, make=make, stage=stage)

    def pieces(to):
        return gb.at[:, pl.ds(pl.multiple_of(to * R, R), R)], y.at[p.f]

    peers = Peers(p, pieces, fss, frs, pieces(p.f), fls)
    gg[...] = jnp.zeros_like(gg)

    def piece(k):
        to = lax.rem(p.c + k, nc)
        return remote(zb.at[to], gout.at[p.c], css.at[k], crs.at[k], "ctx", to)

    mine = pltpu.make_async_copy(zb.at[p.c], gout.at[p.c], cls)

    def grads():
        peers.wait()
        for c in range(nc):

            def fn(r):
                v = y[0, c, r].astype(f32)
                for m in range(1, nf):
                    v = v + y[m, c, r].astype(f32)
                zb[c, r] = v.astype(bf16)

            each(fn, 0, R)
        for k in range(1, nc):
            piece(k).start()
        mine.start()

    def rows(r, dn):
        t = tok[r].astype(f32)
        inv = lax.rsqrt(jnp.mean(t * t, axis=-1, keepdims=True) + EPS)
        xn = t * inv
        e = dn * g[...]
        dx[r] = dh[r] + inv * (e - xn * jnp.mean(e * xn, axis=-1, keepdims=True))
        gg[...] += jnp.sum((xn * dn).reshape(CH // 8, 8, E), axis=0)

    weights.wait()
    rs.compute()

    def products(b, _):
        slot = b % 2

        @pl.when(b + 1 < nc)
        def _():
            for cp in column(b + 1, 1 - slot):
                cp.start()

        for cp in column(b, slot):
            cp.wait()
        gt[pl.ds(0, Q), :] = dg(dqkv[...], big[0, slot], 1, 0)
        gt[pl.ds(Q, H), :] = dg(oT[...], big[1, slot], 1, 0)
        gb[b] = gt[...].T.astype(bf16)
        return 0

    lax.fori_loop(0, nc, products, 0)
    peers.start()
    for s in rs.all_steps():
        s()
    grads()
    rs.total(rows)

    groups = E // 128
    sa = jnp.sum(gg[...], axis=0, keepdims=True)
    sm = jnp.sum(ggm[...], axis=0, keepdims=True)
    for i in range(groups):
        gbuf[p.f, i] = jnp.concatenate(
            [sa[:, i * 128 : (i + 1) * 128], sm[:, i * 128 : (i + 1) * 128], jnp.zeros((6, 128), f32)], axis=0
        )

    def over(k):
        to = lax.rem(p.f + k, nf)
        return remote(gbuf.at[p.f], gbuf.at[p.f], s1.at[k], r1.at[k], "fsdp", to)

    for k in range(1, nf):
        over(k).start()
    for k in range(1, nf):
        over(k).wait()
    v = gbuf[0]
    for m in range(1, nf):
        v = v + gbuf[m]
    gsum[...] = v
    per = 128 // R

    def along(k):
        to = lax.rem(p.c + k, nc)
        return remote(gsum.at[(to * nf + p.f) // per], gfin.at[p.c], s2.at[k], r2.at[k], "ctx", to)

    for k in range(1, nc):
        along(k).start()
    own = pltpu.make_async_copy(gsum.at[(p.c * nf + p.f) // per], gfin.at[p.c], l2)
    own.start()
    own.wait()
    for k in range(1, nc):
        along(k).wait()
    t = gfin[0]
    for m in range(1, nc):
        t = t + gfin[m]
    ggout[...] = t
    for k in range(1, nc):
        piece(k).wait()
    mine.wait()
    rs.finish()


def close_call(nc, nf, dqkv, wq, oT, n1, da, tok, dh, g, ggm):
    T, E = tok.shape
    S = n1.shape[0]
    Q, H = dqkv.shape[0], oT.shape[0]
    A = Q + H
    R = E // (nc * nf)
    nz = nc // 2
    VMEM = pltpu.VMEM
    return pl.pallas_call(
        functools.partial(close_kernel, nc, nf),
        in_specs=[VM, ANY, VM, ANY, ANY, VM, VM, VM, VM],
        out_specs=[VM, ANY, VM],
        out_shape=[
            jax.ShapeDtypeStruct((T, E), f32),
            jax.ShapeDtypeStruct((nc, R, A), bf16),
            jax.ShapeDtypeStruct((8, 128), f32),
        ],
        scratch_shapes=scatter_scratch(nz, T, E)
        + [VMEM((2, T, E), bf16), VMEM((T, Q), bf16), VMEM((E, Q), bf16), VMEM((2, 2, S, nf * R), bf16)]
        + [VMEM((A, nf * R), f32), VMEM((nc, nf * R, A), bf16)]
        + [
            VMEM((nf, nc, R, A), bf16),
            VMEM((nc, R, A), bf16),
            VMEM((8, E), f32),
            VMEM((nf, E // 128, 8, 128), f32),
            VMEM((E // 128, 8, 128), f32),
            VMEM((nc, 8, 128), f32),
            DMA((7, nz, CUTS)),
            DMA((5,)),
        ]
        + [DMA((nf,)), DMA((nf,)), DMA, DMA((nc,)), DMA((nc,)), DMA]
        + [DMA((nf,)), DMA((nf,)), DMA((nc,)), DMA((nc,)), DMA],
        compiler_params=params(4),
        name="close_row",
    )(dqkv, wq, oT, n1, da, tok, dh, g, ggm)


def rms(v):
    inv = lax.rsqrt(jnp.mean(v * v, axis=-1, keepdims=True) + EPS)
    return v * inv, inv


def rms_back(x, inv, e):
    return inv * (e - x * jnp.mean(e * x, axis=-1, keepdims=True))


def rotate(v, cos, sin, sign):
    heads = v.shape[0] // HD
    v = v.reshape(heads, 2, HD // 2, v.shape[1])
    a, b = v[:, 0], v[:, 1]
    s = sign * sin
    return jnp.stack([a * cos - b * s, b * cos + a * s], axis=1).reshape(heads * HD, -1)


def local(
    tokens, seq_ids, positions, block_ids, gain_attn, w_query, w_key, w_value, w_out,
    gain_mlp, w_gate, w_up, w_down, out_grad,
):
    nc = lax.axis_size("ctx")
    nf = lax.axis_size("fsdp")
    nz = nc // 2
    T, E = tokens.shape[1:]
    R = w_query.shape[0]
    S = T * nc
    FFL = w_gate.shape[1] // nc
    nh = QUERY_HEADS // nc
    rep = nc // KEY_VALUE_HEADS
    QW = nh * HD
    KO, VO, OO, GO = QW, QW + HD, QW + 2 * HD, 2 * QW + 2 * HD
    tok, og = tokens[0], out_grad[0]

    def exchange(w):
        return lax.all_to_all(w, "ctx", 0, 0, tiled=True)


    gains = jnp.pad(jnp.stack([gain_attn, gain_mlp], axis=1).astype(bf16), ((0, 0), (0, 126)))
    ids = jnp.pad(jnp.concatenate([seq_ids, positions, block_ids], axis=0), ((0, 5), (0, 0)))
    row_tok, ids, wa, wm = open_call(
        nc, nf, tok, ids, gains, w_query, w_key, w_value, w_out, w_gate, w_up, w_down
    )
    wm = exchange(wm)
    wa = wa.reshape(E, -1)
    g_attn, g_mlp = wa[:, GO].astype(f32)[None], wa[:, GO + 1].astype(f32)[None]

    seq, pos, blk = (ids[:, i].reshape(S) for i in range(3))
    place = jnp.arange(S, dtype=jnp.int32)
    cut = jnp.sum((seq == 0).astype(jnp.int32))
    first = place - pos
    last = jnp.minimum(first + BLOCK * (blk + 1), jnp.where(seq == 0, cut, S))
    st, en = first[None], last[None]
    freq = ROPE_BASE ** (-(jnp.arange(HD // 2, dtype=f32) * 2.0) / HD)
    ang = freq[:, None] * pos.astype(f32)[None, :]
    cos, sin = jnp.cos(ang), jnp.sin(ang)

    x1r, _ = rms(row_tok.reshape(S, E).astype(f32))
    n1 = (x1r * g_attn).astype(bf16)
    w_qkv, w_o = wa[:, :OO], wa[:, OO:GO]
    qkv = dg(w_qkv, n1, 0, 1)
    qkT = rotate(qkv[:VO], cos, sin, 1.0).astype(bf16)
    qT, kT = qkT[:QW], qkT[QW:]
    vT = qkv[VO:].astype(bf16)
    k, v = kT.T, vT.T
    oT, oTb, lse = attn_fwd(qT, k, vT, st, en)

    middle = (oTb, w_o, tok, og, g_mlp, wm)
    if nz <= 4:
        hidden, n2, dm, wm, d_gate, d_up, act = middle_call(nc, nf, True, *middle)
        n2, dm, wm = n2.reshape(S, E), dm.reshape(S, E), wm.reshape(E, -1)
    else:
        hidden, n2, dm, wm = middle_call(nc, nf, False, *middle)
        n2, dm, wm = n2.reshape(S, E), dm.reshape(S, E), wm.reshape(E, -1)
        w_d = wm[:, 2 * FFL :]
        gu = dg(n2, wm[:, : 2 * FFL], 1, 0)
        gate, up = gu[:, :FFL], gu[:, FFL:]
        sg = jax.nn.sigmoid(gate)
        act = (gate * sg * up).astype(bf16)
        d_act = dg(dm, w_d, 1, 0)
        d_gate = (d_act * up * sg * (1.0 + gate * (1.0 - sg))).astype(bf16)
        d_up = (d_act * gate * sg).astype(bf16)
    turn = (n2, dm, d_gate, d_up, act, wm, hidden, og, g_mlp)
    if nz <= 4:
        dh, da, layer_out, ggm, gm = turn_call(nc, nf, True, *turn)[:5]
    else:
        dh, da, ggm, gm = turn_call(nc, nf, False, *turn)[:4]
        mlp = dg(act, w_d, 1, 1).astype(bf16)
        mlp = lax.psum_scatter(mlp, "ctx", scatter_dimension=0, tiled=True)
        layer_out = (hidden + RES * mlp.astype(f32)).astype(bf16)
    da = da.reshape(S, E)
    gm = exchange(gm)

    dqkv = attn_bwd(qT, da, w_o.T, oT, lse, st, en, cos, sin, k, kT, v)
    input_grad, ga, gains = close_call(nc, nf, dqkv, wa, oTb, n1, da, tok, dh, g_attn, ggm)
    at = lax.rem((lax.axis_index("ctx") * nf + lax.axis_index("fsdp")) * R, 128)
    gains = lax.dynamic_slice_in_dim(gains, at, R, 1)

    def kv_rows(g):
        g = g.astype(f32).reshape(KEY_VALUE_HEADS, rep, R, HD)
        return jnp.transpose(jnp.sum(g, axis=1), (1, 0, 2)).reshape(R, -1)

    grads = finish_call(gm, ga)
    return (
        layer_out[None],
        input_grad[None],
        gains[0],
        grads[3],
        kv_rows(ga[:, :, KO:VO]),
        kv_rows(ga[:, :, VO:OO]),
        grads[4],
        gains[1],
        *grads[:3],
    )


def solution(mesh):
    w1, w2 = P(("ctx", "fsdp")), P(("ctx", "fsdp"), None)
    act, ids = P("fsdp", "ctx", None), P("fsdp", "ctx")
    return jax.shard_map(
        local,
        mesh=mesh,
        in_specs=(act, ids, ids, ids, w1, w2, w2, w2, w2, w1, w2, w2, w2, act),
        out_specs=(act, act, w1, w2, w2, w2, w2, w1, w2, w2, w2),
        check_vma=False,
    )
```

```python
import functools

import jax
import jax.numpy as jnp
from jax import lax
from jax.experimental import pallas as pl
from jax.experimental.pallas import tpu as pltpu
from jax.sharding import PartitionSpec as P

QUERY_HEADS = 32
KEY_VALUE_HEADS = 8
HD = 64
BLOCK = 256
EPS = 1e-05
ROPE_BASE = 10000000.0
SCALE = 0.015625
RES = 0.22
NEG = -1e30
bf16 = jnp.bfloat16
f32 = jnp.float32


def dg(a, b, ca, cb):
    return lax.dot_general(a, b, (((ca,), (cb,)), ((), ())), preferred_element_type=f32)


def lanes(v, heads):
    return jnp.concatenate([v[h * HD : (h + 1) * HD, :] for h in range(heads)], axis=1)


def turned_back(v, cos, sin):
    half = HD // 2
    out = []
    for h in range(v.shape[0] // HD):
        a, b = v[h * HD : h * HD + half, :], v[h * HD + half : (h + 1) * HD, :]
        out += [a * cos + b * sin, b * cos - a * sin]
    return jnp.concatenate(out, axis=0)


def key_blocks(st, en, tk):
    return jnp.min(st) // tk, (jnp.max(en) + tk - 1) // tk


def attn_fwd_kernel(nh, tq, tk, q_ref, k_ref, v_ref, st_ref, en_ref, o_ref, ob_ref, l_ref, a_ref):
    lo, hi = key_blocks(st_ref[...], en_ref[...], tk)
    q = lanes(q_ref[...] * jnp.asarray(SCALE, bf16), nh)
    st = jnp.concatenate([st_ref[...]] * nh, axis=1)
    en = jnp.concatenate([en_ref[...]] * nh, axis=1)
    W = nh * tq
    a_ref[...] = jnp.zeros_like(a_ref)

    def body(j, c):
        m, l = c
        off = pl.multiple_of(j * tk, tk)
        jj = off + lax.broadcasted_iota(jnp.int32, (tk, W), 0)
        s = dg(k_ref[pl.ds(off, tk), :], q, 1, 0)
        s = jnp.where((jj >= st) & (jj < en), s, NEG)
        mn = jnp.maximum(m, jnp.max(s, axis=0, keepdims=True))
        p = jnp.exp(s - mn)
        sh = jnp.exp(m - mn)
        l = l * sh + jnp.sum(p, axis=0, keepdims=True)
        a_ref[...] = a_ref[...] * sh + dg(v_ref[:, pl.ds(off, tk)], p.astype(bf16), 1, 0)
        return mn, l

    m, l = lax.fori_loop(lo, hi, body, (jnp.full((1, W), 0.1 * NEG, f32), jnp.zeros((1, W), f32)))
    o = a_ref[...] / l
    ls = m + jnp.log(l)
    for h in range(nh):
        oh = o[:, h * tq : (h + 1) * tq]
        o_ref[h * HD : (h + 1) * HD, :] = oh
        ob_ref[h * HD : (h + 1) * HD, :] = oh.astype(bf16)
        l_ref[h : h + 1, :] = ls[:, h * tq : (h + 1) * tq]


def attn_fwd(qT, k, vT, st, en, tq=256, tk=256):
    n, S = qT.shape
    nh = n // HD
    blk = lambda r: pl.BlockSpec((r, tq), lambda i: (0, i))
    full = lambda s: pl.BlockSpec(s, lambda i: (0, 0))
    return pl.pallas_call(
        functools.partial(attn_fwd_kernel, nh, tq, tk),
        grid=(S // tq,),
        in_specs=[blk(n), full((S, HD)), full((HD, S)), blk(1), blk(1)],
        out_specs=[blk(n), blk(n), blk(nh)],
        out_shape=[
            jax.ShapeDtypeStruct((n, S), f32),
            jax.ShapeDtypeStruct((n, S), bf16),
            jax.ShapeDtypeStruct((nh, S), f32),
        ],
        scratch_shapes=[pltpu.VMEM((HD, nh * tq), f32)],
        cost_estimate=pl.CostEstimate(
            flops=2 * S * S * n, bytes_accessed=8 * n * S, transcendentals=S * S * nh // 2
        ),
        name="attn_fwd",
    )(qT, k, vT, st, en)


def attn_bwd_kernel(
    nh, tq, tk, q_ref, da_ref, wo_ref, o_ref, lse_ref, st_ref, en_ref, cos_ref, sin_ref, k_ref, kT_ref, v_ref,
    out_ref, dk_ref, dv_ref, acc,
):
    i = pl.program_id(0)
    n = nh * HD

    @pl.when(i == 0)
    def _():
        dk_ref[...] = jnp.zeros_like(dk_ref)
        dv_ref[...] = jnp.zeros_like(dv_ref)

    here = pl.ds(pl.multiple_of(i * tq, tq), tq)
    lo, hi = key_blocks(st_ref[...], en_ref[...], tk)
    q = lanes(q_ref[...] * jnp.asarray(SCALE, bf16), nh)
    do = lanes(dg(wo_ref[...], da_ref[...], 1, 1).astype(bf16), nh)
    o = lanes(o_ref[...], nh)
    dl = jnp.sum(do.astype(f32) * o, axis=0, keepdims=True)
    ls = jnp.concatenate([lse_ref[h : h + 1, :] for h in range(nh)], axis=1)
    st = jnp.concatenate([st_ref[...]] * nh, axis=1)
    en = jnp.concatenate([en_ref[...]] * nh, axis=1)
    acc[...] = jnp.zeros_like(acc)

    def body(j, _):
        off = pl.multiple_of(j * tk, tk)
        at = pl.ds(off, tk)
        jj = off + lax.broadcasted_iota(jnp.int32, (tk, nh * tq), 0)
        s = dg(k_ref[at, :], q, 1, 0)
        dp = dg(v_ref[at, :], do, 1, 0)
        p = jnp.exp(jnp.where((jj >= st) & (jj < en), s - ls, NEG))
        ds = (p * (dp - dl)).astype(bf16)
        acc[...] += dg(kT_ref[:, at], ds, 1, 0)
        dk_ref[:, at] += dg(q, ds, 1, 1)
        dv_ref[:, at] += dg(do, p.astype(bf16), 1, 1)
        return 0

    lax.fori_loop(lo, hi, body, 0)
    dq = jnp.concatenate([acc[:, h * tq : (h + 1) * tq] for h in range(nh)], axis=0) * SCALE
    out_ref[pl.ds(0, n), here] = turned_back(dq, cos_ref[:, here], sin_ref[:, here]).astype(bf16)

    @pl.when(i == pl.num_programs(0) - 1)
    def _():
        out_ref[pl.ds(n, HD), :] = turned_back(dk_ref[...], cos_ref[...], sin_ref[...]).astype(bf16)
        out_ref[pl.ds(n + HD, HD), :] = dv_ref[...].astype(bf16)


def attn_bwd(qT, da, woT, oT, lse, st, en, cos, sin, k, kT, v, tq=256, tk=256):
    n, S = qT.shape
    E = da.shape[1]
    nh = n // HD
    blk = lambda r: pl.BlockSpec((r, tq), lambda i: (0, i))
    full = lambda s: pl.BlockSpec(s, lambda i: (0, 0))
    return pl.pallas_call(
        functools.partial(attn_bwd_kernel, nh, tq, tk),
        grid=(S // tq,),
        in_specs=[
            blk(n), pl.BlockSpec((tq, E), lambda i: (i, 0)), full((n, E)), blk(n), blk(nh), blk(1), blk(1),
            full((HD // 2, S)), full((HD // 2, S)), full((S, HD)), full((HD, S)), full((S, HD)),
        ],
        out_specs=full((n + 2 * HD, S)),
        out_shape=jax.ShapeDtypeStruct((n + 2 * HD, S), bf16),
        scratch_shapes=[pltpu.VMEM((HD, S), f32), pltpu.VMEM((HD, S), f32), pltpu.VMEM((HD, nh * tq), f32)],
        cost_estimate=pl.CostEstimate(
            flops=5 * S * S * n, bytes_accessed=10 * n * S, transcendentals=S * S * nh // 2
        ),
        name="attn_bwd",
    )(qT, da, woT, oT, lse, st, en, cos, sin, k, kT, v)


MESH = pl.DeviceIdType.MESH
CH = 16


class Place:
    def __init__(self, nc, nf):
        self.nc, self.nf, self.nz = nc, nf, nc // 2
        self.c = lax.axis_index("ctx")
        self.f = lax.axis_index("fsdp")
        self.z = self.c // 2
        self.j = self.c % 2
        self.sib = self.z * 2 + (1 - self.j)
        self.low = self.z > 0
        self.high = self.z < self.nz - 1


def remote(src, dst, ss, rs, axis, idx):
    return pltpu.make_async_remote_copy(
        src_ref=src, dst_ref=dst, send_sem=ss, recv_sem=rs, device_id={axis: idx}, device_id_type=MESH
    )


def greet(p, line=True, ctx=False, fsdp=False):
    sem = pltpu.get_barrier_semaphore()
    count = 0

    def tell(axis, idx):
        pl.semaphore_signal(sem, inc=1, device_id={axis: idx}, device_id_type=MESH)

    if ctx:
        for k in range(1, p.nc):
            tell("ctx", lax.rem(p.c + k, p.nc))
        count = p.nc - 1
    elif line:
        tell("ctx", p.sib)

        @pl.when(p.low)
        def _():
            tell("ctx", p.c - 2)

        @pl.when(p.high)
        def _():
            tell("ctx", p.c + 2)

        count = 1 + p.low.astype(jnp.int32) + p.high.astype(jnp.int32)
    if fsdp:
        for k in range(1, p.nf):
            tell("fsdp", lax.rem(p.f + k, p.nf))
        count = count + p.nf - 1
    pl.semaphore_wait(sem, count)


def each(fn, start, size, step=CH):
    def body(r, _):
        fn(pl.ds(pl.multiple_of(start + r * step, step), step))
        return 0

    lax.fori_loop(0, size // step, body, 0)


class Gather:
    def __init__(self, p, own, full, rows, ss, rs, ls):
        self.p, self.own, self.full, self.rows, self.ss, self.rs, self.ls = p, own, full, rows, ss, rs, ls

    def slot(self, k):
        return self.full.at[k, self.rows]

    def copy(self, way, k, to, src=None):
        return remote(self.slot(k) if src is None else src, self.slot(k), self.ss.at[way, k], self.rs.at[k], "ctx", to)

    def first(self):
        p = self.p
        src = None if self.own is None else self.own.at[self.rows]

        @pl.when(p.high)
        def _():
            self.copy(0, p.c, p.c + 2, src).start()

        @pl.when(p.low)
        def _():
            self.copy(1, p.c, p.c - 2, src).start()

        self.copy(2, p.c, p.sib, src).start()
        if src is not None:
            pltpu.make_async_copy(src, self.slot(p.c), self.ls).start()

    def step(self, t):
        p = self.p

        @pl.when(p.z - t >= 0)
        def _():
            k = p.c - 2 * t
            self.copy(2, k, p.sib).wait_recv()

            @pl.when(p.high)
            def _():
                self.copy(0, k, p.c + 2).start()

            self.copy(2, k, p.sib).start()

        @pl.when(p.z + t < p.nz)
        def _():
            k = p.c + 2 * t
            self.copy(2, k, p.sib).wait_recv()

            @pl.when(p.low)
            def _():
                self.copy(1, k, p.c - 2).start()

            self.copy(2, k, p.sib).start()

    def arrived(self, k):
        self.copy(2, k, self.p.sib).wait_recv()

    def finish(self, arrived=False):
        p = self.p
        if not arrived:
            for y in range(p.nz):
                self.arrived(2 * y + 1 - p.j)
        for y in range(p.nz):
            k = 2 * y + p.j
            self.copy(2, k, p.sib).wait_send()

            @pl.when(p.high & (y <= p.z))
            def _(k=k):
                self.copy(0, k, p.c + 2).wait_send()

            @pl.when(p.low & (y >= p.z))
            def _(k=k):
                self.copy(1, k, p.c - 2).wait_send()

        if self.own is not None:
            pltpu.make_async_copy(self.own.at[self.rows], self.slot(p.c), self.ls).wait()

    def all_steps(self):
        return [self.first] + [functools.partial(self.step, t) for t in range(1, self.p.nz)]


class Scatter:
    def __init__(self, p, a, x, ud, T, sems, part=None, make=None, stage=None):
        self.p, self.a, self.x, self.ud, self.T, self.sems = p, a, x, ud, T, sems
        self.part, self.make, self.stage = part, make, stage
        self.size = T // CUTS

    def cross(self, y, slot=0):
        p = self.p
        src = self.part.at[2 * y + 1 - p.j] if self.part is not None else self.stage.at[slot]
        return remote(src, self.x.at[y], self.sems.at[0, y, 0], self.sems.at[1, y, 0], "ctx", p.sib)

    def load(self, y):
        return pltpu.make_async_copy(self.part.at[2 * y + self.p.j], self.a.at[y], self.sems.at[2, y, 0])

    def go_up(self, y, h):
        at = pl.ds(h * self.size, self.size)
        ss, rs = self.sems.at[3, y, h], self.sems.at[4, y, h]
        return remote(self.a.at[y, at], self.ud.at[y, at], ss, rs, "ctx", self.p.c + 2)

    def go_down(self, y, h, last=False):
        at = pl.ds(h * self.size, self.size)
        ss, rs = self.sems.at[5, y, h], self.sems.at[6, y, h]
        return remote(self.a.at[y, at], self.ud.at[self.p.nz if last else y, at], ss, rs, "ctx", self.p.c - 2)

    def begin(self, cross=True, load=True):
        nz = self.p.nz
        order = []
        for i in range(nz):
            order += [y for y in (nz - 1 - i, i) if y not in order]
        for y in order:
            if cross:
                self.cross(y).start()
            if load:
                self.load(y).start()

    def turn(self, i):
        p = self.p
        upper = p.z // (p.nz // 2)
        return upper * i + (1 - upper) * (p.nz - 1 - i)

    def compute(self):
        p = self.p

        def body(i, _):
            y, slot = self.turn(i), i % 2

            @pl.when(i > 1)
            def _():
                self.cross(self.turn(i - 2), slot).wait_send()

            self.make(2 * y + 1 - p.j, self.stage.at[slot])
            self.cross(y, slot).start()
            self.make(2 * y + p.j, self.a.at[y])
            inner = i < p.nz - 1
            pl.when((p.z == 0) & inner)(functools.partial(self.edge, y, True, False))
            pl.when((p.z == p.nz - 1) & (i < p.nz - 2))(functools.partial(self.edge, y, False, False))
            pl.when((p.z == p.nz - 1) & (i == p.nz - 2))(functools.partial(self.edge, y, False, True))
            return 0

        lax.fori_loop(0, p.nz, body, 0)

    def edge(self, y, up, last):
        self.ready(y)
        for h in range(CUTS):
            self.add(y, h, None)
            if up:
                self.go_up(y, h).start()
            else:
                self.go_down(y, h, last).start()

    def ready(self, y):
        if self.part is not None:
            self.load(y).wait()
        self.cross(y).wait_recv()

    def add(self, y, h, extra):
        def fn(r):
            v = self.a[y, r].astype(f32) + self.x[y, r].astype(f32)
            if extra is not None:
                v = v + extra[y, r].astype(f32)
            self.a[y, r] = v.astype(bf16)

        each(fn, h * self.size, self.size)

    def edges(self):
        p = self.p

        @pl.when(p.z == 0)
        def _():
            for y in range(p.nz - 1, 0, -1):
                self.edge(y, True, False)

        @pl.when(p.z == p.nz - 1)
        def _():
            for y in range(p.nz - 1):
                self.edge(y, False, y == p.nz - 2)

    def step(self, t, h):
        p = self.p

        def upward():
            y = p.nz - 1 - t + p.z
            if h == 0:
                self.ready(y)
            self.go_up(y, h).wait_recv()
            self.add(y, h, self.ud)
            self.go_up(y, h).start()

        def downward():
            y = t - (p.nz - 1 - p.z)
            if h == 0:
                self.ready(y)
            self.go_down(y, h).wait_recv()
            self.add(y, h, self.ud)
            self.go_down(y, h, t == p.nz - 2).start()

        half = p.nz // 2
        goes_up = p.low & p.high & (p.z <= t)
        goes_down = p.low & p.high & (p.nz - 1 - p.z <= t)
        pl.when(goes_up & (p.z < half))(upward)
        pl.when(goes_down)(downward)
        pl.when(goes_up & (p.z >= half))(upward)

    def total(self, fn, after=None):
        p = self.p
        z = p.z
        self.ready(z)
        for h in range(CUTS):
            pl.when(p.low)(lambda: self.go_up(z, h).wait_recv())
            pl.when(p.high)(lambda: self.go_down(z, h, True).wait_recv())

            def run(low, high):
                def body(r):
                    v = self.a[z, r].astype(f32) + self.x[z, r].astype(f32)
                    if low:
                        v = v + self.ud[z, r].astype(f32)
                    if high:
                        v = v + self.ud[p.nz, r].astype(f32)
                    fn(r, v)

                each(body, h * self.size, self.size)

            pl.when(p.low & p.high)(lambda: run(True, True))
            pl.when(p.z == 0)(lambda: run(False, p.nz > 1))
            pl.when(p.z == p.nz - 1)(lambda: run(True, False))
            if after is not None:
                after(h)

    def finish(self, staged=True):
        p = self.p
        for y in range(p.nz):
            if self.part is not None:
                self.cross(y).wait_send()

            @pl.when(p.z < y)
            def _(y=y):
                for h in range(CUTS):
                    self.go_up(y, h).wait_send()

            @pl.when(p.z > y)
            def _(y=y):
                for h in range(CUTS):
                    self.go_down(y, h).wait_send()

        if self.part is None and staged:
            self.sent()

    def sent(self):
        for i in range(max(self.p.nz - 2, 0), self.p.nz):
            self.cross(self.turn(i), i % 2).wait_send()

    def all_steps(self):
        return [functools.partial(self.step, i, h) for i in range(1, self.p.nz - 1) for h in range(CUTS)]


class Gathers:
    def __init__(self, p, own, full, T, ss, rs, ls):
        n = T // CUTS
        self.all = [Gather(p, own, full, pl.ds(h * n, n), ss.at[h], rs.at[h], ls.at[h]) for h in range(CUTS)]

    def first(self, h):
        self.all[h].first()

    def step(self, t):
        for g in self.all:
            g.step(t)

    def all_steps(self):
        return [functools.partial(g.step, t) for t in range(1, self.all[0].p.nz) for g in self.all]

    def arrived(self, k):
        for g in self.all:
            g.arrived(k)

    def finish(self, arrived=False):
        for g in self.all:
            g.finish(arrived)


CUTS = 2


def interleave(first, second):
    for i in range(max(len(first), len(second))):
        if i < len(first):
            first[i]()
        if i < len(second):
            second[i]()


def strips(fn, width, step):
    def body(i, _):
        fn(pl.ds(pl.multiple_of(i * step, step), step))
        return 0

    lax.fori_loop(0, width // step, body, 0)


def interleave(first, second):
    for i in range(max(len(first), len(second))):
        if i < len(first):
            first[i]()
        if i < len(second):
            second[i]()


class Peers:
    def __init__(self, p, pick, ss, rs, keep, ls):
        self.p, self.pick, self.ss, self.rs, self.keep, self.ls = p, pick, ss, rs, keep, ls

    def copy(self, k):
        p = self.p
        to = lax.rem(p.f + k, p.nf)
        src, dst = self.pick(to)
        return remote(src, dst, self.ss.at[k], self.rs.at[k], "fsdp", to)

    def start(self):
        for k in range(1, self.p.nf):
            self.copy(k).start()
        if self.keep is not None:
            pltpu.make_async_copy(*self.keep, self.ls).start()

    def wait(self):
        for k in range(1, self.p.nf):
            self.copy(k).wait()
        if self.keep is not None:
            pltpu.make_async_copy(*self.keep, self.ls).wait()


DMA = pltpu.SemaphoreType.DMA


def gather_sems(nc):
    return [DMA((3, nc)), DMA((nc,)), DMA]


def gathers_sems(nc):
    return [DMA((CUTS, 3, nc)), DMA((CUTS, nc)), DMA((CUTS,))]


def scatter_scratch(nz, T, E):
    return [pltpu.VMEM((nz, T, E), bf16)] * 2 + [pltpu.VMEM((nz + 1, T, E), bf16)]


def params(cid):
    return pltpu.CompilerParams(collective_id=cid, has_side_effects=True, vmem_limit_bytes=62 * 1024 * 1024)


ANY = pl.BlockSpec(memory_space=pl.ANY)
VM = pl.BlockSpec(memory_space=pltpu.VMEM)


def open_kernel(
    nc, nf, tok, ids, gains, wq, wk, wv, wo, wg, wu, wd, row, ids_row, w, wm,
    qv, kv, vv, ov, gv, bigv, wl, wmv, lsem, msem,
    gss, grs, gls, iss, irs, ils, ass, ars, fss, frs, als,
):
    p = Place(nc, nf)
    T = tok.shape[0]
    R, QW = wq.shape[0], wq.shape[1] // nc
    F = wg.shape[1] // nc
    rep = nc * HD // wk.shape[1]
    small = [
        pltpu.make_async_copy(src, dst, lsem.at[i])
        for i, (src, dst) in enumerate(((wq, qv), (wk, kv), (wv, vv), (wo, ov), (gains, gv)))
    ]
    large = [pltpu.make_async_copy(src, bigv.at[i], lsem.at[5 + i]) for i, src in enumerate((wg, wu, wd))]
    for cp in small + large:
        cp.start()
    greet(p, ctx=True, fsdp=True)
    g = Gathers(p, tok, row, T, gss, grs, gls)
    for h in range(CUTS):
        g.first(h)

    def id_copy(k):
        to = lax.rem(p.c + k, nc)
        return remote(ids, ids_row.at[p.c], iss.at[k], irs.at[k], "ctx", to)

    def block(k):
        to = lax.rem(p.c + k, nc)
        return remote(wl.at[to], w.at[p.c, p.f], ass.at[k], ars.at[k], "ctx", to)

    def onward(c, k, m):
        to = lax.rem(p.f + m, nf)
        return remote(w.at[c, p.f], w.at[c, p.f], fss.at[k, m], frs.at[k, m], "fsdp", to)

    def source(k):
        return lax.rem(p.c + nc - k, nc)

    for cp in small:
        cp.wait()
    for c in range(nc):
        h = c // rep
        at = 0
        for src, i, width in ((qv, c, QW), (kv, h, HD), (vv, h, HD), (ov, c, QW)):
            wl[c, :, pl.ds(at, width)] = src[:, i * width : (i + 1) * width].astype(bf16)
            at += width
        wl[c, :, pl.ds(at, 128)] = gv[...]
    keep_ids = pltpu.make_async_copy(ids, ids_row.at[p.c], ils)
    keep_w = pltpu.make_async_copy(wl.at[p.c], w.at[p.c, p.f], als)
    keep_w.start()
    keep_ids.start()
    for k in range(1, nc):
        block(k).start()
        id_copy(k).start()
    keep_w.wait()

    def spread(k):
        for m in range(1, nf):
            onward(source(k), k, m).start()

    spread(0)
    for i, cp in enumerate(large):
        cp.wait()

        def cast(c, _, i=i):
            wmv[c, :, pl.ds(i * F, F)] = bigv[i, :, pl.ds(pl.multiple_of(c * F, F), F)].astype(bf16)
            return 0

        lax.fori_loop(0, nc, cast, 0)
    keep_m = pltpu.make_async_copy(wmv, wm, msem)
    keep_m.start()
    for k in range(1, nc):
        block(k).wait_recv()
        spread(k)
    for t in range(1, p.nz):
        g.step(t)
    g.finish()
    keep_ids.wait()
    keep_m.wait()
    for k in range(1, nc):
        block(k).wait_send()
        id_copy(k).wait()
    for k in range(nc):
        for m in range(1, nf):
            onward(source(k), k, m).wait()


def open_call(nc, nf, tok, ids, gains, wq, wk, wv, wo, wg, wu, wd):
    T, E = tok.shape
    R = wq.shape[0]
    A = 2 * wq.shape[1] // nc + 2 * HD + 128
    M = 3 * wg.shape[1] // nc
    VMEM = pltpu.VMEM
    return pl.pallas_call(
        functools.partial(open_kernel, nc, nf),
        in_specs=[ANY] * 10,
        out_specs=[ANY] * 4,
        out_shape=[
            jax.ShapeDtypeStruct((nc, T, E), bf16),
            jax.ShapeDtypeStruct((nc,) + ids.shape, jnp.int32),
            jax.ShapeDtypeStruct((nc, nf, R, A), bf16),
            jax.ShapeDtypeStruct((nc, R, M), bf16),
        ],
        scratch_shapes=[VMEM(v.shape, f32) for v in (wq, wk, wv, wo)]
        + [VMEM((R, 128), bf16), VMEM((3,) + wg.shape, f32), VMEM((nc, R, A), bf16), VMEM((nc, R, M), bf16)]
        + [DMA((8,)), DMA]
        + gathers_sems(nc)
        + [DMA((nc,)), DMA((nc,)), DMA, DMA((nc,)), DMA((nc,)), DMA((nc, nf)), DMA((nc, nf)), DMA],
        compiler_params=params(1),
        name="open_row",
    )(tok, ids, gains, wq, wk, wv, wo, wg, wu, wd)


def finish_kernel(F, QW, rep, gm, ga, gg, gu, gd, gq, go, gk, gv):
    each_step = gm.shape[0]
    for i in range(each_step):
        for ref, at in ((gg, 0), (gu, F), (gd, 2 * F)):
            ref[:, i * F : (i + 1) * F] = gm[i, :, pl.ds(at, F)].astype(f32)
        for ref, at in ((gq, 0), (go, QW + 2 * HD)):
            ref[:, i * QW : (i + 1) * QW] = ga[i, :, pl.ds(at, QW)].astype(f32)
    steps = gk.shape[1] * rep // (HD * each_step)
    for step in range(steps):

        @pl.when(pl.program_id(0) == step)
        def _(step=step):
            for i in range(each_step):
                c = step * each_step + i
                at = slice((c // rep) * HD, (c // rep + 1) * HD)
                for ref, lane in ((gk, QW), (gv, QW + HD)):
                    v = ga[i, :, lane : lane + HD].astype(f32)
                    ref[:, at] = v if c % rep == 0 else ref[:, at] + v


def finish_call(gm, ga, rep):
    nc, R, M = gm.shape
    A = ga.shape[2]
    F, QW = M // 3, (A - 2 * HD) // 2
    n = 2
    out = lambda width: pl.BlockSpec((R, n * width), lambda c: (0, c))
    whole = pl.BlockSpec((R, nc * HD // rep), lambda c: (0, 0))
    widths = (F, F, F, QW, QW)
    return pl.pallas_call(
        functools.partial(finish_kernel, F, QW, rep),
        grid=(nc // n,),
        in_specs=[pl.BlockSpec((n, R, M), lambda c: (c, 0, 0)), pl.BlockSpec((n, R, A), lambda c: (c, 0, 0))],
        out_specs=[out(width) for width in widths] + [whole, whole],
        out_shape=[jax.ShapeDtypeStruct((R, nc * width), f32) for width in widths]
        + [jax.ShapeDtypeStruct((R, nc * HD // rep), f32)] * 2,
        name="finish_rows",
    )(gm, ga)


def middle_kernel(nc, nf, fold, *refs):
    it = iter(refs)
    take = lambda n: [next(it) for _ in range(n)]
    oT, wo, tok, og, g, wl = take(6)
    hid, n2, dm, w = take(4)
    outs = take(3) if fold else None
    a, x, ud, stage, oblk, own, dmo, rsem = take(8)
    nss, nrs, nls, dss, drs, dls, fss, frs, fls = take(9)
    p = Place(nc, nf)
    greet(p, fsdp=True)
    T, E = tok.shape
    M = wl.shape[2]
    F, F2 = M // 3, 2 * M // 3
    R = wl.shape[1]
    S = nc * T

    def make(d, ref):
        oblk[...] = oT[:, pl.ds(pl.multiple_of(d * T, T), T)].T

        def fn(r):
            ref[:, r] = dg(oblk[...], wo[r, :], 1, 1).astype(bf16)

        strips(fn, E, 512)

    rs = Scatter(p, a, x, ud, T, rsem, make=make, stage=stage)
    dmg = Gathers(p, dmo, dm, T, dss, drs, dls)
    if fold:
        n2v, wguv, wdv, dact, dmb, out, osem, dsem, csem, wsem = take(10)
        ag = Gathers(p, None, n2v, T, nss, nrs, nls)
        low, high = wl.at[:, :, pl.ds(0, F2)], wl.at[:, :, pl.ds(F2, F)]
        last = Peers(p, lambda to: (high, wdv.at[:, p.f]), fss.at[0], frs.at[0], (high, wdv.at[:, p.f]), fls.at[0])
        firsts = Peers(p, lambda to: (low, wguv.at[:, p.f]), fss.at[1], frs.at[1], (low, wguv.at[:, p.f]), fls.at[1])
        last.start()
        firsts.start()
        saves = [
            pltpu.make_async_copy(wdv, w.at[:, :, :, pl.ds(F2, F)], wsem.at[0]),
            pltpu.make_async_copy(wguv, w.at[:, :, :, pl.ds(0, F2)], wsem.at[1]),
        ]
    else:
        ag = Gathers(p, own, n2, T, nss, nrs, nls)
        every = Peers(p, lambda to: (wl, w.at[:, p.f]), fss.at[0], frs.at[0], (wl, w.at[:, p.f]), fls.at[0])
        every.start()

    def dm_rows(r):
        dmo[r] = (RES * og[r].astype(f32)).astype(bf16)

    each(dm_rows, 0, T)
    for h in range(CUTS):
        dmg.first(h)
    rs.compute()

    def rows(r, v):
        h = tok[r].astype(f32) + RES * v
        hid[r] = h
        v = (h * lax.rsqrt(jnp.mean(h * h, axis=-1, keepdims=True) + EPS) * g[...]).astype(bf16)
        if fold:
            n2v[p.c, r] = v
        else:
            own[r] = v

    interleave(dmg.all_steps(), rs.all_steps())
    rs.total(rows, ag.first)
    dmg.finish()
    steps = [functools.partial(ag.step, t) for t in range(1, p.nz)]
    if not fold:
        for s in steps:
            s()
        ag.finish()
        rs.finish()
        every.wait()
        return

    def dm_load(k, slot):
        return pltpu.make_async_copy(dm.at[k], dmb.at[slot], dsem.at[slot])

    def back(k, _):
        slot = k % 2

        @pl.when(k + 1 < nc)
        def _():
            dm_load(k + 1, 1 - slot).start()

        dm_load(k, slot).wait()

        def fn(at):
            v = jnp.dot(dmb[slot], wdv[:, :, :, at].reshape(E, -1), preferred_element_type=f32)
            dact[pl.ds(pl.multiple_of(k * T, T), T), at] = v

        strips(fn, F, min(512, F))
        return 0

    dm_load(0, 0).start()
    last.wait()
    saves[0].start()
    lax.fori_loop(0, nc, back, 0)

    def results(k, slot):
        rows_ = pl.ds(pl.multiple_of(k * T, T), T)
        return [pltpu.make_async_copy(out.at[slot, i], outs[i].at[rows_], osem.at[slot, i]) for i in range(3)]

    def block(q, _):
        dist, sign, slot = q // 4, (q // 2) % 2, q % 2
        y = p.z + (2 * sign - 1) * dist

        @pl.when((y >= 0) & (y < nc // 2) & (dist + 1 - sign > 0))
        def _():
            k = 2 * y + p.j + slot * (1 - 2 * p.j)
            pl.when(slot == 1)(lambda: ag.arrived(k))
            pltpu.make_async_copy(n2v.at[k], n2.at[k], csem.at[k]).start()

            @pl.when(dist > 0)
            def _():
                for cp in results(k, slot):
                    cp.wait()

            def fn(at):
                up_at = pl.ds(pl.multiple_of(at.start + F, 128), at.size)
                gate = jnp.dot(n2v[k], wguv[:, :, :, at].reshape(E, -1), preferred_element_type=f32)
                up = jnp.dot(n2v[k], wguv[:, :, :, up_at].reshape(E, -1), preferred_element_type=f32)
                d = dact[pl.ds(pl.multiple_of(k * T, T), T), at]
                sg = 1.0 / (1.0 + jnp.exp(-gate))
                silu = gate * sg
                out[slot, 0, :, at] = (d * up * sg * (1.0 + gate * (1.0 - sg))).astype(bf16)
                out[slot, 1, :, at] = (d * silu).astype(bf16)
                out[slot, 2, :, at] = (silu * up).astype(bf16)

            strips(fn, F, min(STRIP, F))
            for cp in results(k, slot):
                cp.start()

        return 0

    nz = nc // 2
    for t, s in enumerate(steps, 1):
        s()
        if t == 2:
            firsts.wait()
            saves[1].start()
            lax.fori_loop(0, 8, block, 0)
    lax.fori_loop(8, 4 * nz, block, 0)
    ag.finish(True)
    rs.finish()
    for slot in range(2):
        for cp in results(0, slot):
            cp.wait()
    for cp in saves:
        cp.wait()
    for k in range(nc):
        pltpu.make_async_copy(n2v.at[k], n2.at[k], csem.at[k]).wait()


STRIP = 512


def middle_call(nc, nf, fold, oT, wo, tok, og, g, wl):
    T, E = tok.shape
    _, R, M = wl.shape
    nz = nc // 2
    F, S = M // 3, nc * T
    VMEM = pltpu.VMEM
    return pl.pallas_call(
        functools.partial(middle_kernel, nc, nf, fold),
        in_specs=[VM, VM, VM, VM, VM, ANY],
        out_specs=[VM, ANY, ANY, ANY] + [ANY] * 3 * fold,
        out_shape=[
            jax.ShapeDtypeStruct((T, E), f32),
            jax.ShapeDtypeStruct((nc, T, E), bf16),
            jax.ShapeDtypeStruct((nc, T, E), bf16),
            jax.ShapeDtypeStruct((nc, nf, R, M), bf16),
        ]
        + [jax.ShapeDtypeStruct((S, F), bf16)] * 3 * fold,
        scratch_shapes=scatter_scratch(nz, T, E)
        + [VMEM((2, T, E), bf16), VMEM((T, oT.shape[0]), bf16)]
        + [VMEM((8, 128) if fold else (T, E), bf16), VMEM((T, E), bf16), DMA((7, nz, CUTS))]
        + gathers_sems(nc)
        + gathers_sems(nc)
        + [DMA((2, nf)), DMA((2, nf)), DMA((2,))]
        + [
            VMEM((nc, T, E), bf16), VMEM((nc, nf, R, 2 * F), bf16), VMEM((nc, nf, R, F), bf16), VMEM((S, F), f32),
            VMEM((2, T, E), bf16), VMEM((2, 3, T, F), bf16), DMA((2, 3)), DMA((2,)), DMA((nc,)), DMA((2,)),
        ]
        * fold,
        compiler_params=params(2),
        name="attn_to_mlp",
    )(oT, wo, tok, og, g, wl)


EARLY, MLP_LATE = 8, True


def turn_kernel(nc, nf, fold, *refs):
    it = iter(refs)
    take = lambda n: [next(it) for _ in range(n)]
    n2, dm, dga, dup, act, wm = take(6)
    hid, og, g, dh, da = take(5)
    lay = next(it) if fold else None
    gg, gs, y, gbuf = take(4)
    mpart = next(it) if fold else None
    a, x, ud, own, rsem = take(5)
    nss, nrs, nls, fss, frs, fls = take(6)
    dguv, actv, wide, nt, go, mp, lsem, ssem = take(8)
    p = Place(nc, nf)
    nz = p.nz
    greet(p, fsdp=True)
    T, E = hid.shape
    S, F = act.shape
    F2 = 2 * F
    R = E // (nc * nf)
    B = nf * R

    def fetch(src, dst, i):
        return pltpu.make_async_copy(src, dst, lsem.at[4 + i])

    big = [
        fetch(wm.at[:, pl.ds(0, F2)], wide.at[pl.ds(0, E), pl.ds(0, F2)], 0),
        fetch(dga, dguv.at[:, pl.ds(0, F)], 1),
        fetch(dup, dguv.at[:, pl.ds(F, F)], 2),
        fetch(act, actv, 3),
    ]

    def make(d, ref):
        tok = dguv[pl.ds(pl.multiple_of(d * T, T), T), :]

        def fn(r):
            ref[:, r] = dg(tok, wide[r, pl.ds(0, F2)], 1, 1).astype(bf16)

        strips(fn, E, 512)

    rs = Scatter(p, a, x, ud, T, rsem, make=make, stage=mp)
    ag = Gathers(p, own, da, T, nss, nrs, nls)
    if fold:
        x2, ud2, wdv, msem, psem = take(5)
        ms = Scatter(p, a, x2, ud2, T, msem, part=mpart)
        big.append(fetch(wm.at[:, pl.ds(F2, F)], wdv, 4))
    for cp in big[:3]:
        cp.start()

    def spot(i):
        return pl.ds(pl.multiple_of(i * B, B), B)

    def column(b, slot):
        at = spot(b)
        return (
            pltpu.make_async_copy(n2.at[:, at], wide.at[pl.ds(0, S), spot(slot)], lsem.at[slot]),
            pltpu.make_async_copy(dm.at[:, at], wide.at[pl.ds(0, S), spot(2 + slot)], lsem.at[2 + slot]),
        )

    def keep(b, slot):
        return pltpu.make_async_copy(go.at[slot], gbuf.at[b], ssem.at[slot])

    def peer(b, k):
        to = lax.rem(p.f + k, nf)
        at = pl.ds(pl.multiple_of(to * R, R), R)
        return remote(gbuf.at[b, at], y.at[p.f, b], fss.at[k, b], frs.at[k, b], "fsdp", to)

    def terms(b, slot):
        at = pl.ds(pl.multiple_of(p.f * R, R), R)
        srcs = [gbuf.at[b, at]] + [y.at[lax.rem(p.f + k, nf), b] for k in range(1, nf)]
        return [
            pltpu.make_async_copy(src, go.at[slot, pl.ds(i * R, R)], fls.at[slot, i]) for i, src in enumerate(srcs)
        ]

    def stored(b, slot):
        return pltpu.make_async_copy(go.at[slot, pl.ds(0, R)], gs.at[b], ssem.at[slot])

    def sums(first, last):
        for b in range(first, last):
            slot = b % 2
            for k in range(1, nf):
                peer(b, k).wait()
            if b > 1:
                stored(b - 2, slot).wait()
            cps = terms(b, slot)
            for cp in cps:
                cp.start()
            for cp in cps:
                cp.wait()

            def fn(r, slot=slot):
                v = go[slot, r].astype(f32)
                for i in range(1, nf):
                    v = v + go[slot, pl.ds(r.start + i * R, CH)].astype(f32)
                go[slot, r] = v.astype(bf16)

            each(fn, 0, R)
            stored(b, slot).start()

    def send(b):
        keep(b, b % 2).wait()
        for k in range(1, nf):
            peer(b, k).start()

    def grads(b, _):
        slot = b % 2

        @pl.when(b + 1 < nc)
        def _():
            for cp in column(b + 1, 1 - slot):
                cp.start()

        now = column(b, slot)
        for at, val, base, width, cp in ((slot, dguv, 0, F2, now[0]), (2 + slot, actv, F2, F, now[1])):
            cp.wait()
            nt[...] = wide[pl.ds(0, S), spot(at)].T
            step = min(512, width)

            def dots(i, _, val=val, base=base, step=step):
                at = pl.multiple_of(i * step, step)
                v = jnp.dot(nt[...], val[:, pl.ds(at, step)], preferred_element_type=f32)
                go[slot, :, pl.ds(pl.multiple_of(base + at, step), step)] = v.astype(bf16)
                return 0

            lax.fori_loop(0, width // step, dots, 0)
        keep(b, slot).start()

        @pl.when(b > 0)
        def _():
            send(b - 1)

        return 0

    def mlp(b, _):
        slot = b % 2
        out = pltpu.make_async_copy(mp.at[slot], mpart.at[b], psem.at[slot])

        @pl.when(b > 1)
        def _():
            out.wait()

        tok = actv[pl.ds(pl.multiple_of(b * T, T), T), :]

        def dots(i, _):
            at = pl.ds(pl.multiple_of(i * 512, 512), 512)
            mp[slot, :, at] = dg(tok, wdv[at, :], 1, 1).astype(bf16)
            return 0

        lax.fori_loop(0, E // 512, dots, 0)
        out.start()
        return 0

    gg[...] = jnp.zeros_like(gg)
    for cp in big[:3]:
        cp.wait()
    for cp in big[3:]:
        cp.start()
    rs.compute()
    for cp in column(0, 0):
        cp.start()
    for cp in big[3:]:
        cp.wait()
    steps = rs.all_steps()
    early = EARLY * nc // 8 if fold else nc
    bounds = [early * i // (len(steps) + 1) for i in range(len(steps) + 2)]
    for i in range(len(steps) + 1):
        lax.fori_loop(bounds[i], bounds[i + 1], grads, 0)
        if i < len(steps):
            steps[i]()
    if fold:
        rs.sent()

    def mlp_terms():
        if fold:
            lax.fori_loop(0, nc, mlp, 0)
            for slot in range(2):
                pltpu.make_async_copy(mp.at[slot], mpart.at[slot], psem.at[slot]).wait()
            ms.begin(load=False)

    def rows(r, dn):
        h = hid[r]
        inv = lax.rsqrt(jnp.mean(h * h, axis=-1, keepdims=True) + EPS)
        xn = h * inv
        e = dn * g[...]
        v = og[r].astype(f32) + inv * (e - xn * jnp.mean(e * xn, axis=-1, keepdims=True))
        dh[r] = v
        own[r] = (RES * v).astype(bf16)
        gg[...] += jnp.sum((xn * dn).reshape(CH // 8, 8, E), axis=0)

    if not MLP_LATE:
        mlp_terms()
    rs.total(rows, ag.first)
    if MLP_LATE:
        mlp_terms()
    rs.finish(not fold)
    if fold:
        ms.begin(cross=False)
        ms.edges()
    more = ms.all_steps() if fold else []
    made, done = early, 0
    late = ag.all_steps()
    for i, s in enumerate(late):
        upto = min(nc, made + max(1, nc // 8))
        lax.fori_loop(made, upto, grads, 0)
        if made < nc and upto == nc:
            send(nc - 1)
        made = upto
        s()
        if i < len(more):
            more[i]()
    if early == nc:
        send(nc - 1)
    sums(0, nc // 2)
    done = nc // 2
    if fold:

        def out(r, v):
            lay[r] = (hid[r] + RES * v).astype(bf16)

        ms.total(out)
        ms.finish()
    ag.finish()
    sums(done, nc)
    for b in range(nc - 2, nc):
        stored(b, b % 2).wait()


def turn_call(nc, nf, fold, n2, dm, dga, dup, act, wm, hid, og, g):
    T, E = hid.shape
    S, F = act.shape
    F2, M = 2 * F, 3 * F
    R = E // (nc * nf)
    B = nf * R
    nz = nc // 2
    VMEM = pltpu.VMEM
    return pl.pallas_call(
        functools.partial(turn_kernel, nc, nf, fold),
        in_specs=[ANY] * 6 + [VM, VM, VM],
        out_specs=[VM, ANY] + [VM] * fold + [VM, ANY, ANY, ANY] + [ANY] * fold,
        out_shape=[jax.ShapeDtypeStruct((T, E), f32), jax.ShapeDtypeStruct((nc, T, E), bf16)]
        + [jax.ShapeDtypeStruct((T, E), bf16)] * fold
        + [
            jax.ShapeDtypeStruct((8, E), f32),
            jax.ShapeDtypeStruct((nc, R, M), bf16),
            jax.ShapeDtypeStruct((nf, nc, R, M), bf16),
            jax.ShapeDtypeStruct((nc, B, M), bf16),
        ]
        + [jax.ShapeDtypeStruct((nc, T, E), bf16)] * fold,
        scratch_shapes=scatter_scratch(nz, T, E)
        + [VMEM((T, E), bf16), DMA((7, nz, CUTS))]
        + gathers_sems(nc)
        + [DMA((nf, nc)), DMA((nf, nc)), DMA((2, nf))]
        + [VMEM((S, F2), bf16), VMEM((S, F), bf16), VMEM((max(E, S), max(F2, 4 * B)), bf16)]
        + [VMEM((B, S), bf16), VMEM((2, B, M), bf16), VMEM((2, T, E), bf16), DMA((9,)), DMA((2,))]
        + [VMEM((nz, T, E), bf16), VMEM((nz + 1, T, E), bf16), VMEM((E, F), bf16), DMA((7, nz, CUTS)), DMA((2,))] * fold,
        compiler_params=params(3),
        name="mlp_to_attn",
    )(n2, dm, dga, dup, act, wm, hid, og, g)


def close_kernel(
    nc, nf, dqkv, wq, oT, n1, da, tok, dh, g, ggm, dx, gout, ggout,
    a, x, ud, stage, dblk, wqv, big, gt, gb, y, zb, gg, gbuf, gsum, gfin, rsem, lsem,
    fss, frs, fls, css, crs, cls, s1, r1, s2, r2, l2,
):
    p = Place(nc, nf)
    greet(p, ctx=True, fsdp=True)
    T, E = tok.shape
    Q = dqkv.shape[0]
    H = oT.shape[0]
    R = E // (nc * nf)
    B = nf * R
    weights = pltpu.make_async_copy(wq.at[:, pl.ds(0, Q)], wqv, lsem.at[4])
    weights.start()

    def column(b, slot):
        at = pl.ds(pl.multiple_of(b * B, B), B)
        return (
            pltpu.make_async_copy(n1.at[:, at], big.at[0, slot], lsem.at[slot]),
            pltpu.make_async_copy(da.at[:, at], big.at[1, slot], lsem.at[2 + slot]),
        )

    for cp in column(0, 0):
        cp.start()

    def make(d, ref):
        dblk[...] = dqkv[:, pl.ds(pl.multiple_of(d * T, T), T)].T

        def fn(r):
            ref[:, r] = dg(dblk[...], wqv[r, :], 1, 1).astype(bf16)

        strips(fn, E, 512)

    rs = Scatter(p, a, x, ud, T, rsem, make=make, stage=stage)

    def pieces(to):
        return gb.at[:, pl.ds(pl.multiple_of(to * R, R), R)], y.at[p.f]

    peers = Peers(p, pieces, fss, frs, pieces(p.f), fls)
    gg[...] = jnp.zeros_like(gg)

    def piece(k):
        to = lax.rem(p.c + k, nc)
        return remote(zb.at[to], gout.at[p.c], css.at[k], crs.at[k], "ctx", to)

    mine = pltpu.make_async_copy(zb.at[p.c], gout.at[p.c], cls)

    def grads():
        peers.wait()
        for c in range(nc):

            def fn(r):
                v = y[0, c, r].astype(f32)
                for m in range(1, nf):
                    v = v + y[m, c, r].astype(f32)
                zb[c, r] = v.astype(bf16)

            each(fn, 0, R)
        for k in range(1, nc):
            piece(k).start()
        mine.start()

    def rows(r, dn):
        t = tok[r].astype(f32)
        inv = lax.rsqrt(jnp.mean(t * t, axis=-1, keepdims=True) + EPS)
        xn = t * inv
        e = dn * g[...]
        dx[r] = dh[r] + inv * (e - xn * jnp.mean(e * xn, axis=-1, keepdims=True))
        gg[...] += jnp.sum((xn * dn).reshape(CH // 8, 8, E), axis=0)

    weights.wait()
    rs.compute()

    def products(b, _):
        slot = b % 2

        @pl.when(b + 1 < nc)
        def _():
            for cp in column(b + 1, 1 - slot):
                cp.start()

        for cp in column(b, slot):
            cp.wait()
        gt[pl.ds(0, Q), :] = dg(dqkv[...], big[0, slot], 1, 0)
        gt[pl.ds(Q, H), :] = dg(oT[...], big[1, slot], 1, 0)
        gb[b] = gt[...].T.astype(bf16)
        return 0

    lax.fori_loop(0, nc, products, 0)
    peers.start()
    for s in rs.all_steps():
        s()
    grads()
    rs.total(rows)

    groups = E // 128
    sa = jnp.sum(gg[...], axis=0, keepdims=True)
    sm = jnp.sum(ggm[...], axis=0, keepdims=True)
    for i in range(groups):
        gbuf[p.f, i] = jnp.concatenate(
            [sa[:, i * 128 : (i + 1) * 128], sm[:, i * 128 : (i + 1) * 128], jnp.zeros((6, 128), f32)], axis=0
        )

    def over(k):
        to = lax.rem(p.f + k, nf)
        return remote(gbuf.at[p.f], gbuf.at[p.f], s1.at[k], r1.at[k], "fsdp", to)

    for k in range(1, nf):
        over(k).start()
    for k in range(1, nf):
        over(k).wait()
    v = gbuf[0]
    for m in range(1, nf):
        v = v + gbuf[m]
    gsum[...] = v
    per = 128 // R

    def along(k):
        to = lax.rem(p.c + k, nc)
        return remote(gsum.at[(to * nf + p.f) // per], gfin.at[p.c], s2.at[k], r2.at[k], "ctx", to)

    for k in range(1, nc):
        along(k).start()
    own = pltpu.make_async_copy(gsum.at[(p.c * nf + p.f) // per], gfin.at[p.c], l2)
    own.start()
    own.wait()
    for k in range(1, nc):
        along(k).wait()
    t = gfin[0]
    for m in range(1, nc):
        t = t + gfin[m]
    ggout[...] = t
    for k in range(1, nc):
        piece(k).wait()
    mine.wait()
    rs.finish()


def close_call(nc, nf, dqkv, wq, oT, n1, da, tok, dh, g, ggm):
    T, E = tok.shape
    S = n1.shape[0]
    Q, H = dqkv.shape[0], oT.shape[0]
    A = Q + H
    R = E // (nc * nf)
    nz = nc // 2
    VMEM = pltpu.VMEM
    return pl.pallas_call(
        functools.partial(close_kernel, nc, nf),
        in_specs=[VM, ANY, VM, ANY, ANY, VM, VM, VM, VM],
        out_specs=[VM, ANY, VM],
        out_shape=[
            jax.ShapeDtypeStruct((T, E), f32),
            jax.ShapeDtypeStruct((nc, R, A), bf16),
            jax.ShapeDtypeStruct((8, 128), f32),
        ],
        scratch_shapes=scatter_scratch(nz, T, E)
        + [VMEM((2, T, E), bf16), VMEM((T, Q), bf16), VMEM((E, Q), bf16), VMEM((2, 2, S, nf * R), bf16)]
        + [VMEM((A, nf * R), f32), VMEM((nc, nf * R, A), bf16)]
        + [
            VMEM((nf, nc, R, A), bf16),
            VMEM((nc, R, A), bf16),
            VMEM((8, E), f32),
            VMEM((nf, E // 128, 8, 128), f32),
            VMEM((E // 128, 8, 128), f32),
            VMEM((nc, 8, 128), f32),
            DMA((7, nz, CUTS)),
            DMA((5,)),
        ]
        + [DMA((nf,)), DMA((nf,)), DMA, DMA((nc,)), DMA((nc,)), DMA]
        + [DMA((nf,)), DMA((nf,)), DMA((nc,)), DMA((nc,)), DMA],
        compiler_params=params(4),
        name="close_row",
    )(dqkv, wq, oT, n1, da, tok, dh, g, ggm)


def rms(v):
    inv = lax.rsqrt(jnp.mean(v * v, axis=-1, keepdims=True) + EPS)
    return v * inv, inv


def rms_back(x, inv, e):
    return inv * (e - x * jnp.mean(e * x, axis=-1, keepdims=True))


def rotate(v, cos, sin, sign):
    heads = v.shape[0] // HD
    v = v.reshape(heads, 2, HD // 2, v.shape[1])
    a, b = v[:, 0], v[:, 1]
    s = sign * sin
    return jnp.stack([a * cos - b * s, b * cos + a * s], axis=1).reshape(heads * HD, -1)


def local(
    tokens, seq_ids, positions, block_ids, gain_attn, w_query, w_key, w_value, w_out,
    gain_mlp, w_gate, w_up, w_down, out_grad,
):
    nc = lax.axis_size("ctx")
    nf = lax.axis_size("fsdp")
    nz = nc // 2
    T, E = tokens.shape[1:]
    R = w_query.shape[0]
    S = T * nc
    FFL = w_gate.shape[1] // nc
    nh = QUERY_HEADS // nc
    rep = nc // KEY_VALUE_HEADS
    QW = nh * HD
    KO, VO, OO, GO = QW, QW + HD, QW + 2 * HD, 2 * QW + 2 * HD
    tok, og = tokens[0], out_grad[0]

    def exchange(w):
        return lax.all_to_all(w, "ctx", 0, 0, tiled=True)


    gains = jnp.pad(jnp.stack([gain_attn, gain_mlp], axis=1).astype(bf16), ((0, 0), (0, 126)))
    ids = jnp.pad(jnp.concatenate([seq_ids, positions, block_ids], axis=0), ((0, 5), (0, 0)))
    row_tok, ids, wa, wm = open_call(
        nc, nf, tok, ids, gains, w_query, w_key, w_value, w_out, w_gate, w_up, w_down
    )
    wm = exchange(wm)
    wa = wa.reshape(E, -1)
    g_attn, g_mlp = wa[:, GO].astype(f32)[None], wa[:, GO + 1].astype(f32)[None]

    seq, pos, blk = (ids[:, i].reshape(S) for i in range(3))
    place = jnp.arange(S, dtype=jnp.int32)
    cut = jnp.sum((seq == 0).astype(jnp.int32))
    first = place - pos
    last = jnp.minimum(first + BLOCK * (blk + 1), jnp.where(seq == 0, cut, S))
    st, en = first[None], last[None]
    freq = ROPE_BASE ** (-(jnp.arange(HD // 2, dtype=f32) * 2.0) / HD)
    ang = freq[:, None] * pos.astype(f32)[None, :]
    cos, sin = jnp.cos(ang), jnp.sin(ang)

    x1r, _ = rms(row_tok.reshape(S, E).astype(f32))
    n1 = (x1r * g_attn).astype(bf16)
    w_qkv, w_o = wa[:, :OO], wa[:, OO:GO]
    qkv = dg(w_qkv, n1, 0, 1)
    qkT = rotate(qkv[:VO], cos, sin, 1.0).astype(bf16)
    qT, kT = qkT[:QW], qkT[QW:]
    vT = qkv[VO:].astype(bf16)
    k, v = kT.T, vT.T
    oT, oTb, lse = attn_fwd(qT, k, vT, st, en)

    middle = (oTb, w_o, tok, og, g_mlp, wm)
    if nz <= 4:
        hidden, n2, dm, wm, d_gate, d_up, act = middle_call(nc, nf, True, *middle)
        n2, dm, wm = n2.reshape(S, E), dm.reshape(S, E), wm.reshape(E, -1)
    else:
        hidden, n2, dm, wm = middle_call(nc, nf, False, *middle)
        n2, dm, wm = n2.reshape(S, E), dm.reshape(S, E), wm.reshape(E, -1)
        w_d = wm[:, 2 * FFL :]
        gu = dg(n2, wm[:, : 2 * FFL], 1, 0)
        gate, up = gu[:, :FFL], gu[:, FFL:]
        sg = jax.nn.sigmoid(gate)
        act = (gate * sg * up).astype(bf16)
        d_act = dg(dm, w_d, 1, 0)
        d_gate = (d_act * up * sg * (1.0 + gate * (1.0 - sg))).astype(bf16)
        d_up = (d_act * gate * sg).astype(bf16)
    turn = (n2, dm, d_gate, d_up, act, wm, hidden, og, g_mlp)
    if nz <= 4:
        dh, da, layer_out, ggm, gm = turn_call(nc, nf, True, *turn)[:5]
    else:
        dh, da, ggm, gm = turn_call(nc, nf, False, *turn)[:4]
        mlp = dg(act, w_d, 1, 1).astype(bf16)
        mlp = lax.psum_scatter(mlp, "ctx", scatter_dimension=0, tiled=True)
        layer_out = (hidden + RES * mlp.astype(f32)).astype(bf16)
    da = da.reshape(S, E)
    gm = exchange(gm)

    dqkv = attn_bwd(qT, da, w_o.T, oT, lse, st, en, cos, sin, k, kT, v)
    input_grad, ga, gains = close_call(nc, nf, dqkv, wa, oTb, n1, da, tok, dh, g_attn, ggm)
    at = lax.rem((lax.axis_index("ctx") * nf + lax.axis_index("fsdp")) * R, 128)
    gains = lax.dynamic_slice_in_dim(gains, at, R, 1)

    grads = finish_call(gm, ga, rep)
    return (
        layer_out[None],
        input_grad[None],
        gains[0],
        grads[3],
        grads[5],
        grads[6],
        grads[4],
        gains[1],
        *grads[:3],
    )


def solution(mesh):
    w1, w2 = P(("ctx", "fsdp")), P(("ctx", "fsdp"), None)
    act, ids = P("fsdp", "ctx", None), P("fsdp", "ctx")
    return jax.shard_map(
        local,
        mesh=mesh,
        in_specs=(act, ids, ids, ids, w1, w2, w2, w2, w2, w1, w2, w2, w2, act),
        out_specs=(act, act, w1, w2, w2, w2, w2, w1, w2, w2, w2),
        check_vma=False,
    )
```
